32 devices in a mesh: grp: 2 (over y), rows: 4 (over z), wt: 4 (over x, core).
Axes of the slice: x: 2, y: 2, z: 4, core: 2. Of those that a mesh axis runs over, the one named last changes fastest.
Arguments:
- latents: float32 [8, 640, 8, 128], P(('grp', 'wt'), None, 'rows'), parts along dimension 0, may hold values from -48 to 48
- teacher: float32 [8, 640, 8, 128], P(('grp', 'wt'), None, 'rows'), parts along dimension 0, may hold values from -6 to 6
- norm_gain: float32 [640], replicated, may hold values from 0.25 to 1.75
- norm_shift: float32 [640], replicated, may hold values from -3 to 3
- conv_weight: bfloat16 [640, 9, 640], P('wt'), may hold values from -0.078125 to 0.078125
- conv_bias: float32 [640], replicated, may hold values from -3 to 3
Outputs:
- mean_loss: float32 [2], P('grp'), parts along dimension 0
- grad_latents: float32 [8, 640, 8, 128], P(('grp', 'wt'), None, 'rows'), parts along dimension 0
- grad_weight: float32 [1280, 9, 640], P(('grp', 'wt')), parts along dimension 0
- param_grads: float32 [6, 640], P('grp'), parts along dimension 0
The draws below stay inside these ranges and needn't reach their ends.
There are 2 independent parts, one for each index of `grp`. The reference program is written for one: setup_inputs(seed, part) draws one part's arguments, and reference() takes and returns one part's arrays. A program takes and returns all parts, laid end to end along the dimension named above; an argument that names none is the same for every part. Nothing has to cross between parts.
All inputs are finite; a program needn't handle non-finite values.
Results may differ from the reference program's by a relative error of at most 0.0013.
Values may be sent and summed in bfloat16 or wider, within the bound.
No kernel may reach another device: no remote copies, remote signals or barrier semaphores. Data moves between devices by JAX's collectives and lax.ppermute only.
A program may use at most 64 MiB of HBM per device.

```python
import math
import jax
import jax.numpy as jnp
from jax import lax

C = 640
GROUPS = 32
WIDTH = 128
IMAGES = 4
HEIGHT = 8


def draw_latents(key, part):
    key_noise = jax.random.fold_in(key, 11)
    key_channel = jax.random.fold_in(key, 12)
    key_row = jax.random.fold_in(key, 13)
    shape = (IMAGES, C, HEIGHT, WIDTH)
    base_noise = jnp.clip(jax.random.normal(key_noise, shape, jnp.float32), -4.0, 4.0)
    channel_scale = jnp.exp(jax.random.uniform(key_channel, (1, C, 1, 1), jnp.float32, math.log(0.5), math.log(2.0)))
    row_ramp = (jnp.arange(HEIGHT, dtype=jnp.float32) / max(HEIGHT - 1, 1)).reshape(1, 1, HEIGHT, 1)
    row_jitter = jnp.exp(jax.random.uniform(key_row, (IMAGES, 1, HEIGHT, 1), jnp.float32, 0.0, math.log(2.0)))
    row_scale = 0.6 * jnp.exp(row_ramp * math.log(3.0)) * row_jitter
    return base_noise * channel_scale * row_scale


def block_scale(rng, dims, pieces, least, largest):
    loudness = 1.0
    for dim, blocks in pieces:
        draws = jax.random.uniform(jax.random.fold_in(jax.random.fold_in(rng, 6), dim), (blocks,), jnp.float32, least / len(pieces), largest / len(pieces))
        loudness = loudness * jnp.repeat(jnp.exp(draws), dims[dim] // blocks).reshape((-1,) + (1,) * (len(dims) - 1 - dim))
    return loudness


def noise(rng, extent, spread, bound, shards=(), held_as=jnp.bfloat16):
    result = jax.random.normal(rng, extent, jnp.float32) * spread
    if len(shards) > 0:
        result = block_scale(rng, extent, shards, -0.22, 0.18) * result
    return jnp.clip(result, min=-bound, max=bound).astype(held_as)


def setup_inputs(seed: int = 0, part: int = 0) -> dict:
    arg_keys = jax.random.split(jax.random.key(seed), 7)
    part_keys = jax.random.split(jax.random.fold_in(arg_keys[6], part), 7)
    return {
        "latents": draw_latents(jax.random.fold_in(jax.random.fold_in(arg_keys[6], part), 71), part),
        "teacher": noise(part_keys[1], (IMAGES, C, HEIGHT, WIDTH), 1.0, 6.0, ((0, 4), (2, 4)), jnp.float32),
        "norm_gain": jnp.clip(1.0 + 0.15 * jax.random.normal(arg_keys[2], (C,), jnp.float32), 0.25, 1.75),
        "norm_shift": noise(arg_keys[3], (C,), 0.5, 3.0, (), jnp.float32),
        "conv_weight": noise(arg_keys[4], (C, 9, C), (9 * C) ** -0.5, 0.078125, ((0, 4),)),
        "conv_bias": noise(arg_keys[5], (C,), 0.5, 3.0, (), jnp.float32),
    }


epsilon = 1e-05

def conv_taps(weights, padded, strip_rows, column_count):
    running = None
    for tap_index in range(9):
        tap_row, tap_col = (tap_index // 3, tap_index % 3)
        window = padded[:, :, tap_row:tap_row + strip_rows, tap_col:tap_col + column_count]
        window = window.reshape(padded.shape[0], padded.shape[1], strip_rows * column_count)
        product = jnp.einsum('oi,nip->nop', weights[:, tap_index, :].astype(jnp.float32), window.astype(jnp.float32), precision=lax.Precision.HIGHEST)
        running = product if running is None else running + product
    return running

def transpose_taps(weights, padded, strip_rows, column_count):
    running = None
    for tap_index in range(9):
        tap_row, tap_col = (tap_index // 3, tap_index % 3)
        window = padded[:, :, 2 - tap_row:2 - tap_row + strip_rows, 2 - tap_col:2 - tap_col + column_count]
        window = window.reshape(padded.shape[0], padded.shape[1], strip_rows * column_count)
        product = jnp.einsum('oi,nop->nip', weights[:, tap_index, :].astype(jnp.float32), window.astype(jnp.float32), precision=lax.Precision.HIGHEST)
        running = product if running is None else running + product
    return running

def weight_terms(residual, padded, strip_rows, column_count):
    columns = []
    for tap_index in range(9):
        tap_row, tap_col = (tap_index // 3, tap_index % 3)
        window = padded[:, :, tap_row:tap_row + strip_rows, tap_col:tap_col + column_count]
        window = window.reshape(padded.shape[0], padded.shape[1], strip_rows * column_count)
        columns.append(jnp.einsum('nop,nip->oi', residual.astype(jnp.float32), window.astype(jnp.float32), precision=lax.Precision.HIGHEST))
    return jnp.stack(columns, axis=1)

def reference(latents, teacher, norm_gain, norm_shift, conv_weight, conv_bias):
    images, channels, height, column_count = latents.shape
    cell_count = height * column_count
    grouped = latents.reshape(images, GROUPS, channels // GROUPS, cell_count)
    group_mean = lax.optimization_barrier(jnp.mean(grouped, axis=(2, 3), keepdims=True))
    centered = grouped - group_mean
    group_var = lax.optimization_barrier(jnp.mean(jnp.square(centered), axis=(2, 3), keepdims=True))
    inverse = lax.rsqrt(group_var + epsilon)
    normed = (centered * inverse).reshape(images, channels, cell_count)
    gain_column = norm_gain[None, :, None]
    pre_norm = normed * gain_column + norm_shift[None, :, None]
    sigmoid_pre = jax.nn.sigmoid(pre_norm)
    hidden = lax.optimization_barrier((pre_norm * sigmoid_pre).astype(jnp.bfloat16))
    frame_pad = ((0, 0), (0, 0), (1, 1), (1, 1))
    padded = jnp.pad(hidden.reshape(images, channels, height, column_count), frame_pad)
    conv_out = conv_taps(conv_weight, padded, height, column_count)
    residual = latents.reshape(images, channels, cell_count) + conv_out + conv_bias[None, :, None] - teacher.reshape(images, channels, cell_count)
    total_cells = images * cell_count
    mean_loss = (jnp.sum(jnp.square(residual)) / (total_cells * channels)).reshape(1)
    low_residual = lax.optimization_barrier(residual.astype(jnp.bfloat16))
    padded_residual = jnp.pad(low_residual.reshape(images, channels, height, column_count), frame_pad)
    grad_weight = weight_terms(low_residual, padded, height, column_count) / total_cells
    grad_hidden = transpose_taps(conv_weight, padded_residual, height, column_count)
    grad_pre = grad_hidden * sigmoid_pre * (1.0 + pre_norm * (1.0 - sigmoid_pre))
    param_grads = jnp.stack([lax.optimization_barrier(jnp.sum(residual, axis=(0, 2))), lax.optimization_barrier(jnp.sum(grad_pre * normed, axis=(0, 2))), lax.optimization_barrier(jnp.sum(grad_pre, axis=(0, 2)))]) / total_cells
    grad_norm = (grad_pre * gain_column).reshape(grouped.shape)
    normed_groups = normed.reshape(grouped.shape)
    first_mean = lax.optimization_barrier(jnp.mean(grad_norm, axis=(2, 3), keepdims=True))
    second_mean = lax.optimization_barrier(jnp.mean(grad_norm * normed_groups, axis=(2, 3), keepdims=True))
    grad_latents = residual.reshape(latents.shape) + (inverse * (grad_norm - first_mean - normed_groups * second_mean)).reshape(latents.shape)
    return (mean_loss, grad_latents, grad_weight, param_grads)
```

```python
import functools

import jax
import jax.numpy as jnp
from jax import lax
from jax.experimental import pallas as pl
from jax.experimental.pallas import tpu as pltpu
from jax.sharding import PartitionSpec as P

GROUPS = 32
LANES = 128
epsilon = 1e-05
F32 = jnp.float32
BF16 = jnp.bfloat16


def with_halo(shard, sides, width):
    for axis, dim in sides:
        devices, length = (lax.axis_size(axis), shard.shape[dim])
        up = [(i, (i + 1) % devices) for i in range(devices - 1)]
        down = [(j, i) for i, j in up]
        last = lax.slice_in_dim(shard, length - width, length, axis=dim)
        leading = lax.slice_in_dim(shard, 0, width, axis=dim)
        before = lax.ppermute(last, axis, up)
        after = lax.ppermute(leading, axis, down)
        shard = jnp.concatenate([before, shard, after], axis=dim)
    return shard


def conv_taps(weights, padded, strip_rows, column_count):
    running = None
    for tap_index in range(9):
        tap_row, tap_col = (tap_index // 3, tap_index % 3)
        window = padded[:, :, tap_row : tap_row + strip_rows, tap_col : tap_col + column_count]
        window = window.reshape(padded.shape[0], padded.shape[1], strip_rows * column_count)
        product = jnp.einsum(
            "oi,nip->nop", weights[:, tap_index, :], window, preferred_element_type=jnp.float32
        )
        running = product if running is None else running + product
    return running


def transpose_taps(weights, padded, strip_rows, column_count):
    running = None
    for tap_index in range(9):
        tap_row, tap_col = (tap_index // 3, tap_index % 3)
        window = padded[
            :, :, 2 - tap_row : 2 - tap_row + strip_rows, 2 - tap_col : 2 - tap_col + column_count
        ]
        window = window.reshape(padded.shape[0], padded.shape[1], strip_rows * column_count)
        product = jnp.einsum(
            "oi,nop->nip", weights[:, tap_index, :], window, preferred_element_type=jnp.float32
        )
        running = product if running is None else running + product
    return running


def weight_terms(residual, padded, strip_rows, column_count):
    columns = []
    for tap_index in range(9):
        tap_row, tap_col = (tap_index // 3, tap_index % 3)
        window = padded[:, :, tap_row : tap_row + strip_rows, tap_col : tap_col + column_count]
        window = window.reshape(padded.shape[0], padded.shape[1], strip_rows * column_count)
        columns.append(
            jnp.einsum("nop,nip->oi", residual, window, preferred_element_type=jnp.float32)
        )
    return jnp.stack(columns, axis=1)


def generic(latents, teacher, norm_gain, norm_shift, conv_weight, conv_bias):
    row_devices = lax.axis_size("rows")
    panel_devices = lax.axis_size("wt")
    images, channels, strip_rows, column_count = latents.shape
    cell_count = strip_rows * column_count
    total_cells = panel_devices * row_devices * cell_count
    group_cells = channels // GROUPS * cell_count * row_devices
    grouped = latents.reshape(images, GROUPS, channels // GROUPS, cell_count)
    group_sum, square_sum = lax.psum(
        (
            jnp.sum(grouped, axis=(2, 3), keepdims=True),
            jnp.sum(jnp.square(grouped), axis=(2, 3), keepdims=True),
        ),
        "rows",
    )
    group_mean = group_sum / group_cells
    centered = grouped - group_mean
    group_var = square_sum / group_cells - jnp.square(group_mean)
    inverse = lax.rsqrt(group_var + epsilon)
    normed = (centered * inverse).reshape(images, channels, cell_count)
    gain_column = norm_gain[None, :, None]
    pre_norm = normed * gain_column + norm_shift[None, :, None]
    sigmoid_pre = jax.nn.sigmoid(pre_norm)
    hidden = (pre_norm * sigmoid_pre).astype(jnp.bfloat16)
    column_pad = ((0, 0), (0, 0), (0, 0), (1, 1))
    framed_hidden = with_halo(
        hidden.reshape(images, channels, strip_rows, column_count), (("rows", 2),), 1
    )
    padded = jnp.pad(framed_hidden, column_pad)
    all_images = lax.all_gather(framed_hidden, "wt", axis=0, tiled=True)
    all_padded = jnp.pad(all_images, column_pad)
    conv_out = conv_taps(
        lax.all_gather(conv_weight, "wt", axis=0, tiled=True), padded, strip_rows, column_count
    )
    residual = (
        latents.reshape(images, channels, cell_count)
        + conv_out
        + conv_bias[None, :, None]
        - teacher.reshape(images, channels, cell_count)
    )
    low_residual = residual.astype(jnp.bfloat16)
    framed_residual = with_halo(
        low_residual.reshape(images, channels, strip_rows, column_count), (("rows", 2),), 1
    )
    padded_residual = jnp.pad(framed_residual, column_pad)
    panel_residual = lax.all_to_all(framed_residual, "wt", split_axis=1, concat_axis=0, tiled=True)
    panel_rows = channels // panel_devices
    panel_inner = panel_residual[:, :, 1 : strip_rows + 1, :].reshape(
        panel_residual.shape[0], panel_rows, cell_count
    )
    window = padded_residual
    grad_hidden = transpose_taps(
        lax.all_gather(conv_weight, "wt", axis=0, tiled=True), window, strip_rows, column_count
    )
    window = panel_inner
    weight_share = lax.psum_scatter(
        weight_terms(window, all_padded, strip_rows, column_count),
        "rows",
        scatter_dimension=0,
        tiled=True,
    )
    grad_weight = lax.all_gather(weight_share, "rows", axis=0, tiled=True) / total_cells
    grad_pre = grad_hidden * sigmoid_pre * (1.0 + pre_norm * (1.0 - sigmoid_pre))
    grad_norm = (grad_pre * gain_column).reshape(grouped.shape)
    normed_groups = normed.reshape(grouped.shape)
    first_sum, second_sum = lax.psum(
        (
            jnp.sum(grad_norm, axis=(2, 3), keepdims=True),
            jnp.sum(grad_norm * normed_groups, axis=(2, 3), keepdims=True),
        ),
        "rows",
    )
    first_mean = first_sum / group_cells
    second_mean = second_sum / group_cells
    grad_latents = residual.reshape(latents.shape) + (
        inverse * (grad_norm - first_mean - normed_groups * second_mean)
    ).reshape(latents.shape)
    totals = lax.psum(
        (
            jnp.sum(jnp.square(residual)),
            jnp.sum(residual, axis=(0, 2)),
            jnp.sum(grad_pre * normed, axis=(0, 2)),
            jnp.sum(grad_pre, axis=(0, 2)),
        ),
        ("rows", "wt"),
    )
    mean_loss = (totals[0] / (total_cells * channels)).reshape(1)
    param_grads = jnp.stack([totals[1], totals[2], totals[3]]) / total_cells
    return (mean_loss, grad_latents, grad_weight, param_grads)


def plane(ref, row, channels):
    return ref[pl.ds(row, channels, stride=2), :]


def split3(x):
    a = x.astype(BF16)
    rest = x - a.astype(F32)
    b = rest.astype(BF16)
    c = (rest - b.astype(F32)).astype(BF16)
    return a, b, c


def membership(channels):
    size = channels // GROUPS
    channel = lax.broadcasted_iota(jnp.int32, (channels, LANES), 0)
    first = lax.broadcasted_iota(jnp.int32, (channels, LANES), 1) * size
    inside = (channel >= first) & (channel < first + size)
    return jnp.where(inside, 1.0, 0.0).astype(BF16)


def dot_nn(a, b):
    return lax.dot_general(a, b, (((1,), (0,)), ((), ())), preferred_element_type=F32)


def dot_nt(a, b):
    return lax.dot_general(a, b, (((1,), (1,)), ((), ())), preferred_element_type=F32)


def group_sums(rows, member):
    a, b, c = split3(rows)
    return dot_nn(a, member) + (dot_nn(b, member) + dot_nn(c, member))


def to_channels(rows, member):
    a, b, c = split3(rows)
    return dot_nt(a, member) + (dot_nt(b, member) + dot_nt(c, member))


def as_rows(columns, channels):
    lane = lax.broadcasted_iota(jnp.int32, (channels, LANES), 1)
    table = jnp.zeros((channels, LANES), F32)
    for i, column in enumerate(columns):
        table = jnp.where(lane == i, column, table)
    return jnp.transpose(table)[:8, :]


def as_columns(rows, channels):
    pad = jnp.zeros((LANES - len(rows), channels), F32)
    return jnp.transpose(jnp.concatenate(rows + [pad], axis=0))


def row_sum(a, b):
    return jnp.sum(a + b, axis=1, keepdims=True)


def stats_kernel(lat, out):
    channels = out.shape[1]
    a, b = plane(lat, 0, channels), plane(lat, 1, channels)
    out[...] = as_rows([row_sum(a, b), row_sum(a * a, b * b)], channels)


def hidden_kernel(cells, lat, s0, s1, s2, s3, gain, shift, hidden, table):
    channels = s0.shape[1]
    member = membership(channels)
    sums = group_sums((s0[...] + s1[...]) + (s2[...] + s3[...]), member)
    mean = sums[0:1] / cells
    var = sums[1:2] / cells - mean * mean
    inverse = lax.rsqrt(var + epsilon)
    pad = jnp.zeros((6, LANES), F32)
    rows = to_channels(jnp.concatenate([mean, inverse, pad], axis=0), member)
    columns = as_columns([rows[0:1], rows[1:2], gain[...], shift[...]], channels)
    table[...] = columns
    for row in range(2):
        normed = (plane(lat, row, channels) - columns[:, 0:1]) * columns[:, 1:2]
        pre = normed * columns[:, 2:3] + columns[:, 3:4]
        hidden[row] = (pre * jax.nn.sigmoid(pre)).astype(BF16)


def shifts(x):
    wide = x.astype(F32)
    lane = lax.broadcasted_iota(jnp.int32, x.shape, 1)
    left = jnp.where(lane == 0, 0.0, pltpu.roll(wide, 1, 1)).astype(BF16)
    right = jnp.where(lane == LANES - 1, 0.0, pltpu.roll(wide, LANES - 1, 1)).astype(BF16)
    return left, x, right


def conv_kernel(
    place, near, far0, far1, far2, side, diag0, diag1, diag2, before, mine, after, lat, tea, bias,
    res, low, full, framed, total,
):
    me, part = place[0], place[1]
    panel = near.shape[1]
    channels = near.shape[2]

    def rows(k):
        return pl.ds(pl.multiple_of((me ^ k) * panel, panel), panel)

    for row, source in enumerate((before[0], mine[0], mine[1], after[0])):
        for kx, moved in enumerate(shifts(source)):
            framed[kx, row] = moved
    other = 1 - part

    def gather(i, carry):
        for first in (0, 3, 6):
            full[first + i, rows(0), :] = near[first + i]
            full[first + i, rows(1), :] = side[first + i]
        for k, first, second, third in ((2, far0, far1, far2), (3, diag0, diag1, diag2)):
            full[part * 3 + i, rows(k), :] = first[i]
            full[other * 3 + i, rows(k), :] = second[i]
            full[6 + i, rows(k), :] = third[i]
        return carry

    lax.fori_loop(0, 3, gather, 0)

    total[...] = jnp.zeros_like(total)

    def tap_step(tap, carry):
        ky = tap // 3
        kx = tap - 3 * ky
        window = jnp.concatenate([framed[kx, ky], framed[kx, ky + 1]], axis=1)
        total[...] += dot_nn(full[tap], window)
        return carry

    lax.fori_loop(0, 9, tap_step, 0)
    for row in range(2):
        value = (
            plane(lat, row, channels)
            + total[:, row * LANES : (row + 1) * LANES]
            + bias[:, 0:1]
            - plane(tea, row, channels)
        )
        res[row] = value
        low[row] = value.astype(BF16)


def back_kernel(full, before, low, after, res, lat, table, grad, sums, framed, total):
    channels = low.shape[1]
    for row, source in enumerate((before[0], low[0], low[1], after[0])):
        for kx, moved in enumerate(shifts(source)):
            framed[kx, row] = jnp.transpose(moved)
    total[...] = jnp.zeros_like(total)

    def tap_step(tap, carry):
        ky = tap // 3
        kx = tap - 3 * ky
        window = jnp.concatenate([framed[2 - kx, 2 - ky], framed[2 - kx, 3 - ky]], axis=0)
        total[...] += dot_nn(window, full[tap])
        return carry

    lax.fori_loop(0, 9, tap_step, 0)
    columns = table[...]
    first = second = bottom = loss = None
    for row in range(2):
        normed = (plane(lat, row, channels) - columns[:, 0:1]) * columns[:, 1:2]
        pre = normed * columns[:, 2:3] + columns[:, 3:4]
        s = jax.nn.sigmoid(pre)
        value = jnp.transpose(total[row * LANES : (row + 1) * LANES, :]) * s * (1.0 + pre * (1.0 - s))
        grad[row] = value
        r = res[row]
        terms = (value, value * normed, r, r * r)
        if row == 0:
            first, second, bottom, loss = terms
        else:
            first, second, bottom, loss = (
                first + terms[0], second + terms[1], bottom + terms[2], loss + terms[3],
            )
    add = functools.partial(jnp.sum, axis=1, keepdims=True)
    sums[...] = as_rows([add(first), add(second), add(bottom), add(loss)], channels)


def latents_kernel(cells, s0, s1, s2, s3, res, grad, lat, table, gain, out, both):
    channels = s0.shape[1]
    member = membership(channels)
    sums = (s0[...] + s1[...]) + (s2[...] + s3[...])
    both[...] = sums
    rows = sums * gain[...]
    means = group_sums(rows, member) / cells
    rows = to_channels(means, member)
    columns = as_columns([rows[0:1], rows[1:2]], channels)
    constants = table[...]
    inverse = constants[:, 1:2]
    for row in range(2):
        normed = (plane(lat, row, channels) - constants[:, 0:1]) * inverse
        change = grad[row] * constants[:, 2:3] - columns[:, 0:1] - normed * columns[:, 1:2]
        out[pl.ds(row, channels, stride=2), :] = res[row] + inverse * change


def weight_kernel(cells, place, *refs):
    panels, hiddens, out, spread, lefts = refs[:4], refs[4:20], refs[20], refs[21], refs[22]
    strip = place[0]
    panel = panels[0].shape[2]
    channels = hiddens[0].shape[1]
    for k in range(4):
        spread[k, 0] = jnp.zeros((channels, LANES), BF16)
        spread[k, 9] = jnp.zeros((channels, LANES), BF16)
        for m in range(4):
            for row in range(2):
                spread[k, 1 + 2 * (strip ^ m) + row] = hiddens[4 * m + k][row]
    for m in range(4):
        for k in range(4):
            for row in range(2):
                lane = pl.ds((2 * k + row) * LANES, LANES)
                moved = shifts(panels[m][k, row])
                for kx in range(3):
                    lefts[strip ^ m, kx * panel : (kx + 1) * panel, lane] = moved[2 - kx]
    out[...] = jnp.zeros_like(out)

    def step(i, carry):
        s = i // 3
        ky = i - 3 * s
        right = jnp.concatenate(
            [spread[k, 2 * s + ky + row] for k in range(4) for row in range(2)], axis=1
        )
        product = dot_nt(lefts[s], right).reshape(3, panel, channels)
        scale = jnp.where(s == 3, 1.0 / cells, 1.0)
        out[pl.ds(3 * ky, 3)] = (out[pl.ds(3 * ky, 3)] + product) * scale
        return carry

    lax.fori_loop(0, 12, step, 0)


VM = pl.BlockSpec(memory_space=pltpu.VMEM)
SM = pl.BlockSpec(memory_space=pltpu.SMEM)


def call(kernel, outs, specs, args, scratch=(), mib=8, us=3):
    return pl.pallas_call(
        kernel,
        out_shape=outs,
        in_specs=specs,
        out_specs=jax.tree.map(lambda _: VM, outs),
        scratch_shapes=scratch,
        compiler_params=pltpu.CompilerParams(vmem_limit_bytes=mib << 20),
        cost_estimate=pl.CostEstimate(
            flops=int(us * 1e9), bytes_accessed=int(us * 3e6), transcendentals=0
        ),
    )(*args)


def shape(dims, dtype):
    return jax.ShapeDtypeStruct(dims, dtype)


def swap(x, axis, mask):
    size = lax.axis_size(axis)
    return lax.ppermute(x, axis, [(i, i ^ mask) for i in range(size)])


def strips_of_four(latents, teacher, norm_gain, norm_shift, conv_weight, conv_bias):
    row_devices = lax.axis_size("rows")
    panel_devices = lax.axis_size("wt")
    _, channels, strip_rows, width = latents.shape
    panel = conv_weight.shape[0]
    strip_cells = strip_rows * width
    total_cells = panel_devices * row_devices * strip_cells
    group_cells = channels // GROUPS * strip_cells * row_devices
    up = [(i, i + 1) for i in range(row_devices - 1)]
    down = [(i + 1, i) for i in range(row_devices - 1)]
    lat = latents.reshape(channels * strip_rows, width)
    tea = teacher.reshape(channels * strip_rows, width)
    gain, shift = norm_gain.reshape(1, channels), norm_shift.reshape(1, channels)
    part = lax.axis_index("grp").astype(jnp.int32)
    here = lax.axis_index("wt").astype(jnp.int32)
    strip = lax.axis_index("rows").astype(jnp.int32)

    near = jnp.transpose(conv_weight, (1, 0, 2))
    far0 = swap(lax.dynamic_slice_in_dim(near, part * 3, 3, axis=0), "wt", 2)
    far2 = swap(near[6:9], "wt", 2)
    side = swap(near, "wt", 1)

    stats = call(stats_kernel, shape((8, channels), F32), [VM], (lat,))
    hidden, table = call(
        functools.partial(hidden_kernel, group_cells),
        (shape((strip_rows, channels, width), BF16), shape((channels, LANES), F32)),
        [VM] * 7,
        (lat, stats, *(swap(stats, "rows", m) for m in (1, 2, 3)), gain, shift),
    )
    before = lax.ppermute(hidden[1:2], "rows", up)
    after = lax.ppermute(hidden[0:1], "rows", down)
    far0, far2, hidden = lax.optimization_barrier((far0, far2, hidden))
    far1 = swap(far0, "grp", 1)
    own = [hidden] + [swap(hidden, "rows", m) for m in (1, 2, 3)]
    across = [swap(hidden, "wt", 2)]
    diag0, diag1, diag2 = swap(far0, "wt", 1), swap(far1, "wt", 1), swap(far2, "wt", 1)

    res, low, full = call(
        conv_kernel,
        (
            shape((strip_rows, channels, width), F32),
            shape((strip_rows, channels, width), BF16),
            shape((9, channels, channels), BF16),
        ),
        [SM] + [VM] * 14,
        (
            jnp.stack([here, part]), near, far0, far1, far2, side, diag0, diag1, diag2,
            before, hidden, after, lat, tea, conv_bias.reshape(channels, 1),
        ),
        [pltpu.VMEM((3, 4, channels, LANES), BF16), pltpu.VMEM((channels, 2 * LANES), F32)],
        mib=30, us=8,
    )

    low_before = lax.ppermute(low[1:2], "rows", up)
    low_after = lax.ppermute(low[0:1], "rows", down)

    def block(k):
        return lax.dynamic_slice_in_dim(low, (here ^ k) * panel, panel, axis=1)

    stacked = jnp.stack([block(0)] + [swap(block(k), "wt", k) for k in (1, 2, 3)])
    panels = [stacked] + [swap(stacked, "rows", m) for m in (1, 2, 3)]

    across += [swap(x, "wt", 2) for x in own[1:]]
    hiddens = []
    for x, y in zip(own, across):
        hiddens += [x, swap(x, "wt", 1), y, swap(y, "wt", 1)]

    grad, sums = call(
        back_kernel,
        (shape((strip_rows, channels, width), F32), shape((8, channels), F32)),
        [VM] * 7,
        (full, low_before, low, low_after, res, lat, table),
        [pltpu.VMEM((3, 4, LANES, channels), BF16), pltpu.VMEM((2 * LANES, channels), F32)],
        mib=22, us=8,
    )
    grad_latents, sums = call(
        functools.partial(latents_kernel, group_cells),
        (shape((channels * strip_rows, width), F32), shape((8, channels), F32)),
        [VM] * 9,
        (sums, *(swap(sums, "rows", m) for m in (1, 2, 3)), res, grad, lat, table, gain),
    )
    one, two, three = (swap(sums, "wt", m) for m in (1, 2, 3))
    sums = (sums + one) + (two + three)
    mean_loss = (jnp.sum(sums[3]) / (total_cells * channels)).reshape(1)
    param_grads = jnp.stack([sums[2], sums[1], sums[0]]) / total_cells

    grad_weight = call(
        functools.partial(weight_kernel, total_cells),
        shape((9, panel, channels), F32),
        [SM] + [VM] * 20,
        [strip.reshape(1)] + panels + hiddens,
        [
            pltpu.VMEM((4, 10, channels, LANES), BF16),
            pltpu.VMEM((4, 3 * panel, 8 * LANES), BF16),
        ],
        mib=34, us=15,
    )
    return (
        mean_loss,
        grad_latents.reshape(latents.shape),
        jnp.transpose(grad_weight, (1, 0, 2)),
        param_grads,
    )


def solution(mesh):
    placed = (
        P(("grp", "wt"), None, "rows", None),
        P(("grp", "wt"), None, "rows", None),
        P(),
        P(),
        P("wt", None, None),
        P(),
    )
    small = mesh.shape["rows"] == 4 and mesh.shape["wt"] == 4 and mesh.shape["grp"] == 2
    return jax.shard_map(
        strips_of_four if small else generic,
        mesh=mesh,
        in_specs=placed,
        out_specs=(
            P("grp"),
            P(("grp", "wt"), None, "rows", None),
            P(("grp", "wt"), None, None),
            P("grp", None),
        ),
        check_vma=False,
    )
```

```python
import functools

import jax
import jax.numpy as jnp
from jax import lax
from jax.experimental import pallas as pl
from jax.experimental.pallas import tpu as pltpu
from jax.sharding import PartitionSpec as P

GROUPS = 32
LANES = 128
epsilon = 1e-05
F32 = jnp.float32
BF16 = jnp.bfloat16


def with_halo(shard, sides, width):
    for axis, dim in sides:
        devices, length = (lax.axis_size(axis), shard.shape[dim])
        up = [(i, (i + 1) % devices) for i in range(devices - 1)]
        down = [(j, i) for i, j in up]
        last = lax.slice_in_dim(shard, length - width, length, axis=dim)
        leading = lax.slice_in_dim(shard, 0, width, axis=dim)
        before = lax.ppermute(last, axis, up)
        after = lax.ppermute(leading, axis, down)
        shard = jnp.concatenate([before, shard, after], axis=dim)
    return shard


def conv_taps(weights, padded, strip_rows, column_count):
    running = None
    for tap_index in range(9):
        tap_row, tap_col = (tap_index // 3, tap_index % 3)
        window = padded[:, :, tap_row : tap_row + strip_rows, tap_col : tap_col + column_count]
        window = window.reshape(padded.shape[0], padded.shape[1], strip_rows * column_count)
        product = jnp.einsum(
            "oi,nip->nop", weights[:, tap_index, :], window, preferred_element_type=jnp.float32
        )
        running = product if running is None else running + product
    return running


def transpose_taps(weights, padded, strip_rows, column_count):
    running = None
    for tap_index in range(9):
        tap_row, tap_col = (tap_index // 3, tap_index % 3)
        window = padded[
            :, :, 2 - tap_row : 2 - tap_row + strip_rows, 2 - tap_col : 2 - tap_col + column_count
        ]
        window = window.reshape(padded.shape[0], padded.shape[1], strip_rows * column_count)
        product = jnp.einsum(
            "oi,nop->nip", weights[:, tap_index, :], window, preferred_element_type=jnp.float32
        )
        running = product if running is None else running + product
    return running


def weight_terms(residual, padded, strip_rows, column_count):
    columns = []
    for tap_index in range(9):
        tap_row, tap_col = (tap_index // 3, tap_index % 3)
        window = padded[:, :, tap_row : tap_row + strip_rows, tap_col : tap_col + column_count]
        window = window.reshape(padded.shape[0], padded.shape[1], strip_rows * column_count)
        columns.append(
            jnp.einsum("nop,nip->oi", residual, window, preferred_element_type=jnp.float32)
        )
    return jnp.stack(columns, axis=1)


def generic(latents, teacher, norm_gain, norm_shift, conv_weight, conv_bias):
    row_devices = lax.axis_size("rows")
    panel_devices = lax.axis_size("wt")
    images, channels, strip_rows, column_count = latents.shape
    cell_count = strip_rows * column_count
    total_cells = panel_devices * row_devices * cell_count
    group_cells = channels // GROUPS * cell_count * row_devices
    grouped = latents.reshape(images, GROUPS, channels // GROUPS, cell_count)
    group_sum, square_sum = lax.psum(
        (
            jnp.sum(grouped, axis=(2, 3), keepdims=True),
            jnp.sum(jnp.square(grouped), axis=(2, 3), keepdims=True),
        ),
        "rows",
    )
    group_mean = group_sum / group_cells
    centered = grouped - group_mean
    group_var = square_sum / group_cells - jnp.square(group_mean)
    inverse = lax.rsqrt(group_var + epsilon)
    normed = (centered * inverse).reshape(images, channels, cell_count)
    gain_column = norm_gain[None, :, None]
    pre_norm = normed * gain_column + norm_shift[None, :, None]
    sigmoid_pre = jax.nn.sigmoid(pre_norm)
    hidden = (pre_norm * sigmoid_pre).astype(jnp.bfloat16)
    column_pad = ((0, 0), (0, 0), (0, 0), (1, 1))
    framed_hidden = with_halo(
        hidden.reshape(images, channels, strip_rows, column_count), (("rows", 2),), 1
    )
    padded = jnp.pad(framed_hidden, column_pad)
    all_images = lax.all_gather(framed_hidden, "wt", axis=0, tiled=True)
    all_padded = jnp.pad(all_images, column_pad)
    conv_out = conv_taps(
        lax.all_gather(conv_weight, "wt", axis=0, tiled=True), padded, strip_rows, column_count
    )
    residual = (
        latents.reshape(images, channels, cell_count)
        + conv_out
        + conv_bias[None, :, None]
        - teacher.reshape(images, channels, cell_count)
    )
    low_residual = residual.astype(jnp.bfloat16)
    framed_residual = with_halo(
        low_residual.reshape(images, channels, strip_rows, column_count), (("rows", 2),), 1
    )
    padded_residual = jnp.pad(framed_residual, column_pad)
    panel_residual = lax.all_to_all(framed_residual, "wt", split_axis=1, concat_axis=0, tiled=True)
    panel_rows = channels // panel_devices
    panel_inner = panel_residual[:, :, 1 : strip_rows + 1, :].reshape(
        panel_residual.shape[0], panel_rows, cell_count
    )
    window = padded_residual
    grad_hidden = transpose_taps(
        lax.all_gather(conv_weight, "wt", axis=0, tiled=True), window, strip_rows, column_count
    )
    window = panel_inner
    weight_share = lax.psum_scatter(
        weight_terms(window, all_padded, strip_rows, column_count),
        "rows",
        scatter_dimension=0,
        tiled=True,
    )
    grad_weight = lax.all_gather(weight_share, "rows", axis=0, tiled=True) / total_cells
    grad_pre = grad_hidden * sigmoid_pre * (1.0 + pre_norm * (1.0 - sigmoid_pre))
    grad_norm = (grad_pre * gain_column).reshape(grouped.shape)
    normed_groups = normed.reshape(grouped.shape)
    first_sum, second_sum = lax.psum(
        (
            jnp.sum(grad_norm, axis=(2, 3), keepdims=True),
            jnp.sum(grad_norm * normed_groups, axis=(2, 3), keepdims=True),
        ),
        "rows",
    )
    first_mean = first_sum / group_cells
    second_mean = second_sum / group_cells
    grad_latents = residual.reshape(latents.shape) + (
        inverse * (grad_norm - first_mean - normed_groups * second_mean)
    ).reshape(latents.shape)
    totals = lax.psum(
        (
            jnp.sum(jnp.square(residual)),
            jnp.sum(residual, axis=(0, 2)),
            jnp.sum(grad_pre * normed, axis=(0, 2)),
            jnp.sum(grad_pre, axis=(0, 2)),
        ),
        ("rows", "wt"),
    )
    mean_loss = (totals[0] / (total_cells * channels)).reshape(1)
    param_grads = jnp.stack([totals[1], totals[2], totals[3]]) / total_cells
    return (mean_loss, grad_latents, grad_weight, param_grads)


def plane(ref, row, channels):
    return ref[pl.ds(row, channels, stride=2), :]


def split3(x):
    a = x.astype(BF16)
    rest = x - a.astype(F32)
    b = rest.astype(BF16)
    c = (rest - b.astype(F32)).astype(BF16)
    return a, b, c


def membership(channels):
    size = channels // GROUPS
    channel = lax.broadcasted_iota(jnp.int32, (channels, LANES), 0)
    first = lax.broadcasted_iota(jnp.int32, (channels, LANES), 1) * size
    inside = (channel >= first) & (channel < first + size)
    return jnp.where(inside, 1.0, 0.0).astype(BF16)


def dot_nn(a, b):
    return lax.dot_general(a, b, (((1,), (0,)), ((), ())), preferred_element_type=F32)


def dot_nt(a, b):
    return lax.dot_general(a, b, (((1,), (1,)), ((), ())), preferred_element_type=F32)


def group_sums(rows, member):
    a, b, c = split3(rows)
    return dot_nn(a, member) + (dot_nn(b, member) + dot_nn(c, member))


def to_channels(rows, member):
    a, b, c = split3(rows)
    return dot_nt(a, member) + (dot_nt(b, member) + dot_nt(c, member))


def as_rows(columns, channels):
    lane = lax.broadcasted_iota(jnp.int32, (channels, LANES), 1)
    table = jnp.zeros((channels, LANES), F32)
    for i, column in enumerate(columns):
        table = jnp.where(lane == i, column, table)
    return jnp.transpose(table)[:8, :]


def as_columns(rows, channels):
    pad = jnp.zeros((LANES - len(rows), channels), F32)
    return jnp.transpose(jnp.concatenate(rows + [pad], axis=0))


def row_sum(a, b):
    return jnp.sum(a + b, axis=1, keepdims=True)


def stats_kernel(lat, out):
    channels = out.shape[1]
    a, b = plane(lat, 0, channels), plane(lat, 1, channels)
    out[...] = as_rows([row_sum(a, b), row_sum(a * a, b * b)], channels)


def hidden_kernel(cells, lat, s0, s1, s2, s3, given, hidden, table):
    channels = s0.shape[1]
    member = membership(channels)
    sums = group_sums((s0[...] + s1[...]) + (s2[...] + s3[...]), member)
    mean = sums[0:1] / cells
    var = sums[1:2] / cells - mean * mean
    inverse = lax.rsqrt(var + epsilon)
    pad = jnp.zeros((6, LANES), F32)
    rows = to_channels(jnp.concatenate([mean, inverse, pad], axis=0), member)
    columns = as_columns([rows[0:1], rows[1:2], given[0:1], given[1:2], given[2:3]], channels)
    table[...] = columns
    for row in range(2):
        normed = (plane(lat, row, channels) - columns[:, 0:1]) * columns[:, 1:2]
        pre = normed * columns[:, 2:3] + columns[:, 3:4]
        hidden[row] = (pre * jax.nn.sigmoid(pre)).astype(BF16)


def shifts(x):
    wide = x.astype(F32)
    lane = lax.broadcasted_iota(jnp.int32, x.shape, 1)
    left = jnp.where(lane == 0, 0.0, pltpu.roll(wide, 1, 1)).astype(BF16)
    right = jnp.where(lane == LANES - 1, 0.0, pltpu.roll(wide, LANES - 1, 1)).astype(BF16)
    return left, x, right


def frame_kernel(place, mine, above, below, lat, tea, table, framed, packed, base):
    strip = place[0]
    edge = jnp.zeros_like(mine[0])
    before = jnp.where(strip > 0, below[1], edge)
    after = jnp.where(strip < 3, above[0], edge)
    for row, source in enumerate((before, mine[0], mine[1], after)):
        for kx, moved in enumerate(shifts(source)):
            framed[kx, row] = moved
    packed[0] = mine[...]
    packed[1] = above[...]
    packed[2] = below[...]
    channels = mine.shape[1]
    for row in range(2):
        base[row] = plane(lat, row, channels) + table[:, 4:5] - plane(tea, row, channels)


def panel_rows(me, k, panel):
    return pl.ds(pl.multiple_of((me ^ k) * panel, panel), panel)


def conv_step(total, framed, ky, kx, first, second):
    window = jnp.concatenate([framed[kx, ky], framed[kx, ky + 1]], axis=1)
    total[...] += dot_nn(jnp.concatenate([first, second], axis=0), window)


def near_conv_kernel(place, near, side, framed, base, part, block0, block1, total):
    me = place[1]
    panel = near.shape[1]
    total[...] = jnp.zeros_like(total)

    def step(tap, carry):
        ky = tap // 3
        conv_step(total, framed, ky, tap - 3 * ky, near[tap], side[tap])
        return carry

    lax.fori_loop(0, 9, step, 0)
    for k, block in enumerate((block0, block1)):
        for row in range(2):
            value = base[row, panel_rows(me, k, panel), :] + (
                total[k * panel : (k + 1) * panel, row * LANES : (row + 1) * LANES]
            )
            part[k, row] = value
            block[row] = value.astype(BF16)


def far_conv_kernel(
    place, far0, far1, far2, diag0, diag1, diag2, framed, base, part, res, low, block23, total
):
    me, half = place[1], place[2]
    panel = far0.shape[1]
    total[...] = jnp.zeros_like(total)

    def step(i, carry):
        conv_step(total, framed, half, i, far0[i], diag0[i])
        conv_step(total, framed, 1 - half, i, far1[i], diag1[i])
        conv_step(total, framed, 2, i, far2[i], diag2[i])
        return carry

    lax.fori_loop(0, 3, step, 0)
    for k in range(4):
        rows = panel_rows(me, k, panel)
        for row in range(2):
            if k < 2:
                value = part[k, row]
            else:
                value = base[row, rows, :] + (
                    total[(k - 2) * panel : (k - 1) * panel, row * LANES : (row + 1) * LANES]
                )
                block23[k - 2, row] = value.astype(BF16)
            res[row, rows, :] = value
            low[row, rows, :] = value.astype(BF16)


def back_kernel(
    place, near, side, far0, far1, far2, diag0, diag1, diag2, before, low, after, res, lat, table,
    grad, sums, framed, total, full,
):
    me, half = place[1], place[2]
    panel, channels = near.shape[1:]
    other = 1 - half

    def gather(i, carry):
        for first in (0, 3, 6):
            full[first + i, panel_rows(me, 0, panel), :] = near[first + i]
            full[first + i, panel_rows(me, 1, panel), :] = side[first + i]
        for k, first, second, third in ((2, far0, far1, far2), (3, diag0, diag1, diag2)):
            rows = panel_rows(me, k, panel)
            full[half * 3 + i, rows, :] = first[i]
            full[other * 3 + i, rows, :] = second[i]
            full[6 + i, rows, :] = third[i]
        return carry

    lax.fori_loop(0, 3, gather, 0)
    for row, source in enumerate((before[0], low[0], low[1], after[0])):
        for kx, moved in enumerate(shifts(source)):
            framed[kx, row] = jnp.transpose(moved)
    total[...] = jnp.zeros_like(total)

    def tap_step(tap, carry):
        ky = tap // 3
        kx = tap - 3 * ky
        window = jnp.concatenate([framed[2 - kx, 2 - ky], framed[2 - kx, 3 - ky]], axis=0)
        total[...] += dot_nn(window, full[tap])
        return carry

    lax.fori_loop(0, 9, tap_step, 0)
    columns = table[...]
    first = second = bottom = loss = None
    for row in range(2):
        normed = (plane(lat, row, channels) - columns[:, 0:1]) * columns[:, 1:2]
        pre = normed * columns[:, 2:3] + columns[:, 3:4]
        s = jax.nn.sigmoid(pre)
        value = jnp.transpose(total[row * LANES : (row + 1) * LANES, :]) * s * (1.0 + pre * (1.0 - s))
        grad[row] = value
        r = res[row]
        terms = (value, value * normed, r, r * r)
        if row == 0:
            first, second, bottom, loss = terms
        else:
            first, second, bottom, loss = (
                first + terms[0], second + terms[1], bottom + terms[2], loss + terms[3],
            )
    add = functools.partial(jnp.sum, axis=1, keepdims=True)
    sums[...] = as_rows([add(first), add(second), add(bottom), add(loss)], channels)


def latents_kernel(cells, total, given, res, grad, lat, table, out):
    channels = total.shape[1]
    member = membership(channels)
    rows = total[...] * given[0:1]
    means = group_sums(rows, member) / cells
    rows = to_channels(means, member)
    columns = as_columns([rows[0:1], rows[1:2]], channels)
    constants = table[...]
    inverse = constants[:, 1:2]
    for row in range(2):
        normed = (plane(lat, row, channels) - constants[:, 0:1]) * inverse
        change = grad[row] * constants[:, 2:3] - columns[:, 0:1] - normed * columns[:, 1:2]
        out[pl.ds(row, channels, stride=2), :] = res[row] + inverse * change


def weight_pair(place, pair, panels, spread, lefts, emit):
    panel, channels = panels[0].shape[2], spread.shape[2]
    for m in range(2):
        for k in range(4):
            for row in range(2):
                lane = pl.ds((2 * k + row) * LANES, LANES)
                moved = shifts(panels[m][k, row])
                for kx in range(3):
                    lefts[(place & 1) ^ m, kx * panel : (kx + 1) * panel, lane] = moved[2 - kx]

    def step(ky, carry):
        product = None
        for m in range(2):
            right = jnp.concatenate(
                [spread[k, 4 * pair + 2 * m + ky + row] for k in range(4) for row in range(2)], axis=1
            )
            part = dot_nt(lefts[m], right)
            product = part if product is None else product + part
        emit(pl.ds(3 * ky, 3), product.reshape(3, panel, channels))
        return carry

    lax.fori_loop(0, 3, step, 0)


def near_weight_kernel(place, *refs):
    panels, threes, ones, out, spread, lefts = refs[:2], refs[2:6], refs[6:10], refs[10], refs[11], refs[12]
    strip = place[0]
    channels = spread.shape[2]
    for k in range(4):
        spread[k, 0] = jnp.zeros((channels, LANES), BF16)
        spread[k, 9] = jnp.zeros((channels, LANES), BF16)
        for m, source in ((0, threes[k].at[0]), (1, threes[k].at[1]), (3, threes[k].at[2]), (2, ones[k])):
            for row in range(2):
                spread[k, 1 + 2 * ((strip + m) & 3) + row] = source[row]

    def emit(taps, product):
        out[taps] = product

    weight_pair(strip, strip // 2, panels, spread, lefts, emit)


def far_weight_kernel(cells, place, panel2, panel3, spread, near, out, lefts):
    strip = place[0]

    def emit(taps, product):
        out[taps] = (near[taps] + product) / cells

    weight_pair(strip, 1 - strip // 2, (panel2, panel3), spread, lefts, emit)


VM = pl.BlockSpec(memory_space=pltpu.VMEM)
SM = pl.BlockSpec(memory_space=pltpu.SMEM)


def call(kernel, outs, specs, args, scratch=(), mib=8, us=3):
    return pl.pallas_call(
        kernel,
        out_shape=outs,
        in_specs=specs,
        out_specs=jax.tree.map(lambda _: VM, outs),
        scratch_shapes=scratch,
        compiler_params=pltpu.CompilerParams(vmem_limit_bytes=mib << 20),
        cost_estimate=pl.CostEstimate(
            flops=int(us * 1e9), bytes_accessed=int(us * 3e6), transcendentals=0
        ),
    )(*args)


def shape(dims, dtype):
    return jax.ShapeDtypeStruct(dims, dtype)


def swap(x, axis, mask):
    size = lax.axis_size(axis)
    return lax.ppermute(x, axis, [(i, i ^ mask) for i in range(size)])


def ring(x, axis, step):
    size = lax.axis_size(axis)
    return lax.ppermute(x, axis, [((i + step) % size, i) for i in range(size)])


def after_all(x, *others):
    return lax.optimization_barrier((x, *others))[0]


def strips_of_four(latents, teacher, norm_gain, norm_shift, conv_weight, conv_bias):
    row_devices = lax.axis_size("rows")
    panel_devices = lax.axis_size("wt")
    _, channels, strip_rows, width = latents.shape
    panel = conv_weight.shape[0]
    strip_cells = strip_rows * width
    total_cells = panel_devices * row_devices * strip_cells
    group_cells = channels // GROUPS * strip_cells * row_devices
    up = [(i, i + 1) for i in range(row_devices - 1)]
    down = [(i + 1, i) for i in range(row_devices - 1)]
    lat = latents.reshape(channels * strip_rows, width)
    tea = teacher.reshape(channels * strip_rows, width)
    given = jnp.stack([norm_gain, norm_shift, conv_bias])
    part = lax.axis_index("grp").astype(jnp.int32)
    here = lax.axis_index("wt").astype(jnp.int32)
    strip = lax.axis_index("rows").astype(jnp.int32)
    place = jnp.stack([strip, here, part])

    near = jnp.transpose(conv_weight, (1, 0, 2))
    far0 = swap(lax.dynamic_slice_in_dim(near, part * 3, 3, axis=0), "wt", 2)
    side = swap(near, "wt", 1)

    stats = call(stats_kernel, shape((8, channels), F32), [VM], (lat,))
    hidden, table = call(
        functools.partial(hidden_kernel, group_cells),
        (shape((strip_rows, channels, width), BF16), shape((channels, LANES), F32)),
        [VM] * 6,
        (lat, after_all(stats, far0, side), *(swap(stats, "rows", m) for m in (1, 2, 3)), given),
    )
    above, below = ring(hidden, "rows", 1), ring(hidden, "rows", 3)
    far1 = swap(after_all(far0, hidden), "grp", 1)
    far2 = swap(after_all(near, hidden)[6:9], "wt", 2)
    framed, packed, base = call(
        frame_kernel,
        (
            shape((3, 4, channels, width), BF16),
            shape((3, strip_rows, channels, width), BF16),
            shape((strip_rows, channels, width), F32),
        ),
        [SM] + [VM] * 6,
        (place, after_all(hidden, far1, far2), above, below, lat, tea, table),
        us=10,
    )
    beyond = ring(hidden, "rows", 2)
    threes = [packed, None, swap(packed, "wt", 2), None]
    part0, block0, block1 = call(
        near_conv_kernel,
        (
            shape((2, strip_rows, panel, width), F32),
            shape((strip_rows, panel, width), BF16),
            shape((strip_rows, panel, width), BF16),
        ),
        [SM] + [VM] * 4,
        (place, near, side, framed, base),
        [pltpu.VMEM((2 * panel, 2 * LANES), F32)],
        us=20,
    )
    far0, far1, far2, _ = lax.optimization_barrier((far0, far1, far2, framed))
    diag0, diag1, diag2 = swap(far0, "wt", 1), swap(far1, "wt", 1), swap(far2, "wt", 1)
    weights = (near, side, far0, far1, far2, diag0, diag1, diag2)
    res, low, block23 = call(
        far_conv_kernel,
        (
            shape((strip_rows, channels, width), F32),
            shape((strip_rows, channels, width), BF16),
            shape((2, strip_rows, panel, width), BF16),
        ),
        [SM] + [VM] * 9,
        (place, *weights[2:], framed, base, part0),
        [pltpu.VMEM((2 * panel, 2 * LANES), F32)],
        us=0.05,
    )

    low_before = lax.ppermute(low[1:2], "rows", up)
    low_after = lax.ppermute(low[0:1], "rows", down)
    block1 = swap(block1, "wt", 1)
    block23 = swap(block23, "wt", 2)
    stacked = after_all(jnp.stack([block0, block1, block23[0], swap(block23[1], "wt", 1)]), beyond)
    panels = [stacked] + [swap(stacked, "rows", m) for m in (1, 3, 2)]
    panels[2:] = panels[:1:-1]

    ones = [beyond, None, swap(beyond, "wt", 2), None]
    for k in (0, 2):
        threes[k + 1], ones[k + 1] = swap(threes[k], "wt", 1), swap(ones[k], "wt", 1)

    grad, sums = call(
        back_kernel,
        (shape((strip_rows, channels, width), F32), shape((8, channels), F32)),
        [SM] + [VM] * 14,
        (
            place, *weights, low_before, after_all(low, panels[1], threes[2]), low_after, res, lat, table,
        ),
        [
            pltpu.VMEM((3, 4, LANES, channels), BF16),
            pltpu.VMEM((2 * LANES, channels), F32),
            pltpu.VMEM((9, channels, channels), BF16),
        ],
        mib=20, us=30,
    )
    sums = after_all(sums, panels[3])
    one, two, three = (swap(sums, "rows", m) for m in (1, 2, 3))
    sums = (sums + one) + (two + three)
    near_weight, spread = call(
        near_weight_kernel,
        (shape((9, panel, channels), F32), shape((4, 10, channels, width), BF16)),
        [SM] + [VM] * 10,
        [after_all(place, sums)] + panels[:2] + threes + ones,
        [pltpu.VMEM((2, 3 * panel, 8 * LANES), BF16)],
        mib=12, us=30,
    )
    grad_latents = call(
        functools.partial(latents_kernel, group_cells),
        shape((channels * strip_rows, width), F32),
        [VM] * 6,
        (after_all(sums, near_weight, panels[2]), given, res, grad, lat, table),
        us=0.05,
    )
    one, two, three = (swap(sums, "wt", m) for m in (1, 2, 3))
    sums = (sums + one) + (two + three)
    mean_loss = (jnp.sum(sums[3]) / (total_cells * channels)).reshape(1)
    param_grads = jnp.stack([sums[2], sums[1], sums[0]]) / total_cells

    grad_weight = call(
        functools.partial(far_weight_kernel, total_cells),
        shape((9, panel, channels), F32),
        [SM] + [VM] * 4,
        [place] + panels[2:] + [spread, near_weight],
        [pltpu.VMEM((2, 3 * panel, 8 * LANES), BF16)],
        mib=14, us=0.05,
    )
    return (
        mean_loss,
        grad_latents.reshape(latents.shape),
        jnp.transpose(grad_weight, (1, 0, 2)),
        param_grads,
    )


def solution(mesh):
    placed = (
        P(("grp", "wt"), None, "rows", None),
        P(("grp", "wt"), None, "rows", None),
        P(),
        P(),
        P("wt", None, None),
        P(),
    )
    small = mesh.shape["rows"] == 4 and mesh.shape["wt"] == 4 and mesh.shape["grp"] == 2
    return jax.shard_map(
        strips_of_four if small else generic,
        mesh=mesh,
        in_specs=placed,
        out_specs=(
            P("grp"),
            P(("grp", "wt"), None, "rows", None),
            P(("grp", "wt"), None, None),
            P("grp", None),
        ),
        check_vma=False,
    )
```

```python
import functools

import jax
import jax.numpy as jnp
from jax import lax
from jax.experimental import pallas as pl
from jax.experimental.pallas import tpu as pltpu
from jax.sharding import PartitionSpec as P

GROUPS = 32
LANES = 128
epsilon = 1e-05
F32 = jnp.float32
BF16 = jnp.bfloat16


def with_halo(shard, sides, width):
    for axis, dim in sides:
        devices, length = (lax.axis_size(axis), shard.shape[dim])
        up = [(i, (i + 1) % devices) for i in range(devices - 1)]
        down = [(j, i) for i, j in up]
        last = lax.slice_in_dim(shard, length - width, length, axis=dim)
        leading = lax.slice_in_dim(shard, 0, width, axis=dim)
        before = lax.ppermute(last, axis, up)
        after = lax.ppermute(leading, axis, down)
        shard = jnp.concatenate([before, shard, after], axis=dim)
    return shard


def conv_taps(weights, padded, strip_rows, column_count):
    running = None
    for tap_index in range(9):
        tap_row, tap_col = (tap_index // 3, tap_index % 3)
        window = padded[:, :, tap_row : tap_row + strip_rows, tap_col : tap_col + column_count]
        window = window.reshape(padded.shape[0], padded.shape[1], strip_rows * column_count)
        product = jnp.einsum(
            "oi,nip->nop", weights[:, tap_index, :], window, preferred_element_type=jnp.float32
        )
        running = product if running is None else running + product
    return running


def transpose_taps(weights, padded, strip_rows, column_count):
    running = None
    for tap_index in range(9):
        tap_row, tap_col = (tap_index // 3, tap_index % 3)
        window = padded[
            :, :, 2 - tap_row : 2 - tap_row + strip_rows, 2 - tap_col : 2 - tap_col + column_count
        ]
        window = window.reshape(padded.shape[0], padded.shape[1], strip_rows * column_count)
        product = jnp.einsum(
            "oi,nop->nip", weights[:, tap_index, :], window, preferred_element_type=jnp.float32
        )
        running = product if running is None else running + product
    return running


def weight_terms(residual, padded, strip_rows, column_count):
    columns = []
    for tap_index in range(9):
        tap_row, tap_col = (tap_index // 3, tap_index % 3)
        window = padded[:, :, tap_row : tap_row + strip_rows, tap_col : tap_col + column_count]
        window = window.reshape(padded.shape[0], padded.shape[1], strip_rows * column_count)
        columns.append(
            jnp.einsum("nop,nip->oi", residual, window, preferred_element_type=jnp.float32)
        )
    return jnp.stack(columns, axis=1)


def generic(latents, teacher, norm_gain, norm_shift, conv_weight, conv_bias):
    row_devices = lax.axis_size("rows")
    panel_devices = lax.axis_size("wt")
    images, channels, strip_rows, column_count = latents.shape
    cell_count = strip_rows * column_count
    total_cells = panel_devices * row_devices * cell_count
    group_cells = channels // GROUPS * cell_count * row_devices
    grouped = latents.reshape(images, GROUPS, channels // GROUPS, cell_count)
    group_sum, square_sum = lax.psum(
        (
            jnp.sum(grouped, axis=(2, 3), keepdims=True),
            jnp.sum(jnp.square(grouped), axis=(2, 3), keepdims=True),
        ),
        "rows",
    )
    group_mean = group_sum / group_cells
    centered = grouped - group_mean
    group_var = square_sum / group_cells - jnp.square(group_mean)
    inverse = lax.rsqrt(group_var + epsilon)
    normed = (centered * inverse).reshape(images, channels, cell_count)
    gain_column = norm_gain[None, :, None]
    pre_norm = normed * gain_column + norm_shift[None, :, None]
    sigmoid_pre = jax.nn.sigmoid(pre_norm)
    hidden = (pre_norm * sigmoid_pre).astype(jnp.bfloat16)
    column_pad = ((0, 0), (0, 0), (0, 0), (1, 1))
    framed_hidden = with_halo(
        hidden.reshape(images, channels, strip_rows, column_count), (("rows", 2),), 1
    )
    padded = jnp.pad(framed_hidden, column_pad)
    all_images = lax.all_gather(framed_hidden, "wt", axis=0, tiled=True)
    all_padded = jnp.pad(all_images, column_pad)
    conv_out = conv_taps(
        lax.all_gather(conv_weight, "wt", axis=0, tiled=True), padded, strip_rows, column_count
    )
    residual = (
        latents.reshape(images, channels, cell_count)
        + conv_out
        + conv_bias[None, :, None]
        - teacher.reshape(images, channels, cell_count)
    )
    low_residual = residual.astype(jnp.bfloat16)
    framed_residual = with_halo(
        low_residual.reshape(images, channels, strip_rows, column_count), (("rows", 2),), 1
    )
    padded_residual = jnp.pad(framed_residual, column_pad)
    panel_residual = lax.all_to_all(framed_residual, "wt", split_axis=1, concat_axis=0, tiled=True)
    panel_rows = channels // panel_devices
    panel_inner = panel_residual[:, :, 1 : strip_rows + 1, :].reshape(
        panel_residual.shape[0], panel_rows, cell_count
    )
    window = padded_residual
    grad_hidden = transpose_taps(
        lax.all_gather(conv_weight, "wt", axis=0, tiled=True), window, strip_rows, column_count
    )
    window = panel_inner
    weight_share = lax.psum_scatter(
        weight_terms(window, all_padded, strip_rows, column_count),
        "rows",
        scatter_dimension=0,
        tiled=True,
    )
    grad_weight = lax.all_gather(weight_share, "rows", axis=0, tiled=True) / total_cells
    grad_pre = grad_hidden * sigmoid_pre * (1.0 + pre_norm * (1.0 - sigmoid_pre))
    grad_norm = (grad_pre * gain_column).reshape(grouped.shape)
    normed_groups = normed.reshape(grouped.shape)
    first_sum, second_sum = lax.psum(
        (
            jnp.sum(grad_norm, axis=(2, 3), keepdims=True),
            jnp.sum(grad_norm * normed_groups, axis=(2, 3), keepdims=True),
        ),
        "rows",
    )
    first_mean = first_sum / group_cells
    second_mean = second_sum / group_cells
    grad_latents = residual.reshape(latents.shape) + (
        inverse * (grad_norm - first_mean - normed_groups * second_mean)
    ).reshape(latents.shape)
    totals = lax.psum(
        (
            jnp.sum(jnp.square(residual)),
            jnp.sum(residual, axis=(0, 2)),
            jnp.sum(grad_pre * normed, axis=(0, 2)),
            jnp.sum(grad_pre, axis=(0, 2)),
        ),
        ("rows", "wt"),
    )
    mean_loss = (totals[0] / (total_cells * channels)).reshape(1)
    param_grads = jnp.stack([totals[1], totals[2], totals[3]]) / total_cells
    return (mean_loss, grad_latents, grad_weight, param_grads)


def plane(ref, row, channels):
    return ref[pl.ds(row, channels, stride=2), :]


def split3(x):
    a = x.astype(BF16)
    rest = x - a.astype(F32)
    b = rest.astype(BF16)
    c = (rest - b.astype(F32)).astype(BF16)
    return a, b, c


def membership(channels):
    size = channels // GROUPS
    channel = lax.broadcasted_iota(jnp.int32, (channels, LANES), 0)
    first = lax.broadcasted_iota(jnp.int32, (channels, LANES), 1) * size
    inside = (channel >= first) & (channel < first + size)
    return jnp.where(inside, 1.0, 0.0).astype(BF16)


def dot_nn(a, b):
    return lax.dot_general(a, b, (((1,), (0,)), ((), ())), preferred_element_type=F32)


def dot_nt(a, b):
    return lax.dot_general(a, b, (((1,), (1,)), ((), ())), preferred_element_type=F32)


def group_sums(rows, member):
    a, b, c = split3(rows)
    return dot_nn(a, member) + (dot_nn(b, member) + dot_nn(c, member))


def to_channels(rows, member):
    a, b, c = split3(rows)
    return dot_nt(a, member) + (dot_nt(b, member) + dot_nt(c, member))


def as_rows(columns, channels):
    lane = lax.broadcasted_iota(jnp.int32, (channels, LANES), 1)
    table = jnp.zeros((channels, LANES), F32)
    for i, column in enumerate(columns):
        table = jnp.where(lane == i, column, table)
    return jnp.transpose(table)[:8, :]


def as_columns(rows, channels):
    pad = jnp.zeros((LANES - len(rows), channels), F32)
    return jnp.transpose(jnp.concatenate(rows + [pad], axis=0))


def row_sum(a, b):
    return jnp.sum(a + b, axis=1, keepdims=True)


def stats_kernel(lat, out):
    channels = out.shape[1]
    a, b = plane(lat, 0, channels), plane(lat, 1, channels)
    out[...] = as_rows([row_sum(a, b), row_sum(a * a, b * b)], channels)


def hidden_kernel(cells, lat, s0, s1, s2, s3, given, hidden, table):
    channels = s0.shape[1]
    member = membership(channels)
    sums = group_sums((s0[...] + s1[...]) + (s2[...] + s3[...]), member)
    mean = sums[0:1] / cells
    var = sums[1:2] / cells - mean * mean
    inverse = lax.rsqrt(var + epsilon)
    pad = jnp.zeros((6, LANES), F32)
    rows = to_channels(jnp.concatenate([mean, inverse, pad], axis=0), member)
    columns = as_columns([rows[0:1], rows[1:2], given[0:1], given[1:2], given[2:3]], channels)
    table[...] = columns
    for row in range(2):
        normed = (plane(lat, row, channels) - columns[:, 0:1]) * columns[:, 1:2]
        pre = normed * columns[:, 2:3] + columns[:, 3:4]
        hidden[row] = (pre * jax.nn.sigmoid(pre)).astype(BF16)


def shifts(x):
    wide = x.astype(F32)
    lane = lax.broadcasted_iota(jnp.int32, x.shape, 1)
    left = jnp.where(lane == 0, 0.0, pltpu.roll(wide, 1, 1)).astype(BF16)
    right = jnp.where(lane == LANES - 1, 0.0, pltpu.roll(wide, LANES - 1, 1)).astype(BF16)
    return left, x, right


def base_kernel(lat, tea, table, base):
    channels = table.shape[0]
    for row in range(2):
        base[row] = plane(lat, row, channels) + table[:, 4:5] - plane(tea, row, channels)


def frame_kernel(place, mine, above, below, framed, packed):
    strip = place[0]
    edge = jnp.zeros_like(mine[0])
    before = jnp.where(strip > 0, below[1], edge)
    after = jnp.where(strip < 3, above[0], edge)
    for row, source in enumerate((before, mine[0], mine[1], after)):
        for kx, moved in enumerate(shifts(source)):
            framed[kx, row] = moved
    packed[0] = mine[...]
    packed[1] = above[...]
    packed[2] = below[...]


def panel_rows(me, k, panel):
    return pl.ds(pl.multiple_of((me ^ k) * panel, panel), panel)


def conv_step(total, framed, ky, kx, first, second):
    window = jnp.concatenate([framed[kx, ky], framed[kx, ky + 1]], axis=1)
    total[...] += dot_nn(jnp.concatenate([first, second], axis=0), window)


def near_conv_kernel(place, near, side, framed, base, part, block0, block1, total):
    me = place[1]
    panel = near.shape[1]
    total[...] = jnp.zeros_like(total)

    def step(tap, carry):
        ky = tap // 3
        conv_step(total, framed, ky, tap - 3 * ky, near[tap], side[tap])
        return carry

    lax.fori_loop(0, 9, step, 0)
    for k, block in enumerate((block0, block1)):
        for row in range(2):
            value = base[row, panel_rows(me, k, panel), :] + (
                total[k * panel : (k + 1) * panel, row * LANES : (row + 1) * LANES]
            )
            part[k, row] = value
            block[row] = value.astype(BF16)


def far_conv_kernel(
    place, far0, far1, far2, diag0, diag1, diag2, framed, base, part, res, low, block23, total
):
    me, half = place[1], place[2]
    panel = far0.shape[1]
    total[...] = jnp.zeros_like(total)

    def run(first, far, diag):
        def step(i, carry):
            tap = first + i
            ky = tap // 3
            conv_step(total, framed, ky, tap - 3 * ky, far[i], diag[i])
            return carry

        lax.fori_loop(0, far.shape[0], step, 0)

    run(2 * half, far0, diag0)
    run(2 - 2 * half, far1, diag1)
    run(4, far2, diag2)
    for k in range(4):
        rows = panel_rows(me, k, panel)
        for row in range(2):
            if k < 2:
                value = part[k, row]
            else:
                value = base[row, rows, :] + (
                    total[(k - 2) * panel : (k - 1) * panel, row * LANES : (row + 1) * LANES]
                )
                block23[k - 2, row] = value.astype(BF16)
            res[row, rows, :] = value
            low[row, rows, :] = value.astype(BF16)


def assemble_kernel(place, near, side, far0, far1, far2, diag0, diag1, diag2, full):
    me, half = place[1], place[2]
    panel = near.shape[1]
    near_taps, side_taps = panel_rows(me, 0, panel), panel_rows(me, 1, panel)
    far_taps, diag_taps = panel_rows(me, 2, panel), panel_rows(me, 3, panel)

    def local(tap, carry):
        full[tap, near_taps, :] = near[tap]
        full[tap, side_taps, :] = side[tap]
        return carry

    lax.fori_loop(0, 9, local, 0)
    for first, far, diag in ((2 * half, far0, diag0), (2 - 2 * half, far1, diag1), (4, far2, diag2)):
        def remote(i, carry, first=first, far=far, diag=diag):
            full[first + i, far_taps, :] = far[i]
            full[first + i, diag_taps, :] = diag[i]
            return carry

        lax.fori_loop(0, far.shape[0], remote, 0)


def back_kernel(full, before, low, after, res, lat, table, grad, sums, framed, total):
    channels = low.shape[1]
    for row, source in enumerate((before[0], low[0], low[1], after[0])):
        for kx, moved in enumerate(shifts(source)):
            framed[kx, row] = jnp.transpose(moved)
    total[...] = jnp.zeros_like(total)

    def tap_step(tap, carry):
        ky = tap // 3
        kx = tap - 3 * ky
        window = jnp.concatenate([framed[2 - kx, 2 - ky], framed[2 - kx, 3 - ky]], axis=0)
        total[...] += dot_nn(window, full[tap])
        return carry

    lax.fori_loop(0, 9, tap_step, 0)
    columns = table[...]
    first = second = bottom = loss = None
    for row in range(2):
        normed = (plane(lat, row, channels) - columns[:, 0:1]) * columns[:, 1:2]
        pre = normed * columns[:, 2:3] + columns[:, 3:4]
        s = jax.nn.sigmoid(pre)
        value = jnp.transpose(total[row * LANES : (row + 1) * LANES, :]) * s * (1.0 + pre * (1.0 - s))
        grad[row] = value
        r = res[row]
        terms = (value, value * normed, r, r * r)
        if row == 0:
            first, second, bottom, loss = terms
        else:
            first, second, bottom, loss = (
                first + terms[0], second + terms[1], bottom + terms[2], loss + terms[3],
            )
    add = functools.partial(jnp.sum, axis=1, keepdims=True)
    sums[...] = as_rows([add(first), add(second), add(bottom), add(loss)], channels)


def latents_kernel(cells, total, given, res, grad, lat, table, out):
    channels = total.shape[1]
    member = membership(channels)
    rows = total[...] * given[0:1]
    means = group_sums(rows, member) / cells
    rows = to_channels(means, member)
    columns = as_columns([rows[0:1], rows[1:2]], channels)
    constants = table[...]
    inverse = constants[:, 1:2]
    for row in range(2):
        normed = (plane(lat, row, channels) - constants[:, 0:1]) * inverse
        change = grad[row] * constants[:, 2:3] - columns[:, 0:1] - normed * columns[:, 1:2]
        out[pl.ds(row, channels, stride=2), :] = res[row] + inverse * change


def weight_pair(strip, pair, aligned, one, two, first, spread, lefts, emit):
    panel, channels = aligned.shape[2], spread.shape[2]
    for m in range(2):
        for k in range(4):
            for row in range(2):
                lane = pl.ds((2 * k + row) * LANES, LANES)
                source = aligned[k, row] if m == 0 else jnp.where(first, one[k, row], two[k, row])
                moved = shifts(source)
                for kx in range(3):
                    lefts[(strip & 1) ^ m, kx * panel : (kx + 1) * panel, lane] = moved[2 - kx]

    def step(ky, carry):
        product = None
        for m in range(2):
            right = jnp.concatenate(
                [spread[k, 4 * pair + 2 * m + ky + row] for k in range(4) for row in range(2)], axis=1
            )
            part = dot_nt(lefts[m], right)
            product = part if product is None else product + part
        emit(pl.ds(3 * ky, 3), product.reshape(3, panel, channels))
        return carry

    lax.fori_loop(0, 3, step, 0)


def spread_kernel(place, *refs):
    threes, ones, spread = refs[:4], refs[4:8], refs[8]
    strip = place[0]
    channels = spread.shape[2]
    for k in range(4):
        spread[k, 0] = jnp.zeros((channels, LANES), BF16)
        spread[k, 9] = jnp.zeros((channels, LANES), BF16)
        for m, source in ((0, threes[k].at[0]), (1, threes[k].at[1]), (3, threes[k].at[2]), (2, ones[k])):
            for row in range(2):
                spread[k, 1 + 2 * ((strip + m) & 3) + row] = source[row]


def near_weight_kernel(place, own, plus, minus, spread, out, lefts):
    strip = place[0]

    def emit(taps, product):
        out[taps] = product

    weight_pair(strip, strip // 2, own, plus, minus, (strip & 1) == 0, spread, lefts, emit)


def far_weight_kernel(cells, place, plus, minus, far, spread, near, out, lefts):
    strip = place[0]

    def emit(taps, product):
        out[taps] = (near[taps] + product) / cells

    weight_pair(strip, 1 - strip // 2, far, minus, plus, (strip & 1) == 0, spread, lefts, emit)


VM = pl.BlockSpec(memory_space=pltpu.VMEM)
SM = pl.BlockSpec(memory_space=pltpu.SMEM)


def call(kernel, outs, specs, args, scratch=(), mib=8, us=3):
    return pl.pallas_call(
        kernel,
        out_shape=outs,
        in_specs=specs,
        out_specs=jax.tree.map(lambda _: VM, outs),
        scratch_shapes=scratch,
        compiler_params=pltpu.CompilerParams(vmem_limit_bytes=mib << 20),
        cost_estimate=pl.CostEstimate(
            flops=int(us * 1e9), bytes_accessed=int(us * 3e6), transcendentals=0
        ),
    )(*args)


def shape(dims, dtype):
    return jax.ShapeDtypeStruct(dims, dtype)


def swap(x, axis, mask):
    size = lax.axis_size(axis)
    return lax.ppermute(x, axis, [(i, i ^ mask) for i in range(size)])


def ring(x, axis, step):
    size = lax.axis_size(axis)
    return lax.ppermute(x, axis, [((i + step) % size, i) for i in range(size)])


def after_all(x, *others):
    return lax.optimization_barrier((x, *others))[0]


def strips_of_four(latents, teacher, norm_gain, norm_shift, conv_weight, conv_bias):
    row_devices = lax.axis_size("rows")
    panel_devices = lax.axis_size("wt")
    _, channels, strip_rows, width = latents.shape
    panel = conv_weight.shape[0]
    strip_cells = strip_rows * width
    total_cells = panel_devices * row_devices * strip_cells
    group_cells = channels // GROUPS * strip_cells * row_devices
    up = [(i, i + 1) for i in range(row_devices - 1)]
    down = [(i + 1, i) for i in range(row_devices - 1)]
    lat = latents.reshape(channels * strip_rows, width)
    tea = teacher.reshape(channels * strip_rows, width)
    given = jnp.stack([norm_gain, norm_shift, conv_bias])
    part = lax.axis_index("grp").astype(jnp.int32)
    here = lax.axis_index("wt").astype(jnp.int32)
    strip = lax.axis_index("rows").astype(jnp.int32)
    place = jnp.stack([strip, here, part])

    near = jnp.transpose(conv_weight, (1, 0, 2))
    far0 = swap(lax.dynamic_slice_in_dim(near, part * 2, 2, axis=0), "wt", 2)

    stats = call(stats_kernel, shape((8, channels), F32), [VM], (lat,))
    hidden, table = call(
        functools.partial(hidden_kernel, group_cells),
        (shape((strip_rows, channels, width), BF16), shape((channels, LANES), F32)),
        [VM] * 6,
        (lat, after_all(stats, far0), *(swap(stats, "rows", m) for m in (1, 2, 3)), given),
    )
    above, below = ring(hidden, "rows", 1), ring(hidden, "rows", 3)
    side = swap(after_all(near, hidden), "wt", 1)
    far2 = swap(after_all(near, hidden)[4:9], "wt", 2)
    far1 = swap(after_all(far0, hidden), "grp", 1)
    base = call(
        base_kernel, shape((strip_rows, channels, width), F32), [VM] * 3, (lat, tea, table), us=5
    )
    framed, packed = call(
        frame_kernel,
        (shape((3, 4, channels, width), BF16), shape((3, strip_rows, channels, width), BF16)),
        [SM] + [VM] * 3,
        (place, after_all(hidden, base), above, below),
        us=5,
    )
    beyond = ring(above, "rows", 1)
    threes = [packed, None, swap(packed, "wt", 2), None]
    part0, block0, block1 = call(
        near_conv_kernel,
        (
            shape((2, strip_rows, panel, width), F32),
            shape((strip_rows, panel, width), BF16),
            shape((strip_rows, panel, width), BF16),
        ),
        [SM] + [VM] * 4,
        (place, near, side, framed, base),
        [pltpu.VMEM((2 * panel, 2 * LANES), F32)],
        us=20,
    )
    far0, far1, far2, _ = lax.optimization_barrier((far0, far1, far2, framed))
    diag0, diag1, diag2 = swap(far0, "wt", 1), swap(far1, "wt", 1), swap(far2, "wt", 1)
    weights = (near, side, far0, far1, far2, diag0, diag1, diag2)
    res, low, block23 = call(
        far_conv_kernel,
        (
            shape((strip_rows, channels, width), F32),
            shape((strip_rows, channels, width), BF16),
            shape((2, strip_rows, panel, width), BF16),
        ),
        [SM] + [VM] * 9,
        (place, *weights[2:], framed, base, part0),
        [pltpu.VMEM((2 * panel, 2 * LANES), F32)],
        us=0.05,
    )

    low_before = lax.ppermute(low[1:2], "rows", up)
    low_after = lax.ppermute(low[0:1], "rows", down)
    block1 = swap(block1, "wt", 1)
    block23 = swap(block23, "wt", 2)
    full = call(
        assemble_kernel,
        shape((9, channels, channels), BF16),
        [SM] + [VM] * 8,
        (after_all(place, low), *weights),
        us=5,
    )
    stacked = jnp.stack([block0, block1, block23[0], swap(block23[1], "wt", 1)])
    plus, minus = ring(stacked, "rows", 1), ring(stacked, "rows", 3)
    far = ring(plus, "rows", 1)

    ones = [beyond, None, swap(beyond, "wt", 2), None]
    for k in (0, 2):
        threes[k + 1], ones[k + 1] = swap(threes[k], "wt", 1), swap(ones[k], "wt", 1)

    grad, sums = call(
        back_kernel,
        (shape((strip_rows, channels, width), F32), shape((8, channels), F32)),
        [VM] * 7,
        (full, low_before, low, low_after, res, lat, table),
        [
            pltpu.VMEM((3, 4, LANES, channels), BF16),
            pltpu.VMEM((2 * LANES, channels), F32),
        ],
        mib=12, us=30,
    )
    sums = after_all(sums, plus, minus)
    one, two, three = (swap(sums, "rows", m) for m in (1, 2, 3))
    sums = (sums + one) + (two + three)
    grad_latents = call(
        functools.partial(latents_kernel, group_cells),
        shape((channels * strip_rows, width), F32),
        [VM] * 6,
        (sums, given, res, grad, lat, table),
        us=0.05,
    )
    spread = call(
        spread_kernel,
        shape((4, 10, channels, width), BF16),
        [SM] + [VM] * 8,
        (place, *threes, *ones),
        us=5,
    )
    near_weight = call(
        near_weight_kernel,
        shape((9, panel, channels), F32),
        [SM] + [VM] * 4,
        (after_all(place, grad_latents), stacked, plus, minus, spread),
        [pltpu.VMEM((2, 3 * panel, 8 * LANES), BF16)],
        mib=12, us=30,
    )
    one, two, three = (swap(sums, "wt", m) for m in (1, 2, 3))
    sums = (sums + one) + (two + three)
    mean_loss = (jnp.sum(sums[3]) / (total_cells * channels)).reshape(1)
    param_grads = jnp.stack([sums[2], sums[1], sums[0]]) / total_cells

    grad_weight = call(
        functools.partial(far_weight_kernel, total_cells),
        shape((9, panel, channels), F32),
        [SM] + [VM] * 5,
        (place, plus, minus, far, spread, near_weight),
        [pltpu.VMEM((2, 3 * panel, 8 * LANES), BF16)],
        mib=14, us=0.05,
    )
    return (
        mean_loss,
        grad_latents.reshape(latents.shape),
        jnp.transpose(grad_weight, (1, 0, 2)),
        param_grads,
    )


def solution(mesh):
    placed = (
        P(("grp", "wt"), None, "rows", None),
        P(("grp", "wt"), None, "rows", None),
        P(),
        P(),
        P("wt", None, None),
        P(),
    )
    small = mesh.shape["rows"] == 4 and mesh.shape["wt"] == 4 and mesh.shape["grp"] == 2
    return jax.shard_map(
        strips_of_four if small else generic,
        mesh=mesh,
        in_specs=placed,
        out_specs=(
            P("grp"),
            P(("grp", "wt"), None, "rows", None),
            P(("grp", "wt"), None, None),
            P("grp", None),
        ),
        check_vma=False,
    )
```

```python
import functools

import jax
import jax.numpy as jnp
from jax import lax
from jax.experimental import pallas as pl
from jax.experimental.pallas import tpu as pltpu
from jax.sharding import PartitionSpec as P

GROUPS = 32
LANES = 128
epsilon = 1e-05
F32 = jnp.float32
BF16 = jnp.bfloat16


def with_halo(shard, sides, width):
    for axis, dim in sides:
        devices, length = (lax.axis_size(axis), shard.shape[dim])
        up = [(i, (i + 1) % devices) for i in range(devices - 1)]
        down = [(j, i) for i, j in up]
        last = lax.slice_in_dim(shard, length - width, length, axis=dim)
        leading = lax.slice_in_dim(shard, 0, width, axis=dim)
        before = lax.ppermute(last, axis, up)
        after = lax.ppermute(leading, axis, down)
        shard = jnp.concatenate([before, shard, after], axis=dim)
    return shard


def conv_taps(weights, padded, strip_rows, column_count):
    running = None
    for tap_index in range(9):
        tap_row, tap_col = (tap_index // 3, tap_index % 3)
        window = padded[:, :, tap_row : tap_row + strip_rows, tap_col : tap_col + column_count]
        window = window.reshape(padded.shape[0], padded.shape[1], strip_rows * column_count)
        product = jnp.einsum(
            "oi,nip->nop", weights[:, tap_index, :], window, preferred_element_type=jnp.float32
        )
        running = product if running is None else running + product
    return running


def transpose_taps(weights, padded, strip_rows, column_count):
    running = None
    for tap_index in range(9):
        tap_row, tap_col = (tap_index // 3, tap_index % 3)
        window = padded[
            :, :, 2 - tap_row : 2 - tap_row + strip_rows, 2 - tap_col : 2 - tap_col + column_count
        ]
        window = window.reshape(padded.shape[0], padded.shape[1], strip_rows * column_count)
        product = jnp.einsum(
            "oi,nop->nip", weights[:, tap_index, :], window, preferred_element_type=jnp.float32
        )
        running = product if running is None else running + product
    return running


def weight_terms(residual, padded, strip_rows, column_count):
    columns = []
    for tap_index in range(9):
        tap_row, tap_col = (tap_index // 3, tap_index % 3)
        window = padded[:, :, tap_row : tap_row + strip_rows, tap_col : tap_col + column_count]
        window = window.reshape(padded.shape[0], padded.shape[1], strip_rows * column_count)
        columns.append(
            jnp.einsum("nop,nip->oi", residual, window, preferred_element_type=jnp.float32)
        )
    return jnp.stack(columns, axis=1)


def generic(latents, teacher, norm_gain, norm_shift, conv_weight, conv_bias):
    row_devices = lax.axis_size("rows")
    panel_devices = lax.axis_size("wt")
    images, channels, strip_rows, column_count = latents.shape
    cell_count = strip_rows * column_count
    total_cells = panel_devices * row_devices * cell_count
    group_cells = channels // GROUPS * cell_count * row_devices
    grouped = latents.reshape(images, GROUPS, channels // GROUPS, cell_count)
    group_sum, square_sum = lax.psum(
        (
            jnp.sum(grouped, axis=(2, 3), keepdims=True),
            jnp.sum(jnp.square(grouped), axis=(2, 3), keepdims=True),
        ),
        "rows",
    )
    group_mean = group_sum / group_cells
    centered = grouped - group_mean
    group_var = square_sum / group_cells - jnp.square(group_mean)
    inverse = lax.rsqrt(group_var + epsilon)
    normed = (centered * inverse).reshape(images, channels, cell_count)
    gain_column = norm_gain[None, :, None]
    pre_norm = normed * gain_column + norm_shift[None, :, None]
    sigmoid_pre = jax.nn.sigmoid(pre_norm)
    hidden = (pre_norm * sigmoid_pre).astype(jnp.bfloat16)
    column_pad = ((0, 0), (0, 0), (0, 0), (1, 1))
    framed_hidden = with_halo(
        hidden.reshape(images, channels, strip_rows, column_count), (("rows", 2),), 1
    )
    padded = jnp.pad(framed_hidden, column_pad)
    all_images = lax.all_gather(framed_hidden, "wt", axis=0, tiled=True)
    all_padded = jnp.pad(all_images, column_pad)
    conv_out = conv_taps(
        lax.all_gather(conv_weight, "wt", axis=0, tiled=True), padded, strip_rows, column_count
    )
    residual = (
        latents.reshape(images, channels, cell_count)
        + conv_out
        + conv_bias[None, :, None]
        - teacher.reshape(images, channels, cell_count)
    )
    low_residual = residual.astype(jnp.bfloat16)
    framed_residual = with_halo(
        low_residual.reshape(images, channels, strip_rows, column_count), (("rows", 2),), 1
    )
    padded_residual = jnp.pad(framed_residual, column_pad)
    panel_residual = lax.all_to_all(framed_residual, "wt", split_axis=1, concat_axis=0, tiled=True)
    panel_rows = channels // panel_devices
    panel_inner = panel_residual[:, :, 1 : strip_rows + 1, :].reshape(
        panel_residual.shape[0], panel_rows, cell_count
    )
    window = padded_residual
    grad_hidden = transpose_taps(
        lax.all_gather(conv_weight, "wt", axis=0, tiled=True), window, strip_rows, column_count
    )
    window = panel_inner
    weight_share = lax.psum_scatter(
        weight_terms(window, all_padded, strip_rows, column_count),
        "rows",
        scatter_dimension=0,
        tiled=True,
    )
    grad_weight = lax.all_gather(weight_share, "rows", axis=0, tiled=True) / total_cells
    grad_pre = grad_hidden * sigmoid_pre * (1.0 + pre_norm * (1.0 - sigmoid_pre))
    grad_norm = (grad_pre * gain_column).reshape(grouped.shape)
    normed_groups = normed.reshape(grouped.shape)
    first_sum, second_sum = lax.psum(
        (
            jnp.sum(grad_norm, axis=(2, 3), keepdims=True),
            jnp.sum(grad_norm * normed_groups, axis=(2, 3), keepdims=True),
        ),
        "rows",
    )
    first_mean = first_sum / group_cells
    second_mean = second_sum / group_cells
    grad_latents = residual.reshape(latents.shape) + (
        inverse * (grad_norm - first_mean - normed_groups * second_mean)
    ).reshape(latents.shape)
    totals = lax.psum(
        (
            jnp.sum(jnp.square(residual)),
            jnp.sum(residual, axis=(0, 2)),
            jnp.sum(grad_pre * normed, axis=(0, 2)),
            jnp.sum(grad_pre, axis=(0, 2)),
        ),
        ("rows", "wt"),
    )
    mean_loss = (totals[0] / (total_cells * channels)).reshape(1)
    param_grads = jnp.stack([totals[1], totals[2], totals[3]]) / total_cells
    return (mean_loss, grad_latents, grad_weight, param_grads)


def plane(ref, row, channels):
    return ref[pl.ds(row, channels, stride=2), :]


def split3(x):
    a = x.astype(BF16)
    rest = x - a.astype(F32)
    b = rest.astype(BF16)
    c = (rest - b.astype(F32)).astype(BF16)
    return a, b, c


def membership(channels):
    size = channels // GROUPS
    channel = lax.broadcasted_iota(jnp.int32, (channels, LANES), 0)
    first = lax.broadcasted_iota(jnp.int32, (channels, LANES), 1) * size
    inside = (channel >= first) & (channel < first + size)
    return jnp.where(inside, 1.0, 0.0).astype(BF16)


def dot_nn(a, b):
    return lax.dot_general(a, b, (((1,), (0,)), ((), ())), preferred_element_type=F32)


def dot_nt(a, b):
    return lax.dot_general(a, b, (((1,), (1,)), ((), ())), preferred_element_type=F32)


def group_sums(rows, member):
    a, b, c = split3(rows)
    return dot_nn(a, member) + (dot_nn(b, member) + dot_nn(c, member))


def to_channels(rows, member):
    a, b, c = split3(rows)
    return dot_nt(a, member) + (dot_nt(b, member) + dot_nt(c, member))


def as_rows(columns, channels):
    lane = lax.broadcasted_iota(jnp.int32, (channels, LANES), 1)
    table = jnp.zeros((channels, LANES), F32)
    for i, column in enumerate(columns):
        table = jnp.where(lane == i, column, table)
    return jnp.transpose(table)[:8, :]


def as_columns(rows, channels):
    pad = jnp.zeros((LANES - len(rows), channels), F32)
    return jnp.transpose(jnp.concatenate(rows + [pad], axis=0))


def row_sum(a, b):
    return jnp.sum(a + b, axis=1, keepdims=True)


def stats_kernel(lat, out):
    channels = out.shape[1]
    a, b = plane(lat, 0, channels), plane(lat, 1, channels)
    out[...] = as_rows([row_sum(a, b), row_sum(a * a, b * b)], channels)


def hidden_kernel(cells, lat, s0, s1, s2, s3, given, hidden, table):
    channels = s0.shape[1]
    member = membership(channels)
    sums = group_sums((s0[...] + s1[...]) + (s2[...] + s3[...]), member)
    mean = sums[0:1] / cells
    var = sums[1:2] / cells - mean * mean
    inverse = lax.rsqrt(var + epsilon)
    pad = jnp.zeros((6, LANES), F32)
    rows = to_channels(jnp.concatenate([mean, inverse, pad], axis=0), member)
    columns = as_columns([rows[0:1], rows[1:2], given[0:1], given[1:2], given[2:3]], channels)
    table[...] = columns
    for row in range(2):
        normed = (plane(lat, row, channels) - columns[:, 0:1]) * columns[:, 1:2]
        pre = normed * columns[:, 2:3] + columns[:, 3:4]
        hidden[row] = (pre * jax.nn.sigmoid(pre)).astype(BF16)


def shifts(x):
    wide = x.astype(F32)
    lane = lax.broadcasted_iota(jnp.int32, x.shape, 1)
    left = jnp.where(lane == 0, 0.0, pltpu.roll(wide, 1, 1)).astype(BF16)
    right = jnp.where(lane == LANES - 1, 0.0, pltpu.roll(wide, LANES - 1, 1)).astype(BF16)
    return left, x, right


def base_kernel(lat, tea, table, base):
    channels = table.shape[0]
    for row in range(2):
        base[row] = plane(lat, row, channels) + table[:, 4:5] - plane(tea, row, channels)


def frame_kernel(place, mine, above, below, framed):
    strip = place[0]
    edge = jnp.zeros_like(mine[0])
    before = jnp.where(strip > 0, below[1], edge)
    after = jnp.where(strip < 3, above[0], edge)
    for row, source in enumerate((before, mine[0], mine[1], after)):
        for kx, moved in enumerate(shifts(source)):
            framed[kx, row] = moved


def panel_rows(me, k, panel):
    return pl.ds(pl.multiple_of((me ^ k) * panel, panel), panel)


def conv_step(total, framed, ky, kx, first, second):
    window = jnp.concatenate([framed[kx, ky], framed[kx, ky + 1]], axis=1)
    total[...] += dot_nn(jnp.concatenate([first, second], axis=0), window)


def near_conv_kernel(place, near, side, framed, base, part, block0, block1, total):
    me = place[1]
    panel = near.shape[1]
    total[...] = jnp.zeros_like(total)

    def step(tap, carry):
        ky = tap // 3
        conv_step(total, framed, ky, tap - 3 * ky, near[tap], side[tap])
        return carry

    lax.fori_loop(0, 9, step, 0)
    for k, block in enumerate((block0, block1)):
        for row in range(2):
            value = base[row, panel_rows(me, k, panel), :] + (
                total[k * panel : (k + 1) * panel, row * LANES : (row + 1) * LANES]
            )
            part[k, row] = value
            block[row] = value.astype(BF16)


def far_conv_kernel(
    place, far0, far1, far2, diag0, diag1, diag2, framed, base, part, res, low, block23, total
):
    me, half = place[1], place[2]
    panel = far0.shape[1]
    total[...] = jnp.zeros_like(total)

    def run(first, far, diag):
        def step(i, carry):
            tap = first + i
            ky = tap // 3
            conv_step(total, framed, ky, tap - 3 * ky, far[i], diag[i])
            return carry

        lax.fori_loop(0, far.shape[0], step, 0)

    taps = far0.shape[0]
    run(taps * half, far0, diag0)
    run(taps - taps * half, far1, diag1)
    run(2 * taps, far2, diag2)
    for k in range(4):
        rows = panel_rows(me, k, panel)
        for row in range(2):
            if k < 2:
                value = part[k, row]
            else:
                value = base[row, rows, :] + (
                    total[(k - 2) * panel : (k - 1) * panel, row * LANES : (row + 1) * LANES]
                )
                block23[k - 2, row] = value.astype(BF16)
            res[row, rows, :] = value
            low[row, rows, :] = value.astype(BF16)


def assemble_kernel(place, near, side, far0, far1, far2, diag0, diag1, diag2, full):
    me, half = place[1], place[2]
    panel = near.shape[1]
    near_taps, side_taps = panel_rows(me, 0, panel), panel_rows(me, 1, panel)
    far_taps, diag_taps = panel_rows(me, 2, panel), panel_rows(me, 3, panel)

    def local(tap, carry):
        full[tap, near_taps, :] = near[tap]
        full[tap, side_taps, :] = side[tap]
        return carry

    lax.fori_loop(0, 9, local, 0)
    taps = far0.shape[0]
    parts = ((taps * half, far0, diag0), (taps - taps * half, far1, diag1), (2 * taps, far2, diag2))
    for first, far, diag in parts:
        def remote(i, carry, first=first, far=far, diag=diag):
            full[first + i, far_taps, :] = far[i]
            full[first + i, diag_taps, :] = diag[i]
            return carry

        lax.fori_loop(0, far.shape[0], remote, 0)


def back_kernel(full, before, low, after, res, lat, table, grad, sums, framed, total):
    channels = low.shape[1]
    for row, source in enumerate((before[0], low[0], low[1], after[0])):
        for kx, moved in enumerate(shifts(source)):
            framed[kx, row] = jnp.transpose(moved)
    total[...] = jnp.zeros_like(total)

    def tap_step(tap, carry):
        ky = tap // 3
        kx = tap - 3 * ky
        window = jnp.concatenate([framed[2 - kx, 2 - ky], framed[2 - kx, 3 - ky]], axis=0)
        total[...] += dot_nn(window, full[tap])
        return carry

    lax.fori_loop(0, 9, tap_step, 0)
    columns = table[...]
    first = second = bottom = loss = None
    for row in range(2):
        normed = (plane(lat, row, channels) - columns[:, 0:1]) * columns[:, 1:2]
        pre = normed * columns[:, 2:3] + columns[:, 3:4]
        s = jax.nn.sigmoid(pre)
        value = jnp.transpose(total[row * LANES : (row + 1) * LANES, :]) * s * (1.0 + pre * (1.0 - s))
        grad[row] = value
        r = res[row]
        terms = (value, value * normed, r, r * r)
        if row == 0:
            first, second, bottom, loss = terms
        else:
            first, second, bottom, loss = (
                first + terms[0], second + terms[1], bottom + terms[2], loss + terms[3],
            )
    add = functools.partial(jnp.sum, axis=1, keepdims=True)
    sums[...] = as_rows([add(first), add(second), add(bottom), add(loss)], channels)


def latents_kernel(cells, total, given, res, grad, lat, table, out):
    channels = total.shape[1]
    member = membership(channels)
    rows = total[...] * given[0:1]
    means = group_sums(rows, member) / cells
    rows = to_channels(means, member)
    columns = as_columns([rows[0:1], rows[1:2]], channels)
    constants = table[...]
    inverse = constants[:, 1:2]
    for row in range(2):
        normed = (plane(lat, row, channels) - constants[:, 0:1]) * inverse
        change = grad[row] * constants[:, 2:3] - columns[:, 0:1] - normed * columns[:, 1:2]
        out[pl.ds(row, channels, stride=2), :] = res[row] + inverse * change


def weight_pair(strip, pair, aligned, one, two, first, spread, lefts, emit):
    panel, channels = aligned.shape[2], spread[0].shape[1]
    for m in range(2):
        for k in range(4):
            for row in range(2):
                lane = pl.ds((2 * k + row) * LANES, LANES)
                source = aligned[k, row] if m == 0 else jnp.where(first, one[k, row], two[k, row])
                moved = shifts(source)
                for kx in range(3):
                    lefts[(strip & 1) ^ m, kx * panel : (kx + 1) * panel, lane] = moved[2 - kx]

    def step(ky, carry):
        product = None
        for m in range(2):
            right = jnp.concatenate(
                [spread[k][4 * pair + 2 * m + ky + row] for k in range(4) for row in range(2)], axis=1
            )
            part = dot_nt(lefts[m], right)
            product = part if product is None else product + part
        emit(pl.ds(3 * ky, 3), product.reshape(3, panel, channels))
        return carry

    lax.fori_loop(0, 3, step, 0)


def spread_kernel(place, mine, above, beyond, below, spread):
    strip = place[0]
    channels = spread.shape[1]
    spread[0] = jnp.zeros((channels, LANES), BF16)
    spread[9] = jnp.zeros((channels, LANES), BF16)
    for m, source in enumerate((mine, above, beyond, below)):
        for row in range(2):
            spread[1 + 2 * ((strip + m) & 3) + row] = source[row]


def near_weight_kernel(place, own, plus, minus, h0, h1, h2, h3, out, lefts):
    strip = place[0]

    def emit(taps, product):
        out[taps] = product

    weight_pair(strip, strip // 2, own, plus, minus, (strip & 1) == 0, (h0, h1, h2, h3), lefts, emit)


def far_weight_kernel(cells, place, plus, minus, far, h0, h1, h2, h3, near, out, lefts):
    strip = place[0]

    def emit(taps, product):
        out[taps] = (near[taps] + product) / cells

    weight_pair(strip, 1 - strip // 2, far, minus, plus, (strip & 1) == 0, (h0, h1, h2, h3), lefts, emit)


VM = pl.BlockSpec(memory_space=pltpu.VMEM)
SM = pl.BlockSpec(memory_space=pltpu.SMEM)


def call(kernel, outs, specs, args, scratch=(), mib=8, us=3):
    return pl.pallas_call(
        kernel,
        out_shape=outs,
        in_specs=specs,
        out_specs=jax.tree.map(lambda _: VM, outs),
        scratch_shapes=scratch,
        compiler_params=pltpu.CompilerParams(vmem_limit_bytes=mib << 20),
        cost_estimate=pl.CostEstimate(
            flops=int(us * 1e9), bytes_accessed=int(us * 3e6), transcendentals=0
        ),
    )(*args)


def shape(dims, dtype):
    return jax.ShapeDtypeStruct(dims, dtype)


def swap(x, axis, mask):
    size = lax.axis_size(axis)
    return lax.ppermute(x, axis, [(i, i ^ mask) for i in range(size)])


def ring(x, axis, step):
    size = lax.axis_size(axis)
    return lax.ppermute(x, axis, [((i + step) % size, i) for i in range(size)])


def after_all(x, *others):
    return lax.optimization_barrier((x, *others))[0]


def strips_of_four(latents, teacher, norm_gain, norm_shift, conv_weight, conv_bias):
    row_devices = lax.axis_size("rows")
    panel_devices = lax.axis_size("wt")
    _, channels, strip_rows, width = latents.shape
    panel = conv_weight.shape[0]
    strip_cells = strip_rows * width
    total_cells = panel_devices * row_devices * strip_cells
    group_cells = channels // GROUPS * strip_cells * row_devices
    up = [(i, i + 1) for i in range(row_devices - 1)]
    down = [(i + 1, i) for i in range(row_devices - 1)]
    lat = latents.reshape(channels * strip_rows, width)
    tea = teacher.reshape(channels * strip_rows, width)
    given = jnp.stack([norm_gain, norm_shift, conv_bias])
    part = lax.axis_index("grp").astype(jnp.int32)
    here = lax.axis_index("wt").astype(jnp.int32)
    strip = lax.axis_index("rows").astype(jnp.int32)
    place = jnp.stack([strip, here, part])

    near = jnp.transpose(conv_weight, (1, 0, 2))
    far0 = swap(lax.dynamic_slice_in_dim(near, part * 3, 3, axis=0), "wt", 2)

    stats = call(stats_kernel, shape((8, channels), F32), [VM], (lat,))
    hidden, table = call(
        functools.partial(hidden_kernel, group_cells),
        (shape((strip_rows, channels, width), BF16), shape((channels, LANES), F32)),
        [VM] * 6,
        (lat, after_all(stats, far0), *(swap(stats, "rows", m) for m in (1, 2, 3)), given),
        us=0.05,
    )
    above, below = ring(hidden, "rows", 1), ring(hidden, "rows", 3)
    side = swap(after_all(near, hidden), "wt", 1)
    far2 = swap(after_all(near, hidden)[6:9], "wt", 2)
    far1 = swap(after_all(far0, hidden), "grp", 1)
    base = call(
        base_kernel, shape((strip_rows, channels, width), F32), [VM] * 3, (lat, tea, table), us=5
    )
    framed = call(
        frame_kernel,
        shape((3, 4, channels, width), BF16),
        [SM] + [VM] * 3,
        (place, after_all(hidden, base), above, below),
        us=5,
    )
    beyond = ring(above, "rows", 1)
    across = [swap(after_all(hidden, framed), "wt", 2), swap(after_all(above, framed), "wt", 2)]
    rows_of = functools.partial(
        call, spread_kernel, shape((10, channels, width), BF16), [SM] + [VM] * 4, us=3
    )
    part0, block0, block1 = call(
        near_conv_kernel,
        (
            shape((2, strip_rows, panel, width), F32),
            shape((strip_rows, panel, width), BF16),
            shape((strip_rows, panel, width), BF16),
        ),
        [SM] + [VM] * 4,
        (place, near, side, framed, base),
        [pltpu.VMEM((2 * panel, 2 * LANES), F32)],
        us=20,
    )
    far0, far1, far2, _ = lax.optimization_barrier((far0, far1, far2, framed))
    diag0, diag1, diag2 = swap(far0, "wt", 1), swap(far1, "wt", 1), swap(far2, "wt", 1)
    weights = (near, side, far0, far1, far2, diag0, diag1, diag2)
    res, low, block23 = call(
        far_conv_kernel,
        (
            shape((strip_rows, channels, width), F32),
            shape((strip_rows, channels, width), BF16),
            shape((2, strip_rows, panel, width), BF16),
        ),
        [SM] + [VM] * 9,
        (place, *weights[2:], framed, base, after_all(part0, across[0])),
        [pltpu.VMEM((2 * panel, 2 * LANES), F32)],
        us=0.05,
    )

    low_before = lax.ppermute(low[1:2], "rows", up)
    low_after = lax.ppermute(low[0:1], "rows", down)
    block1 = swap(block1, "wt", 1)
    block23 = swap(block23, "wt", 2)
    full = call(
        assemble_kernel,
        shape((9, channels, channels), BF16),
        [SM] + [VM] * 8,
        (after_all(place, low), *weights),
        us=5,
    )
    stacked = after_all(jnp.stack([block0, block1, block23[0], swap(block23[1], "wt", 1)]), across[1])
    plus, minus = ring(stacked, "rows", 1), ring(stacked, "rows", 3)
    far = ring(plus, "rows", 1)

    across += [swap(after_all(beyond, stacked), "wt", 2), swap(after_all(below, block23), "wt", 2)]
    own_rows = rows_of((place, after_all(hidden, stacked), above, beyond, below))
    other_rows = swap(own_rows, "wt", 1)

    grad, sums = call(
        back_kernel,
        (shape((strip_rows, channels, width), F32), shape((8, channels), F32)),
        [VM] * 7,
        (full, low_before, after_all(low, across[3]), low_after, res, lat, table),
        [
            pltpu.VMEM((3, 4, LANES, channels), BF16),
            pltpu.VMEM((2 * LANES, channels), F32),
        ],
        mib=12, us=30,
    )
    sums = after_all(sums, plus, minus, across[2])
    across_rows = rows_of((after_all(place, sums), *across))
    diag_rows = swap(across_rows, "wt", 1)
    one, two, three = (swap(sums, "rows", m) for m in (1, 2, 3))
    sums = (sums + one) + (two + three)
    grad_latents = call(
        functools.partial(latents_kernel, group_cells),
        shape((channels * strip_rows, width), F32),
        [VM] * 6,
        (sums, given, res, grad, lat, table),
        us=0.05,
    )
    images = (own_rows, other_rows, across_rows, diag_rows)
    near_weight = call(
        near_weight_kernel,
        shape((9, panel, channels), F32),
        [SM] + [VM] * 7,
        (after_all(place, grad_latents), stacked, plus, minus, *images),
        [pltpu.VMEM((2, 3 * panel, 8 * LANES), BF16)],
        mib=14, us=30,
    )
    one, two, three = (swap(sums, "wt", m) for m in (1, 2, 3))
    sums = (sums + one) + (two + three)
    mean_loss = (jnp.sum(sums[3]) / (total_cells * channels)).reshape(1)
    param_grads = jnp.stack([sums[2], sums[1], sums[0]]) / total_cells

    grad_weight = call(
        functools.partial(far_weight_kernel, total_cells),
        shape((9, panel, channels), F32),
        [SM] + [VM] * 8,
        (place, plus, minus, far, *images, near_weight),
        [pltpu.VMEM((2, 3 * panel, 8 * LANES), BF16)],
        mib=16, us=0.05,
    )
    return (
        mean_loss,
        grad_latents.reshape(latents.shape),
        jnp.transpose(grad_weight, (1, 0, 2)),
        param_grads,
    )


def solution(mesh):
    placed = (
        P(("grp", "wt"), None, "rows", None),
        P(("grp", "wt"), None, "rows", None),
        P(),
        P(),
        P("wt", None, None),
        P(),
    )
    small = mesh.shape["rows"] == 4 and mesh.shape["wt"] == 4 and mesh.shape["grp"] == 2
    return jax.shard_map(
        strips_of_four if small else generic,
        mesh=mesh,
        in_specs=placed,
        out_specs=(
            P("grp"),
            P(("grp", "wt"), None, "rows", None),
            P(("grp", "wt"), None, None),
            P("grp", None),
        ),
        check_vma=False,
    )
```

```python
import functools

import jax
import jax.numpy as jnp
from jax import lax
from jax.experimental import pallas as pl
from jax.experimental.pallas import tpu as pltpu
from jax.sharding import PartitionSpec as P

GROUPS = 32
LANES = 128
epsilon = 1e-05
F32 = jnp.float32
BF16 = jnp.bfloat16


def with_halo(shard, sides, width):
    for axis, dim in sides:
        devices, length = (lax.axis_size(axis), shard.shape[dim])
        up = [(i, (i + 1) % devices) for i in range(devices - 1)]
        down = [(j, i) for i, j in up]
        last = lax.slice_in_dim(shard, length - width, length, axis=dim)
        leading = lax.slice_in_dim(shard, 0, width, axis=dim)
        before = lax.ppermute(last, axis, up)
        after = lax.ppermute(leading, axis, down)
        shard = jnp.concatenate([before, shard, after], axis=dim)
    return shard


def conv_taps(weights, padded, strip_rows, column_count):
    running = None
    for tap_index in range(9):
        tap_row, tap_col = (tap_index // 3, tap_index % 3)
        window = padded[:, :, tap_row : tap_row + strip_rows, tap_col : tap_col + column_count]
        window = window.reshape(padded.shape[0], padded.shape[1], strip_rows * column_count)
        product = jnp.einsum(
            "oi,nip->nop", weights[:, tap_index, :], window, preferred_element_type=jnp.float32
        )
        running = product if running is None else running + product
    return running


def transpose_taps(weights, padded, strip_rows, column_count):
    running = None
    for tap_index in range(9):
        tap_row, tap_col = (tap_index // 3, tap_index % 3)
        window = padded[
            :, :, 2 - tap_row : 2 - tap_row + strip_rows, 2 - tap_col : 2 - tap_col + column_count
        ]
        window = window.reshape(padded.shape[0], padded.shape[1], strip_rows * column_count)
        product = jnp.einsum(
            "oi,nop->nip", weights[:, tap_index, :], window, preferred_element_type=jnp.float32
        )
        running = product if running is None else running + product
    return running


def weight_terms(residual, padded, strip_rows, column_count):
    columns = []
    for tap_index in range(9):
        tap_row, tap_col = (tap_index // 3, tap_index % 3)
        window = padded[:, :, tap_row : tap_row + strip_rows, tap_col : tap_col + column_count]
        window = window.reshape(padded.shape[0], padded.shape[1], strip_rows * column_count)
        columns.append(
            jnp.einsum("nop,nip->oi", residual, window, preferred_element_type=jnp.float32)
        )
    return jnp.stack(columns, axis=1)


def generic(latents, teacher, norm_gain, norm_shift, conv_weight, conv_bias):
    row_devices = lax.axis_size("rows")
    panel_devices = lax.axis_size("wt")
    images, channels, strip_rows, column_count = latents.shape
    cell_count = strip_rows * column_count
    total_cells = panel_devices * row_devices * cell_count
    group_cells = channels // GROUPS * cell_count * row_devices
    grouped = latents.reshape(images, GROUPS, channels // GROUPS, cell_count)
    group_sum, square_sum = lax.psum(
        (
            jnp.sum(grouped, axis=(2, 3), keepdims=True),
            jnp.sum(jnp.square(grouped), axis=(2, 3), keepdims=True),
        ),
        "rows",
    )
    group_mean = group_sum / group_cells
    centered = grouped - group_mean
    group_var = square_sum / group_cells - jnp.square(group_mean)
    inverse = lax.rsqrt(group_var + epsilon)
    normed = (centered * inverse).reshape(images, channels, cell_count)
    gain_column = norm_gain[None, :, None]
    pre_norm = normed * gain_column + norm_shift[None, :, None]
    sigmoid_pre = jax.nn.sigmoid(pre_norm)
    hidden = (pre_norm * sigmoid_pre).astype(jnp.bfloat16)
    column_pad = ((0, 0), (0, 0), (0, 0), (1, 1))
    framed_hidden = with_halo(
        hidden.reshape(images, channels, strip_rows, column_count), (("rows", 2),), 1
    )
    padded = jnp.pad(framed_hidden, column_pad)
    all_images = lax.all_gather(framed_hidden, "wt", axis=0, tiled=True)
    all_padded = jnp.pad(all_images, column_pad)
    conv_out = conv_taps(
        lax.all_gather(conv_weight, "wt", axis=0, tiled=True), padded, strip_rows, column_count
    )
    residual = (
        latents.reshape(images, channels, cell_count)
        + conv_out
        + conv_bias[None, :, None]
        - teacher.reshape(images, channels, cell_count)
    )
    low_residual = residual.astype(jnp.bfloat16)
    framed_residual = with_halo(
        low_residual.reshape(images, channels, strip_rows, column_count), (("rows", 2),), 1
    )
    padded_residual = jnp.pad(framed_residual, column_pad)
    panel_residual = lax.all_to_all(framed_residual, "wt", split_axis=1, concat_axis=0, tiled=True)
    panel_rows = channels // panel_devices
    panel_inner = panel_residual[:, :, 1 : strip_rows + 1, :].reshape(
        panel_residual.shape[0], panel_rows, cell_count
    )
    window = padded_residual
    grad_hidden = transpose_taps(
        lax.all_gather(conv_weight, "wt", axis=0, tiled=True), window, strip_rows, column_count
    )
    window = panel_inner
    weight_share = lax.psum_scatter(
        weight_terms(window, all_padded, strip_rows, column_count),
        "rows",
        scatter_dimension=0,
        tiled=True,
    )
    grad_weight = lax.all_gather(weight_share, "rows", axis=0, tiled=True) / total_cells
    grad_pre = grad_hidden * sigmoid_pre * (1.0 + pre_norm * (1.0 - sigmoid_pre))
    grad_norm = (grad_pre * gain_column).reshape(grouped.shape)
    normed_groups = normed.reshape(grouped.shape)
    first_sum, second_sum = lax.psum(
        (
            jnp.sum(grad_norm, axis=(2, 3), keepdims=True),
            jnp.sum(grad_norm * normed_groups, axis=(2, 3), keepdims=True),
        ),
        "rows",
    )
    first_mean = first_sum / group_cells
    second_mean = second_sum / group_cells
    grad_latents = residual.reshape(latents.shape) + (
        inverse * (grad_norm - first_mean - normed_groups * second_mean)
    ).reshape(latents.shape)
    totals = lax.psum(
        (
            jnp.sum(jnp.square(residual)),
            jnp.sum(residual, axis=(0, 2)),
            jnp.sum(grad_pre * normed, axis=(0, 2)),
            jnp.sum(grad_pre, axis=(0, 2)),
        ),
        ("rows", "wt"),
    )
    mean_loss = (totals[0] / (total_cells * channels)).reshape(1)
    param_grads = jnp.stack([totals[1], totals[2], totals[3]]) / total_cells
    return (mean_loss, grad_latents, grad_weight, param_grads)


def plane(ref, row, channels):
    return ref[pl.ds(row, channels, stride=2), :]


def split3(x):
    a = x.astype(BF16)
    rest = x - a.astype(F32)
    b = rest.astype(BF16)
    c = (rest - b.astype(F32)).astype(BF16)
    return a, b, c


def membership(channels):
    size = channels // GROUPS
    channel = lax.broadcasted_iota(jnp.int32, (channels, LANES), 0)
    first = lax.broadcasted_iota(jnp.int32, (channels, LANES), 1) * size
    inside = (channel >= first) & (channel < first + size)
    return jnp.where(inside, 1.0, 0.0).astype(BF16)


def dot_nn(a, b):
    return lax.dot_general(a, b, (((1,), (0,)), ((), ())), preferred_element_type=F32)


def dot_nt(a, b):
    return lax.dot_general(a, b, (((1,), (1,)), ((), ())), preferred_element_type=F32)


def group_sums(rows, member):
    a, b, c = split3(rows)
    return dot_nn(a, member) + (dot_nn(b, member) + dot_nn(c, member))


def to_channels(rows, member):
    a, b, c = split3(rows)
    return dot_nt(a, member) + (dot_nt(b, member) + dot_nt(c, member))


def as_rows(columns, channels):
    lane = lax.broadcasted_iota(jnp.int32, (channels, LANES), 1)
    table = jnp.zeros((channels, LANES), F32)
    for i, column in enumerate(columns):
        table = jnp.where(lane == i, column, table)
    return jnp.transpose(table)[:8, :]


def as_columns(rows, channels):
    pad = jnp.zeros((LANES - len(rows), channels), F32)
    return jnp.transpose(jnp.concatenate(rows + [pad], axis=0))


def row_sum(a, b):
    return jnp.sum(a + b, axis=1, keepdims=True)


def stats_kernel(lat, out):
    channels = out.shape[1]
    a, b = plane(lat, 0, channels), plane(lat, 1, channels)
    out[...] = as_rows([row_sum(a, b), row_sum(a * a, b * b)], channels)


def hidden_kernel(cells, lat, s0, s1, s2, s3, given, hidden, table):
    channels = s0.shape[1]
    member = membership(channels)
    sums = group_sums((s0[...] + s1[...]) + (s2[...] + s3[...]), member)
    mean = sums[0:1] / cells
    var = sums[1:2] / cells - mean * mean
    inverse = lax.rsqrt(var + epsilon)
    pad = jnp.zeros((6, LANES), F32)
    rows = to_channels(jnp.concatenate([mean, inverse, pad], axis=0), member)
    columns = as_columns([rows[0:1], rows[1:2], given[0:1], given[1:2], given[2:3]], channels)
    table[...] = columns
    for row in range(2):
        normed = (plane(lat, row, channels) - columns[:, 0:1]) * columns[:, 1:2]
        pre = normed * columns[:, 2:3] + columns[:, 3:4]
        hidden[row] = (pre * jax.nn.sigmoid(pre)).astype(BF16)


def shifts(x):
    wide = x.astype(F32)
    lane = lax.broadcasted_iota(jnp.int32, x.shape, 1)
    left = jnp.where(lane == 0, 0.0, pltpu.roll(wide, 1, 1)).astype(BF16)
    right = jnp.where(lane == LANES - 1, 0.0, pltpu.roll(wide, LANES - 1, 1)).astype(BF16)
    return left, x, right


def base_kernel(lat, tea, table, base):
    channels = table.shape[0]
    for row in range(2):
        base[row] = plane(lat, row, channels) + table[:, 4:5] - plane(tea, row, channels)


def frame_kernel(place, mine, above, below, framed):
    strip = place[0]
    edge = jnp.zeros_like(mine[0])
    before = jnp.where(strip > 0, below[1], edge)
    after = jnp.where(strip < 3, above[0], edge)
    for row, source in enumerate((before, mine[0], mine[1], after)):
        for kx, moved in enumerate(shifts(source)):
            framed[kx, row] = moved


def panel_rows(me, k, panel):
    return pl.ds(pl.multiple_of((me ^ k) * panel, panel), panel)


def conv_step(total, framed, ky, kx, first, second):
    window = jnp.concatenate([framed[kx, ky], framed[kx, ky + 1]], axis=1)
    total[...] += dot_nn(jnp.concatenate([first, second], axis=0), window)


def near_conv_kernel(place, near, side, framed, base, part, block0, block1, total):
    me = place[1]
    panel = near.shape[1]
    total[...] = jnp.zeros_like(total)

    def step(tap, carry):
        ky = tap // 3
        conv_step(total, framed, ky, tap - 3 * ky, near[tap], side[tap])
        return carry

    lax.fori_loop(0, 9, step, 0)
    for k, block in enumerate((block0, block1)):
        for row in range(2):
            value = base[row, panel_rows(me, k, panel), :] + (
                total[k * panel : (k + 1) * panel, row * LANES : (row + 1) * LANES]
            )
            part[k, row] = value
            block[row] = value.astype(BF16)


def far_conv_kernel(
    place, far0, far1, far2, diag0, diag1, diag2, framed, base, part, res, low, block23, total
):
    me, half = place[1], place[2]
    panel = far0.shape[1]
    total[...] = jnp.zeros_like(total)

    def run(first, far, diag):
        def step(i, carry):
            tap = first + i
            ky = tap // 3
            conv_step(total, framed, ky, tap - 3 * ky, far[i], diag[i])
            return carry

        lax.fori_loop(0, far.shape[0], step, 0)

    taps = far0.shape[0]
    run(taps * half, far0, diag0)
    run(taps - taps * half, far1, diag1)
    run(2 * taps, far2, diag2)
    for k in range(4):
        rows = panel_rows(me, k, panel)
        for row in range(2):
            if k < 2:
                value = part[k, row]
            else:
                value = base[row, rows, :] + (
                    total[(k - 2) * panel : (k - 1) * panel, row * LANES : (row + 1) * LANES]
                )
                block23[k - 2, row] = value.astype(BF16)
            res[row, rows, :] = value
            low[row, rows, :] = value.astype(BF16)


def assemble_kernel(place, near, side, far0, far1, far2, diag0, diag1, diag2, full):
    me, half = place[1], place[2]
    panel = near.shape[1]
    near_taps, side_taps = panel_rows(me, 0, panel), panel_rows(me, 1, panel)
    far_taps, diag_taps = panel_rows(me, 2, panel), panel_rows(me, 3, panel)

    def local(tap, carry):
        full[tap, near_taps, :] = near[tap]
        full[tap, side_taps, :] = side[tap]
        return carry

    lax.fori_loop(0, 9, local, 0)
    taps = far0.shape[0]
    parts = ((taps * half, far0, diag0), (taps - taps * half, far1, diag1), (2 * taps, far2, diag2))
    for first, far, diag in parts:
        def remote(i, carry, first=first, far=far, diag=diag):
            full[first + i, far_taps, :] = far[i]
            full[first + i, diag_taps, :] = diag[i]
            return carry

        lax.fori_loop(0, far.shape[0], remote, 0)


def back_kernel(full, before, low, after, res, lat, table, grad, sums, framed, total):
    channels = low.shape[1]
    for row, source in enumerate((before[0], low[0], low[1], after[0])):
        for kx, moved in enumerate(shifts(source)):
            framed[kx, row] = jnp.transpose(moved)
    total[...] = jnp.zeros_like(total)

    def tap_step(tap, carry):
        ky = tap // 3
        kx = tap - 3 * ky
        window = jnp.concatenate([framed[2 - kx, 2 - ky], framed[2 - kx, 3 - ky]], axis=0)
        total[...] += dot_nn(window, full[tap])
        return carry

    lax.fori_loop(0, 9, tap_step, 0)
    columns = table[...]
    first = second = bottom = loss = None
    for row in range(2):
        normed = (plane(lat, row, channels) - columns[:, 0:1]) * columns[:, 1:2]
        pre = normed * columns[:, 2:3] + columns[:, 3:4]
        s = jax.nn.sigmoid(pre)
        value = jnp.transpose(total[row * LANES : (row + 1) * LANES, :]) * s * (1.0 + pre * (1.0 - s))
        grad[row] = value
        r = res[row]
        terms = (value, value * normed, r, r * r)
        if row == 0:
            first, second, bottom, loss = terms
        else:
            first, second, bottom, loss = (
                first + terms[0], second + terms[1], bottom + terms[2], loss + terms[3],
            )
    add = functools.partial(jnp.sum, axis=1, keepdims=True)
    sums[...] = as_rows([add(first), add(second), add(bottom), add(loss)], channels)


def latents_kernel(cells, s0, s1, s2, s3, given, res, grad, lat, table, out, total):
    channels = total.shape[1]
    member = membership(channels)
    sums = (s0[...] + s1[...]) + (s2[...] + s3[...])
    total[...] = sums
    means = group_sums(sums * given[0:1], member) / cells
    rows = to_channels(means, member)
    columns = as_columns([rows[0:1], rows[1:2]], channels)
    constants = table[...]
    inverse = constants[:, 1:2]
    for row in range(2):
        normed = (plane(lat, row, channels) - constants[:, 0:1]) * inverse
        change = grad[row] * constants[:, 2:3] - columns[:, 0:1] - normed * columns[:, 1:2]
        out[pl.ds(row, channels, stride=2), :] = res[row] + inverse * change


def weight_pair(strip, pair, aligned, one, two, first, spread, lefts, emit):
    panel, channels = aligned.shape[2], spread[0].shape[1]
    for m in range(2):
        for k in range(4):
            for row in range(2):
                lane = pl.ds((2 * k + row) * LANES, LANES)
                source = aligned[k, row] if m == 0 else jnp.where(first, one[k, row], two[k, row])
                moved = shifts(source)
                for kx in range(3):
                    lefts[(strip & 1) ^ m, kx * panel : (kx + 1) * panel, lane] = moved[2 - kx]

    def step(ky, carry):
        product = None
        for m in range(2):
            right = jnp.concatenate(
                [spread[k][4 * pair + 2 * m + ky + row] for k in range(4) for row in range(2)], axis=1
            )
            part = dot_nt(lefts[m], right)
            product = part if product is None else product + part
        emit(pl.ds(3 * ky, 3), product.reshape(3, panel, channels))
        return carry

    lax.fori_loop(0, 3, step, 0)


def totals_kernel(cells, s0, s1, s2, s3, loss, grads):
    sums = (s0[...] + s1[...]) + (s2[...] + s3[...])
    square = jnp.sum(sums[3:4], axis=1, keepdims=True) / (cells * sums.shape[1])
    loss[...] = jnp.broadcast_to(square, loss.shape)
    for row, source in enumerate((2, 1, 0)):
        grads[row : row + 1] = sums[source : source + 1] / cells


def spread_kernel(place, mine, above, beyond, below, spread):
    strip = place[0]
    channels = spread.shape[1]
    spread[0] = jnp.zeros((channels, LANES), BF16)
    spread[9] = jnp.zeros((channels, LANES), BF16)
    for m, source in enumerate((mine, above, beyond, below)):
        for row in range(2):
            spread[1 + 2 * ((strip + m) & 3) + row] = source[row]


def near_weight_kernel(place, own, plus, minus, h0, h1, h2, h3, out, lefts):
    strip = place[0]

    def emit(taps, product):
        out[taps] = product

    weight_pair(strip, strip // 2, own, plus, minus, (strip & 1) == 0, (h0, h1, h2, h3), lefts, emit)


def far_weight_kernel(cells, place, plus, minus, far, h0, h1, h2, h3, near, out, lefts):
    strip = place[0]

    def emit(taps, product):
        out[taps] = (near[taps] + product) / cells

    weight_pair(strip, 1 - strip // 2, far, minus, plus, (strip & 1) == 0, (h0, h1, h2, h3), lefts, emit)


VM = pl.BlockSpec(memory_space=pltpu.VMEM)
SM = pl.BlockSpec(memory_space=pltpu.SMEM)


def call(kernel, outs, specs, args, scratch=(), mib=8, us=3):
    return pl.pallas_call(
        kernel,
        out_shape=outs,
        in_specs=specs,
        out_specs=jax.tree.map(lambda _: VM, outs),
        scratch_shapes=scratch,
        compiler_params=pltpu.CompilerParams(vmem_limit_bytes=mib << 20),
        cost_estimate=pl.CostEstimate(
            flops=int(us * 1e9), bytes_accessed=int(us * 3e6), transcendentals=0
        ),
    )(*args)


def shape(dims, dtype):
    return jax.ShapeDtypeStruct(dims, dtype)


def swap(x, axis, mask):
    size = lax.axis_size(axis)
    return lax.ppermute(x, axis, [(i, i ^ mask) for i in range(size)])


def ring(x, axis, step):
    size = lax.axis_size(axis)
    return lax.ppermute(x, axis, [((i + step) % size, i) for i in range(size)])


def after_all(x, *others):
    return lax.optimization_barrier((x, *others))[0]


def strips_of_four(latents, teacher, norm_gain, norm_shift, conv_weight, conv_bias):
    row_devices = lax.axis_size("rows")
    panel_devices = lax.axis_size("wt")
    _, channels, strip_rows, width = latents.shape
    panel = conv_weight.shape[0]
    strip_cells = strip_rows * width
    total_cells = panel_devices * row_devices * strip_cells
    group_cells = channels // GROUPS * strip_cells * row_devices
    up = [(i, i + 1) for i in range(row_devices - 1)]
    down = [(i + 1, i) for i in range(row_devices - 1)]
    lat = latents.reshape(channels * strip_rows, width)
    tea = teacher.reshape(channels * strip_rows, width)
    given = jnp.stack([norm_gain, norm_shift, conv_bias])
    part = lax.axis_index("grp").astype(jnp.int32)
    here = lax.axis_index("wt").astype(jnp.int32)
    strip = lax.axis_index("rows").astype(jnp.int32)
    place = jnp.stack([strip, here, part])

    near = jnp.transpose(conv_weight, (1, 0, 2))
    far0 = swap(lax.dynamic_slice_in_dim(near, part * 2, 2, axis=0), "wt", 2)

    stats = call(stats_kernel, shape((8, channels), F32), [VM], (lat,))
    hidden, table = call(
        functools.partial(hidden_kernel, group_cells),
        (shape((strip_rows, channels, width), BF16), shape((channels, LANES), F32)),
        [VM] * 6,
        (lat, after_all(stats, far0), *(swap(stats, "rows", m) for m in (1, 2, 3)), given),
        us=0.05,
    )
    above, below = ring(hidden, "rows", 1), ring(hidden, "rows", 3)
    side = swap(after_all(near, hidden), "wt", 1)
    far2 = swap(after_all(near, far0)[4:9], "wt", 2)
    far1 = swap(after_all(far0, hidden), "grp", 1)
    base = call(
        base_kernel, shape((strip_rows, channels, width), F32), [VM] * 3, (lat, tea, table), us=5
    )
    framed = call(
        frame_kernel,
        shape((3, 4, channels, width), BF16),
        [SM] + [VM] * 3,
        (place, after_all(hidden, base), above, below),
        us=5,
    )
    beyond = ring(above, "rows", 1)
    across = [swap(after_all(hidden, framed), "wt", 2), swap(after_all(above, framed), "wt", 2)]
    rows_of = functools.partial(
        call, spread_kernel, shape((10, channels, width), BF16), [SM] + [VM] * 4, us=3
    )
    part0, block0, block1 = call(
        near_conv_kernel,
        (
            shape((2, strip_rows, panel, width), F32),
            shape((strip_rows, panel, width), BF16),
            shape((strip_rows, panel, width), BF16),
        ),
        [SM] + [VM] * 4,
        (place, near, side, framed, base),
        [pltpu.VMEM((2 * panel, 2 * LANES), F32)],
        us=20,
    )
    far0, far1, far2, _ = lax.optimization_barrier((far0, far1, far2, framed))
    diag0, diag1, diag2 = swap(far0, "wt", 1), swap(far1, "wt", 1), swap(far2, "wt", 1)
    weights = (near, side, far0, far1, far2, diag0, diag1, diag2)
    res, low, block23 = call(
        far_conv_kernel,
        (
            shape((strip_rows, channels, width), F32),
            shape((strip_rows, channels, width), BF16),
            shape((2, strip_rows, panel, width), BF16),
        ),
        [SM] + [VM] * 9,
        (place, *weights[2:], framed, base, part0),
        [pltpu.VMEM((2 * panel, 2 * LANES), F32)],
        us=0.05,
    )

    low_before = lax.ppermute(low[1:2], "rows", up)
    low_after = lax.ppermute(low[0:1], "rows", down)
    block1 = swap(block1, "wt", 1)
    block23 = swap(after_all(block23, across[0]), "wt", 2)
    stacked = after_all(jnp.stack([block0, block1, block23[0], swap(block23[1], "wt", 1)]), across[1])
    plus = ring(stacked, "rows", 1)
    minus = ring(after_all(stacked, plus), "rows", 3)
    far = ring(plus, "rows", 1)
    full = call(
        assemble_kernel,
        shape((9, channels, channels), BF16),
        [SM] + [VM] * 8,
        (after_all(place, stacked), *weights),
        us=5,
    )

    across += [swap(after_all(beyond, stacked), "wt", 2), swap(after_all(below, block23), "wt", 2)]
    own_rows = rows_of((place, after_all(hidden, stacked), above, beyond, below))
    other_rows = swap(own_rows, "wt", 1)

    grad, sums = call(
        back_kernel,
        (shape((strip_rows, channels, width), F32), shape((8, channels), F32)),
        [VM] * 7,
        (full, low_before, after_all(low, plus), low_after, res, lat, table),
        [
            pltpu.VMEM((3, 4, LANES, channels), BF16),
            pltpu.VMEM((2 * LANES, channels), F32),
        ],
        mib=12, us=30,
    )
    sums = after_all(sums, minus)
    across_rows = rows_of((after_all(place, sums), *across))
    diag_rows = swap(across_rows, "wt", 1)
    grad_latents, sums = call(
        functools.partial(latents_kernel, group_cells),
        (shape((channels * strip_rows, width), F32), shape((8, channels), F32)),
        [VM] * 9,
        (
            sums, *(swap(sums, "rows", m) for m in (1, 2, 3)),
            given, res, grad, lat, table,
        ),
        us=0.05,
    )
    images = (own_rows, other_rows, across_rows, diag_rows)
    near_weight = call(
        near_weight_kernel,
        shape((9, panel, channels), F32),
        [SM] + [VM] * 7,
        (after_all(place, grad_latents), stacked, plus, minus, *images),
        [pltpu.VMEM((2, 3 * panel, 8 * LANES), BF16)],
        mib=14, us=30,
    )
    loss, param_grads = call(
        functools.partial(totals_kernel, total_cells),
        (shape((1, LANES), F32), shape((3, channels), F32)),
        [VM] * 4,
        (sums, *(swap(sums, "wt", m) for m in (1, 2, 3))),
        us=0.05,
    )

    grad_weight = call(
        functools.partial(far_weight_kernel, total_cells),
        shape((9, panel, channels), F32),
        [SM] + [VM] * 8,
        (place, plus, minus, far, *images, near_weight),
        [pltpu.VMEM((2, 3 * panel, 8 * LANES), BF16)],
        mib=16, us=0.05,
    )
    return (
        loss[0, :1],
        grad_latents.reshape(latents.shape),
        jnp.transpose(grad_weight, (1, 0, 2)),
        param_grads,
    )


def solution(mesh):
    placed = (
        P(("grp", "wt"), None, "rows", None),
        P(("grp", "wt"), None, "rows", None),
        P(),
        P(),
        P("wt", None, None),
        P(),
    )
    small = mesh.shape["rows"] == 4 and mesh.shape["wt"] == 4 and mesh.shape["grp"] == 2
    return jax.shard_map(
        strips_of_four if small else generic,
        mesh=mesh,
        in_specs=placed,
        out_specs=(
            P("grp"),
            P(("grp", "wt"), None, "rows", None),
            P(("grp", "wt"), None, None),
            P("grp", None),
        ),
        check_vma=False,
    )
```

```python
import functools

import jax
import jax.numpy as jnp
from jax import lax
from jax.experimental import pallas as pl
from jax.experimental.pallas import tpu as pltpu
from jax.sharding import PartitionSpec as P

GROUPS = 32
LANES = 128
epsilon = 1e-05
F32 = jnp.float32
BF16 = jnp.bfloat16


def with_halo(shard, sides, width):
    for axis, dim in sides:
        devices, length = (lax.axis_size(axis), shard.shape[dim])
        up = [(i, (i + 1) % devices) for i in range(devices - 1)]
        down = [(j, i) for i, j in up]
        last = lax.slice_in_dim(shard, length - width, length, axis=dim)
        leading = lax.slice_in_dim(shard, 0, width, axis=dim)
        before = lax.ppermute(last, axis, up)
        after = lax.ppermute(leading, axis, down)
        shard = jnp.concatenate([before, shard, after], axis=dim)
    return shard


def conv_taps(weights, padded, strip_rows, column_count):
    running = None
    for tap_index in range(9):
        tap_row, tap_col = (tap_index // 3, tap_index % 3)
        window = padded[:, :, tap_row : tap_row + strip_rows, tap_col : tap_col + column_count]
        window = window.reshape(padded.shape[0], padded.shape[1], strip_rows * column_count)
        product = jnp.einsum(
            "oi,nip->nop", weights[:, tap_index, :], window, preferred_element_type=jnp.float32
        )
        running = product if running is None else running + product
    return running


def transpose_taps(weights, padded, strip_rows, column_count):
    running = None
    for tap_index in range(9):
        tap_row, tap_col = (tap_index // 3, tap_index % 3)
        window = padded[
            :, :, 2 - tap_row : 2 - tap_row + strip_rows, 2 - tap_col : 2 - tap_col + column_count
        ]
        window = window.reshape(padded.shape[0], padded.shape[1], strip_rows * column_count)
        product = jnp.einsum(
            "oi,nop->nip", weights[:, tap_index, :], window, preferred_element_type=jnp.float32
        )
        running = product if running is None else running + product
    return running


def weight_terms(residual, padded, strip_rows, column_count):
    columns = []
    for tap_index in range(9):
        tap_row, tap_col = (tap_index // 3, tap_index % 3)
        window = padded[:, :, tap_row : tap_row + strip_rows, tap_col : tap_col + column_count]
        window = window.reshape(padded.shape[0], padded.shape[1], strip_rows * column_count)
        columns.append(
            jnp.einsum("nop,nip->oi", residual, window, preferred_element_type=jnp.float32)
        )
    return jnp.stack(columns, axis=1)


def generic(latents, teacher, norm_gain, norm_shift, conv_weight, conv_bias):
    row_devices = lax.axis_size("rows")
    panel_devices = lax.axis_size("wt")
    images, channels, strip_rows, column_count = latents.shape
    cell_count = strip_rows * column_count
    total_cells = panel_devices * row_devices * cell_count
    group_cells = channels // GROUPS * cell_count * row_devices
    grouped = latents.reshape(images, GROUPS, channels // GROUPS, cell_count)
    group_sum, square_sum = lax.psum(
        (
            jnp.sum(grouped, axis=(2, 3), keepdims=True),
            jnp.sum(jnp.square(grouped), axis=(2, 3), keepdims=True),
        ),
        "rows",
    )
    group_mean = group_sum / group_cells
    centered = grouped - group_mean
    group_var = square_sum / group_cells - jnp.square(group_mean)
    inverse = lax.rsqrt(group_var + epsilon)
    normed = (centered * inverse).reshape(images, channels, cell_count)
    gain_column = norm_gain[None, :, None]
    pre_norm = normed * gain_column + norm_shift[None, :, None]
    sigmoid_pre = jax.nn.sigmoid(pre_norm)
    hidden = (pre_norm * sigmoid_pre).astype(jnp.bfloat16)
    column_pad = ((0, 0), (0, 0), (0, 0), (1, 1))
    framed_hidden = with_halo(
        hidden.reshape(images, channels, strip_rows, column_count), (("rows", 2),), 1
    )
    padded = jnp.pad(framed_hidden, column_pad)
    all_images = lax.all_gather(framed_hidden, "wt", axis=0, tiled=True)
    all_padded = jnp.pad(all_images, column_pad)
    conv_out = conv_taps(
        lax.all_gather(conv_weight, "wt", axis=0, tiled=True), padded, strip_rows, column_count
    )
    residual = (
        latents.reshape(images, channels, cell_count)
        + conv_out
        + conv_bias[None, :, None]
        - teacher.reshape(images, channels, cell_count)
    )
    low_residual = residual.astype(jnp.bfloat16)
    framed_residual = with_halo(
        low_residual.reshape(images, channels, strip_rows, column_count), (("rows", 2),), 1
    )
    padded_residual = jnp.pad(framed_residual, column_pad)
    panel_residual = lax.all_to_all(framed_residual, "wt", split_axis=1, concat_axis=0, tiled=True)
    panel_rows = channels // panel_devices
    panel_inner = panel_residual[:, :, 1 : strip_rows + 1, :].reshape(
        panel_residual.shape[0], panel_rows, cell_count
    )
    window = padded_residual
    grad_hidden = transpose_taps(
        lax.all_gather(conv_weight, "wt", axis=0, tiled=True), window, strip_rows, column_count
    )
    window = panel_inner
    weight_share = lax.psum_scatter(
        weight_terms(window, all_padded, strip_rows, column_count),
        "rows",
        scatter_dimension=0,
        tiled=True,
    )
    grad_weight = lax.all_gather(weight_share, "rows", axis=0, tiled=True) / total_cells
    grad_pre = grad_hidden * sigmoid_pre * (1.0 + pre_norm * (1.0 - sigmoid_pre))
    grad_norm = (grad_pre * gain_column).reshape(grouped.shape)
    normed_groups = normed.reshape(grouped.shape)
    first_sum, second_sum = lax.psum(
        (
            jnp.sum(grad_norm, axis=(2, 3), keepdims=True),
            jnp.sum(grad_norm * normed_groups, axis=(2, 3), keepdims=True),
        ),
        "rows",
    )
    first_mean = first_sum / group_cells
    second_mean = second_sum / group_cells
    grad_latents = residual.reshape(latents.shape) + (
        inverse * (grad_norm - first_mean - normed_groups * second_mean)
    ).reshape(latents.shape)
    totals = lax.psum(
        (
            jnp.sum(jnp.square(residual)),
            jnp.sum(residual, axis=(0, 2)),
            jnp.sum(grad_pre * normed, axis=(0, 2)),
            jnp.sum(grad_pre, axis=(0, 2)),
        ),
        ("rows", "wt"),
    )
    mean_loss = (totals[0] / (total_cells * channels)).reshape(1)
    param_grads = jnp.stack([totals[1], totals[2], totals[3]]) / total_cells
    return (mean_loss, grad_latents, grad_weight, param_grads)


def plane(ref, row, channels):
    return ref[pl.ds(row, channels, stride=2), :]


def split3(x):
    a = x.astype(BF16)
    rest = x - a.astype(F32)
    b = rest.astype(BF16)
    c = (rest - b.astype(F32)).astype(BF16)
    return a, b, c


def membership(channels):
    size = channels // GROUPS
    channel = lax.broadcasted_iota(jnp.int32, (channels, LANES), 0)
    first = lax.broadcasted_iota(jnp.int32, (channels, LANES), 1) * size
    inside = (channel >= first) & (channel < first + size)
    return jnp.where(inside, 1.0, 0.0).astype(BF16)


def dot_nn(a, b):
    return lax.dot_general(a, b, (((1,), (0,)), ((), ())), preferred_element_type=F32)


def dot_nt(a, b):
    return lax.dot_general(a, b, (((1,), (1,)), ((), ())), preferred_element_type=F32)


def group_sums(rows, member):
    a, b, c = split3(rows)
    return dot_nn(a, member) + (dot_nn(b, member) + dot_nn(c, member))


def to_channels(rows, member):
    a, b, c = split3(rows)
    return dot_nt(a, member) + (dot_nt(b, member) + dot_nt(c, member))


def as_rows(columns, channels):
    lane = lax.broadcasted_iota(jnp.int32, (channels, LANES), 1)
    table = jnp.zeros((channels, LANES), F32)
    for i, column in enumerate(columns):
        table = jnp.where(lane == i, column, table)
    return jnp.transpose(table)[:8, :]


def as_columns(rows, channels):
    pad = jnp.zeros((LANES - len(rows), channels), F32)
    return jnp.transpose(jnp.concatenate(rows + [pad], axis=0))


def row_sum(a, b):
    return jnp.sum(a + b, axis=1, keepdims=True)


def stats_kernel(lat, out):
    channels = out.shape[1]
    a, b = plane(lat, 0, channels), plane(lat, 1, channels)
    out[...] = as_rows([row_sum(a, b), row_sum(a * a, b * b)], channels)


def hidden_kernel(cells, lat, s0, s1, s2, s3, given, hidden, table):
    channels = s0.shape[1]
    member = membership(channels)
    sums = group_sums((s0[...] + s1[...]) + (s2[...] + s3[...]), member)
    mean = sums[0:1] / cells
    var = sums[1:2] / cells - mean * mean
    inverse = lax.rsqrt(var + epsilon)
    pad = jnp.zeros((6, LANES), F32)
    rows = to_channels(jnp.concatenate([mean, inverse, pad], axis=0), member)
    columns = as_columns([rows[0:1], rows[1:2], given[0:1], given[1:2], given[2:3]], channels)
    table[...] = columns
    for row in range(2):
        normed = (plane(lat, row, channels) - columns[:, 0:1]) * columns[:, 1:2]
        pre = normed * columns[:, 2:3] + columns[:, 3:4]
        hidden[row] = (pre * jax.nn.sigmoid(pre)).astype(BF16)


def shifts(x):
    wide = x.astype(F32)
    lane = lax.broadcasted_iota(jnp.int32, x.shape, 1)
    left = jnp.where(lane == 0, 0.0, pltpu.roll(wide, 1, 1)).astype(BF16)
    right = jnp.where(lane == LANES - 1, 0.0, pltpu.roll(wide, LANES - 1, 1)).astype(BF16)
    return left, x, right


def base_kernel(lat, tea, table, base):
    channels = table.shape[0]
    for row in range(2):
        base[row] = plane(lat, row, channels) + table[:, 4:5] - plane(tea, row, channels)


def frame_kernel(place, mine, above, below, framed):
    strip = place[0]
    edge = jnp.zeros_like(mine[0])
    before = jnp.where(strip > 0, below[1], edge)
    after = jnp.where(strip < 3, above[0], edge)
    for row, source in enumerate((before, mine[0], mine[1], after)):
        for kx, moved in enumerate(shifts(source)):
            framed[kx, row] = moved


def panel_rows(me, k, panel):
    return pl.ds(pl.multiple_of((me ^ k) * panel, panel), panel)


def conv_step(total, framed, ky, kx, first, second):
    window = jnp.concatenate([framed[kx, ky], framed[kx, ky + 1]], axis=1)
    total[...] += dot_nn(jnp.concatenate([first, second], axis=0), window)


def near_conv_kernel(place, near, side, framed, base, part, block0, block1, total):
    me = place[1]
    panel = near.shape[1]
    total[...] = jnp.zeros_like(total)

    def step(tap, carry):
        ky = tap // 3
        conv_step(total, framed, ky, tap - 3 * ky, near[tap], side[tap])
        return carry

    lax.fori_loop(0, 9, step, 0)
    for k, block in enumerate((block0, block1)):
        for row in range(2):
            value = base[row, panel_rows(me, k, panel), :] + (
                total[k * panel : (k + 1) * panel, row * LANES : (row + 1) * LANES]
            )
            part[k, row] = value
            block[row] = value.astype(BF16)


def far_conv_kernel(
    place, far0, far1, far2, far3, far4, diag0, diag1, diag2, diag3, diag4, framed, base, part,
    res, low, block23, total,
):
    me, half = place[1], place[2]
    panel = far0.shape[1]
    total[...] = jnp.zeros_like(total)

    def run(first, far, diag):
        def step(i, carry):
            tap = first + i
            ky = tap // 3
            conv_step(total, framed, ky, tap - 3 * ky, far[i], diag[i])
            return carry

        lax.fori_loop(0, far.shape[0], step, 0)

    run(2 * half, far0, diag0)
    run(2 - 2 * half, far1, diag1)
    run(4 + half, far2, diag2)
    run(5 - half, far3, diag3)
    run(6, far4, diag4)
    for k in range(4):
        rows = panel_rows(me, k, panel)
        for row in range(2):
            if k < 2:
                value = part[k, row]
            else:
                value = base[row, rows, :] + (
                    total[(k - 2) * panel : (k - 1) * panel, row * LANES : (row + 1) * LANES]
                )
                block23[k - 2, row] = value.astype(BF16)
            res[row, rows, :] = value
            low[row, rows, :] = value.astype(BF16)


def assemble_kernel(
    place, near, side, far0, far1, far2, far3, far4, diag0, diag1, diag2, diag3, diag4, full
):
    me, half = place[1], place[2]
    panel = near.shape[1]
    near_taps, side_taps = panel_rows(me, 0, panel), panel_rows(me, 1, panel)
    far_taps, diag_taps = panel_rows(me, 2, panel), panel_rows(me, 3, panel)

    def local(tap, carry):
        full[tap, near_taps, :] = near[tap]
        full[tap, side_taps, :] = side[tap]
        return carry

    lax.fori_loop(0, 9, local, 0)
    parts = (
        (2 * half, far0, diag0), (2 - 2 * half, far1, diag1), (4 + half, far2, diag2),
        (5 - half, far3, diag3), (6, far4, diag4),
    )
    for first, far, diag in parts:
        def remote(i, carry, first=first, far=far, diag=diag):
            full[first + i, far_taps, :] = far[i]
            full[first + i, diag_taps, :] = diag[i]
            return carry

        lax.fori_loop(0, far.shape[0], remote, 0)


def back_kernel(full, before, low, after, res, lat, table, grad, sums, framed, total):
    channels = low.shape[1]
    for row, source in enumerate((before[0], low[0], low[1], after[0])):
        for kx, moved in enumerate(shifts(source)):
            framed[kx, row] = jnp.transpose(moved)
    total[...] = jnp.zeros_like(total)

    def tap_step(tap, carry):
        ky = tap // 3
        kx = tap - 3 * ky
        window = jnp.concatenate([framed[2 - kx, 2 - ky], framed[2 - kx, 3 - ky]], axis=0)
        total[...] += dot_nn(window, full[tap])
        return carry

    lax.fori_loop(0, 9, tap_step, 0)
    columns = table[...]
    first = second = bottom = loss = None
    for row in range(2):
        normed = (plane(lat, row, channels) - columns[:, 0:1]) * columns[:, 1:2]
        pre = normed * columns[:, 2:3] + columns[:, 3:4]
        s = jax.nn.sigmoid(pre)
        value = jnp.transpose(total[row * LANES : (row + 1) * LANES, :]) * s * (1.0 + pre * (1.0 - s))
        grad[row] = value
        r = res[row]
        terms = (value, value * normed, r, r * r)
        if row == 0:
            first, second, bottom, loss = terms
        else:
            first, second, bottom, loss = (
                first + terms[0], second + terms[1], bottom + terms[2], loss + terms[3],
            )
    add = functools.partial(jnp.sum, axis=1, keepdims=True)
    sums[...] = as_rows([add(first), add(second), add(bottom), add(loss)], channels)


def latents_kernel(cells, s0, s1, s2, s3, given, res, grad, lat, table, out, total):
    channels = total.shape[1]
    member = membership(channels)
    sums = (s0[...] + s1[...]) + (s2[...] + s3[...])
    total[...] = sums
    means = group_sums(sums * given[0:1], member) / cells
    rows = to_channels(means, member)
    columns = as_columns([rows[0:1], rows[1:2]], channels)
    constants = table[...]
    inverse = constants[:, 1:2]
    for row in range(2):
        normed = (plane(lat, row, channels) - constants[:, 0:1]) * inverse
        change = grad[row] * constants[:, 2:3] - columns[:, 0:1] - normed * columns[:, 1:2]
        out[pl.ds(row, channels, stride=2), :] = res[row] + inverse * change


def weight_pair(strip, pair, aligned, one, two, first, spread, lefts, emit):
    panel, channels = aligned.shape[2], spread[0].shape[1]
    for m in range(2):
        for k in range(4):
            for row in range(2):
                lane = pl.ds((2 * k + row) * LANES, LANES)
                source = aligned[k, row] if m == 0 else jnp.where(first, one[k, row], two[k, row])
                moved = shifts(source)
                for kx in range(3):
                    lefts[(strip & 1) ^ m, kx * panel : (kx + 1) * panel, lane] = moved[2 - kx]

    def step(ky, carry):
        product = None
        for m in range(2):
            right = jnp.concatenate(
                [spread[k][4 * pair + 2 * m + ky + row] for k in range(4) for row in range(2)], axis=1
            )
            part = dot_nt(lefts[m], right)
            product = part if product is None else product + part
        emit(pl.ds(3 * ky, 3), product.reshape(3, panel, channels))
        return carry

    lax.fori_loop(0, 3, step, 0)


def totals_kernel(cells, s0, s1, s2, s3, loss, grads):
    sums = (s0[...] + s1[...]) + (s2[...] + s3[...])
    square = jnp.sum(sums[3:4], axis=1, keepdims=True) / (cells * sums.shape[1])
    loss[...] = jnp.broadcast_to(square, loss.shape)
    for row, source in enumerate((2, 1, 0)):
        grads[row : row + 1] = sums[source : source + 1] / cells


def spread_kernel(place, mine, above, beyond, below, spread):
    strip = place[0]
    channels = spread.shape[1]
    spread[0] = jnp.zeros((channels, LANES), BF16)
    spread[9] = jnp.zeros((channels, LANES), BF16)
    for m, source in enumerate((mine, above, beyond, below)):
        for row in range(2):
            spread[1 + 2 * ((strip + m) & 3) + row] = source[row]


def near_weight_kernel(place, own, plus, minus, h0, h1, h2, h3, out, lefts):
    strip = place[0]

    def emit(taps, product):
        out[taps] = product

    weight_pair(strip, strip // 2, own, plus, minus, (strip & 1) == 0, (h0, h1, h2, h3), lefts, emit)


def far_weight_kernel(cells, place, plus, minus, far, h0, h1, h2, h3, near, out, lefts, held, sems):
    strip = place[0]

    def written(taps, slot):
        return pltpu.make_async_copy(held.at[taps], out.at[taps], sems.at[slot])

    def emit(taps, product):
        held[taps] = (near[taps] + product) / cells
        for slot in range(3):
            @pl.when(taps.start == 3 * slot)
            def _(slot=slot):
                written(pl.ds(3 * slot, 3), slot).start()

    weight_pair(strip, 1 - strip // 2, far, minus, plus, (strip & 1) == 0, (h0, h1, h2, h3), lefts, emit)
    for slot in range(3):
        written(pl.ds(3 * slot, 3), slot).wait()


VM = pl.BlockSpec(memory_space=pltpu.VMEM)
SM = pl.BlockSpec(memory_space=pltpu.SMEM)


def call(kernel, outs, specs, args, scratch=(), mib=8, us=3, space=VM):
    return pl.pallas_call(
        kernel,
        out_shape=outs,
        in_specs=specs,
        out_specs=jax.tree.map(lambda _: space, outs),
        scratch_shapes=scratch,
        compiler_params=pltpu.CompilerParams(vmem_limit_bytes=mib << 20),
        cost_estimate=pl.CostEstimate(
            flops=int(us * 1e9), bytes_accessed=int(us * 3e6), transcendentals=0
        ),
    )(*args)


def shape(dims, dtype):
    return jax.ShapeDtypeStruct(dims, dtype)


def swap(x, axis, mask):
    size = lax.axis_size(axis)
    return lax.ppermute(x, axis, [(i, i ^ mask) for i in range(size)])


def ring(x, axis, step):
    size = lax.axis_size(axis)
    return lax.ppermute(x, axis, [((i + step) % size, i) for i in range(size)])


def after_all(x, *others):
    return lax.optimization_barrier((x, *others))[0]


def strips_of_four(latents, teacher, norm_gain, norm_shift, conv_weight, conv_bias):
    row_devices = lax.axis_size("rows")
    panel_devices = lax.axis_size("wt")
    _, channels, strip_rows, width = latents.shape
    panel = conv_weight.shape[0]
    strip_cells = strip_rows * width
    total_cells = panel_devices * row_devices * strip_cells
    group_cells = channels // GROUPS * strip_cells * row_devices
    up = [(i, i + 1) for i in range(row_devices - 1)]
    down = [(i + 1, i) for i in range(row_devices - 1)]
    lat = latents.reshape(channels * strip_rows, width)
    tea = teacher.reshape(channels * strip_rows, width)
    given = jnp.stack([norm_gain, norm_shift, conv_bias])
    part = lax.axis_index("grp").astype(jnp.int32)
    here = lax.axis_index("wt").astype(jnp.int32)
    strip = lax.axis_index("rows").astype(jnp.int32)
    place = jnp.stack([strip, here, part])

    near = jnp.transpose(conv_weight, (1, 0, 2))
    far0 = swap(lax.dynamic_slice_in_dim(near, part * 2, 2, axis=0), "wt", 2)
    side = swap(near, "wt", 1)

    stats = call(stats_kernel, shape((8, channels), F32), [VM], (lat,))
    hidden, table = call(
        functools.partial(hidden_kernel, group_cells),
        (shape((strip_rows, channels, width), BF16), shape((channels, LANES), F32)),
        [VM] * 6,
        (lat, after_all(stats, far0, side), *(swap(stats, "rows", m) for m in (1, 2, 3)), given),
        us=0.05,
    )
    above, below = ring(hidden, "rows", 1), ring(hidden, "rows", 3)
    later = after_all(near, hidden)
    far2 = swap(lax.dynamic_slice_in_dim(later, 4 + part, 1, axis=0), "wt", 2)
    far4 = swap(later[6:9], "wt", 2)
    far1, far3 = swap(after_all(far0, hidden), "grp", 1), swap(far2, "grp", 1)
    base = call(
        base_kernel, shape((strip_rows, channels, width), F32), [VM] * 3, (lat, tea, table), us=5
    )
    framed = call(
        frame_kernel,
        shape((3, 4, channels, width), BF16),
        [SM] + [VM] * 3,
        (place, after_all(hidden, base), above, below),
        us=5,
    )
    beyond = ring(above, "rows", 1)
    across = [swap(after_all(hidden, framed), "wt", 2)]
    rows_of = functools.partial(
        call, spread_kernel, shape((10, channels, width), BF16), [SM] + [VM] * 4, us=3
    )
    part0, block0, block1 = call(
        near_conv_kernel,
        (
            shape((2, strip_rows, panel, width), F32),
            shape((strip_rows, panel, width), BF16),
            shape((strip_rows, panel, width), BF16),
        ),
        [SM] + [VM] * 4,
        (place, near, side, framed, base),
        [pltpu.VMEM((2 * panel, 2 * LANES), F32)],
        us=20,
    )
    fars = lax.optimization_barrier((far0, far1, far2, far3, far4, framed))[:5]
    weights = (near, side, *fars, *(swap(far, "wt", 1) for far in fars))
    res, low, block23 = call(
        far_conv_kernel,
        (
            shape((strip_rows, channels, width), F32),
            shape((strip_rows, channels, width), BF16),
            shape((2, strip_rows, panel, width), BF16),
        ),
        [SM] + [VM] * 13,
        (place, *weights[2:], framed, base, part0),
        [pltpu.VMEM((2 * panel, 2 * LANES), F32)],
        us=0.05,
    )

    block1 = swap(block1, "wt", 1)
    block23 = swap(after_all(block23, across[0]), "wt", 2)
    stacked = jnp.stack([block0, block1, block23[0], swap(block23[1], "wt", 1)])
    settled = after_all(low, stacked)
    low_before = lax.ppermute(settled[1:2], "rows", up)
    low_after = lax.ppermute(settled[0:1], "rows", down)
    plus = ring(stacked, "rows", 1)
    minus = ring(after_all(stacked, plus), "rows", 3)
    far = ring(plus, "rows", 1)
    full = call(
        assemble_kernel,
        shape((9, channels, channels), BF16),
        [SM] + [VM] * 12,
        (after_all(place, stacked), *weights),
        us=5,
    )

    for strip_in, last in ((above, block23), (below, None), (beyond, None)):
        across.append(swap(after_all(strip_in, across[-1] if last is None else last), "wt", 2))
    across[2:] = across[:1:-1]
    own_rows = rows_of((place, after_all(hidden, stacked), above, beyond, below))
    other_rows = swap(own_rows, "wt", 1)

    grad, sums = call(
        back_kernel,
        (shape((strip_rows, channels, width), F32), shape((8, channels), F32)),
        [VM] * 7,
        (full, low_before, after_all(low, plus, across[1]), low_after, res, lat, table),
        [
            pltpu.VMEM((3, 4, LANES, channels), BF16),
            pltpu.VMEM((2 * LANES, channels), F32),
        ],
        mib=12, us=30,
    )
    sums = after_all(sums, minus)
    across_rows = rows_of((after_all(place, sums), *across))
    diag_rows = swap(across_rows, "wt", 1)
    grad_latents, sums = call(
        functools.partial(latents_kernel, group_cells),
        (shape((channels * strip_rows, width), F32), shape((8, channels), F32)),
        [VM] * 9,
        (
            sums, *(swap(sums, "rows", m) for m in (1, 2, 3)),
            given, res, grad, lat, table,
        ),
        us=0.05,
    )
    images = (own_rows, other_rows, across_rows, diag_rows)
    near_weight = call(
        near_weight_kernel,
        shape((9, panel, channels), F32),
        [SM] + [VM] * 7,
        (after_all(place, grad_latents), stacked, plus, minus, *images),
        [pltpu.VMEM((2, 3 * panel, 8 * LANES), BF16)],
        mib=14, us=30,
    )
    loss, param_grads = call(
        functools.partial(totals_kernel, total_cells),
        (shape((1, LANES), F32), shape((3, channels), F32)),
        [VM] * 4,
        (sums, *(swap(sums, "wt", m) for m in (1, 2, 3))),
        us=0.05,
    )

    grad_weight = call(
        functools.partial(far_weight_kernel, total_cells),
        shape((9, panel, channels), F32),
        [SM] + [VM] * 8,
        (place, plus, minus, far, *images, near_weight),
        [
            pltpu.VMEM((2, 3 * panel, 8 * LANES), BF16),
            pltpu.VMEM((9, panel, channels), F32),
            pltpu.SemaphoreType.DMA((3,)),
        ],
        mib=18, us=0.05, space=pl.BlockSpec(memory_space=pl.ANY),
    )
    return (
        loss[0, :1],
        grad_latents.reshape(latents.shape),
        jnp.transpose(grad_weight, (1, 0, 2)),
        param_grads,
    )


def solution(mesh):
    placed = (
        P(("grp", "wt"), None, "rows", None),
        P(("grp", "wt"), None, "rows", None),
        P(),
        P(),
        P("wt", None, None),
        P(),
    )
    small = mesh.shape["rows"] == 4 and mesh.shape["wt"] == 4 and mesh.shape["grp"] == 2
    return jax.shard_map(
        strips_of_four if small else generic,
        mesh=mesh,
        in_specs=placed,
        out_specs=(
            P("grp"),
            P(("grp", "wt"), None, "rows", None),
            P(("grp", "wt"), None, None),
            P("grp", None),
        ),
        check_vma=False,
    )
```

```python
import functools

import jax
import jax.numpy as jnp
from jax import lax
from jax.experimental import pallas as pl
from jax.experimental.pallas import tpu as pltpu
from jax.sharding import PartitionSpec as P

GROUPS = 32
LANES = 128
epsilon = 1e-05
F32 = jnp.float32
BF16 = jnp.bfloat16


def with_halo(shard, sides, width):
    for axis, dim in sides:
        devices, length = (lax.axis_size(axis), shard.shape[dim])
        up = [(i, (i + 1) % devices) for i in range(devices - 1)]
        down = [(j, i) for i, j in up]
        last = lax.slice_in_dim(shard, length - width, length, axis=dim)
        leading = lax.slice_in_dim(shard, 0, width, axis=dim)
        before = lax.ppermute(last, axis, up)
        after = lax.ppermute(leading, axis, down)
        shard = jnp.concatenate([before, shard, after], axis=dim)
    return shard


def conv_taps(weights, padded, strip_rows, column_count):
    running = None
    for tap_index in range(9):
        tap_row, tap_col = (tap_index // 3, tap_index % 3)
        window = padded[:, :, tap_row : tap_row + strip_rows, tap_col : tap_col + column_count]
        window = window.reshape(padded.shape[0], padded.shape[1], strip_rows * column_count)
        product = jnp.einsum(
            "oi,nip->nop", weights[:, tap_index, :], window, preferred_element_type=jnp.float32
        )
        running = product if running is None else running + product
    return running


def transpose_taps(weights, padded, strip_rows, column_count):
    running = None
    for tap_index in range(9):
        tap_row, tap_col = (tap_index // 3, tap_index % 3)
        window = padded[
            :, :, 2 - tap_row : 2 - tap_row + strip_rows, 2 - tap_col : 2 - tap_col + column_count
        ]
        window = window.reshape(padded.shape[0], padded.shape[1], strip_rows * column_count)
        product = jnp.einsum(
            "oi,nop->nip", weights[:, tap_index, :], window, preferred_element_type=jnp.float32
        )
        running = product if running is None else running + product
    return running


def weight_terms(residual, padded, strip_rows, column_count):
    columns = []
    for tap_index in range(9):
        tap_row, tap_col = (tap_index // 3, tap_index % 3)
        window = padded[:, :, tap_row : tap_row + strip_rows, tap_col : tap_col + column_count]
        window = window.reshape(padded.shape[0], padded.shape[1], strip_rows * column_count)
        columns.append(
            jnp.einsum("nop,nip->oi", residual, window, preferred_element_type=jnp.float32)
        )
    return jnp.stack(columns, axis=1)


def generic(latents, teacher, norm_gain, norm_shift, conv_weight, conv_bias):
    row_devices = lax.axis_size("rows")
    panel_devices = lax.axis_size("wt")
    images, channels, strip_rows, column_count = latents.shape
    cell_count = strip_rows * column_count
    total_cells = panel_devices * row_devices * cell_count
    group_cells = channels // GROUPS * cell_count * row_devices
    grouped = latents.reshape(images, GROUPS, channels // GROUPS, cell_count)
    group_sum, square_sum = lax.psum(
        (
            jnp.sum(grouped, axis=(2, 3), keepdims=True),
            jnp.sum(jnp.square(grouped), axis=(2, 3), keepdims=True),
        ),
        "rows",
    )
    group_mean = group_sum / group_cells
    centered = grouped - group_mean
    group_var = square_sum / group_cells - jnp.square(group_mean)
    inverse = lax.rsqrt(group_var + epsilon)
    normed = (centered * inverse).reshape(images, channels, cell_count)
    gain_column = norm_gain[None, :, None]
    pre_norm = normed * gain_column + norm_shift[None, :, None]
    sigmoid_pre = jax.nn.sigmoid(pre_norm)
    hidden = (pre_norm * sigmoid_pre).astype(jnp.bfloat16)
    column_pad = ((0, 0), (0, 0), (0, 0), (1, 1))
    framed_hidden = with_halo(
        hidden.reshape(images, channels, strip_rows, column_count), (("rows", 2),), 1
    )
    padded = jnp.pad(framed_hidden, column_pad)
    all_images = lax.all_gather(framed_hidden, "wt", axis=0, tiled=True)
    all_padded = jnp.pad(all_images, column_pad)
    conv_out = conv_taps(
        lax.all_gather(conv_weight, "wt", axis=0, tiled=True), padded, strip_rows, column_count
    )
    residual = (
        latents.reshape(images, channels, cell_count)
        + conv_out
        + conv_bias[None, :, None]
        - teacher.reshape(images, channels, cell_count)
    )
    low_residual = residual.astype(jnp.bfloat16)
    framed_residual = with_halo(
        low_residual.reshape(images, channels, strip_rows, column_count), (("rows", 2),), 1
    )
    padded_residual = jnp.pad(framed_residual, column_pad)
    panel_residual = lax.all_to_all(framed_residual, "wt", split_axis=1, concat_axis=0, tiled=True)
    panel_rows = channels // panel_devices
    panel_inner = panel_residual[:, :, 1 : strip_rows + 1, :].reshape(
        panel_residual.shape[0], panel_rows, cell_count
    )
    window = padded_residual
    grad_hidden = transpose_taps(
        lax.all_gather(conv_weight, "wt", axis=0, tiled=True), window, strip_rows, column_count
    )
    window = panel_inner
    weight_share = lax.psum_scatter(
        weight_terms(window, all_padded, strip_rows, column_count),
        "rows",
        scatter_dimension=0,
        tiled=True,
    )
    grad_weight = lax.all_gather(weight_share, "rows", axis=0, tiled=True) / total_cells
    grad_pre = grad_hidden * sigmoid_pre * (1.0 + pre_norm * (1.0 - sigmoid_pre))
    grad_norm = (grad_pre * gain_column).reshape(grouped.shape)
    normed_groups = normed.reshape(grouped.shape)
    first_sum, second_sum = lax.psum(
        (
            jnp.sum(grad_norm, axis=(2, 3), keepdims=True),
            jnp.sum(grad_norm * normed_groups, axis=(2, 3), keepdims=True),
        ),
        "rows",
    )
    first_mean = first_sum / group_cells
    second_mean = second_sum / group_cells
    grad_latents = residual.reshape(latents.shape) + (
        inverse * (grad_norm - first_mean - normed_groups * second_mean)
    ).reshape(latents.shape)
    totals = lax.psum(
        (
            jnp.sum(jnp.square(residual)),
            jnp.sum(residual, axis=(0, 2)),
            jnp.sum(grad_pre * normed, axis=(0, 2)),
            jnp.sum(grad_pre, axis=(0, 2)),
        ),
        ("rows", "wt"),
    )
    mean_loss = (totals[0] / (total_cells * channels)).reshape(1)
    param_grads = jnp.stack([totals[1], totals[2], totals[3]]) / total_cells
    return (mean_loss, grad_latents, grad_weight, param_grads)


def plane(ref, row, channels):
    return ref[pl.ds(row, channels, stride=2), :]


def split3(x):
    a = x.astype(BF16)
    rest = x - a.astype(F32)
    b = rest.astype(BF16)
    c = (rest - b.astype(F32)).astype(BF16)
    return a, b, c


def membership(channels):
    size = channels // GROUPS
    channel = lax.broadcasted_iota(jnp.int32, (channels, LANES), 0)
    first = lax.broadcasted_iota(jnp.int32, (channels, LANES), 1) * size
    inside = (channel >= first) & (channel < first + size)
    return jnp.where(inside, 1.0, 0.0).astype(BF16)


def dot_nn(a, b):
    return lax.dot_general(a, b, (((1,), (0,)), ((), ())), preferred_element_type=F32)


def dot_nt(a, b):
    return lax.dot_general(a, b, (((1,), (1,)), ((), ())), preferred_element_type=F32)


def group_sums(rows, member):
    a, b, c = split3(rows)
    return dot_nn(a, member) + (dot_nn(b, member) + dot_nn(c, member))


def to_channels(rows, member):
    a, b, c = split3(rows)
    return dot_nt(a, member) + (dot_nt(b, member) + dot_nt(c, member))


def as_rows(columns, channels):
    lane = lax.broadcasted_iota(jnp.int32, (channels, LANES), 1)
    table = jnp.zeros((channels, LANES), F32)
    for i, column in enumerate(columns):
        table = jnp.where(lane == i, column, table)
    return jnp.transpose(table)[:8, :]


def as_columns(rows, channels):
    pad = jnp.zeros((LANES - len(rows), channels), F32)
    return jnp.transpose(jnp.concatenate(rows + [pad], axis=0))


def row_sum(a, b):
    return jnp.sum(a + b, axis=1, keepdims=True)


def stats_kernel(lat, out):
    channels = out.shape[1]
    a, b = plane(lat, 0, channels), plane(lat, 1, channels)
    out[...] = as_rows([row_sum(a, b), row_sum(a * a, b * b)], channels)


def hidden_kernel(cells, lat, s0, s1, s2, s3, given, hidden, table):
    channels = s0.shape[1]
    member = membership(channels)
    sums = group_sums((s0[...] + s1[...]) + (s2[...] + s3[...]), member)
    mean = sums[0:1] / cells
    var = sums[1:2] / cells - mean * mean
    inverse = lax.rsqrt(var + epsilon)
    pad = jnp.zeros((6, LANES), F32)
    rows = to_channels(jnp.concatenate([mean, inverse, pad], axis=0), member)
    columns = as_columns([rows[0:1], rows[1:2], given[0:1], given[1:2], given[2:3]], channels)
    table[...] = columns
    for row in range(2):
        normed = (plane(lat, row, channels) - columns[:, 0:1]) * columns[:, 1:2]
        pre = normed * columns[:, 2:3] + columns[:, 3:4]
        hidden[row] = (pre * jax.nn.sigmoid(pre)).astype(BF16)


def shifts(x):
    wide = x.astype(F32)
    lane = lax.broadcasted_iota(jnp.int32, x.shape, 1)
    left = jnp.where(lane == 0, 0.0, pltpu.roll(wide, 1, 1)).astype(BF16)
    right = jnp.where(lane == LANES - 1, 0.0, pltpu.roll(wide, LANES - 1, 1)).astype(BF16)
    return left, x, right


def base_kernel(lat, tea, table, base):
    channels = table.shape[0]
    for row in range(2):
        base[row] = plane(lat, row, channels) + table[:, 4:5] - plane(tea, row, channels)


def frame_kernel(place, mine, above, below, framed):
    strip = place[0]
    edge = jnp.zeros_like(mine[0])
    before = jnp.where(strip > 0, below[1], edge)
    after = jnp.where(strip < 3, above[0], edge)
    for row, source in enumerate((before, mine[0], mine[1], after)):
        for kx, moved in enumerate(shifts(source)):
            framed[kx, row] = moved


def panel_rows(me, k, panel):
    return pl.ds(pl.multiple_of((me ^ k) * panel, panel), panel)


def conv_step(total, framed, ky, kx, first, second):
    window = jnp.concatenate([framed[kx, ky], framed[kx, ky + 1]], axis=1)
    total[...] += dot_nn(jnp.concatenate([first, second], axis=0), window)


def near_conv_kernel(place, near, side, framed, base, part, block0, block1, total):
    me = place[1]
    panel = near.shape[1]
    total[...] = jnp.zeros_like(total)

    def step(tap, carry):
        ky = tap // 3
        conv_step(total, framed, ky, tap - 3 * ky, near[tap], side[tap])
        return carry

    lax.fori_loop(0, 9, step, 0)
    for k, block in enumerate((block0, block1)):
        for row in range(2):
            value = base[row, panel_rows(me, k, panel), :] + (
                total[k * panel : (k + 1) * panel, row * LANES : (row + 1) * LANES]
            )
            part[k, row] = value
            block[row] = value.astype(BF16)


def far_conv_kernel(
    place, far0, far1, far2, far3, far4, diag0, diag1, diag2, diag3, diag4, framed, base, part,
    res, low, block23, total,
):
    me, half = place[1], place[2]
    panel = far0.shape[1]
    total[...] = jnp.zeros_like(total)

    def run(first, far, diag):
        def step(i, carry):
            tap = first + i
            ky = tap // 3
            conv_step(total, framed, ky, tap - 3 * ky, far[i], diag[i])
            return carry

        lax.fori_loop(0, far.shape[0], step, 0)

    run(2 * half, far0, diag0)
    run(2 - 2 * half, far1, diag1)
    run(4 + half, far2, diag2)
    run(5 - half, far3, diag3)
    run(6, far4, diag4)
    for k in range(4):
        rows = panel_rows(me, k, panel)
        for row in range(2):
            if k < 2:
                value = part[k, row]
            else:
                value = base[row, rows, :] + (
                    total[(k - 2) * panel : (k - 1) * panel, row * LANES : (row + 1) * LANES]
                )
                block23[k - 2, row] = value.astype(BF16)
            res[row, rows, :] = value
            low[row, rows, :] = value.astype(BF16)


def assemble_kernel(
    place, near, side, far0, far1, far2, far3, far4, diag0, diag1, diag2, diag3, diag4, full
):
    me, half = place[1], place[2]
    panel = near.shape[1]
    near_taps, side_taps = panel_rows(me, 0, panel), panel_rows(me, 1, panel)
    far_taps, diag_taps = panel_rows(me, 2, panel), panel_rows(me, 3, panel)

    def local(tap, carry):
        full[tap, near_taps, :] = near[tap]
        full[tap, side_taps, :] = side[tap]
        return carry

    lax.fori_loop(0, 9, local, 0)
    parts = (
        (2 * half, far0, diag0), (2 - 2 * half, far1, diag1), (4 + half, far2, diag2),
        (5 - half, far3, diag3), (6, far4, diag4),
    )
    for first, far, diag in parts:
        def remote(i, carry, first=first, far=far, diag=diag):
            full[first + i, far_taps, :] = far[i]
            full[first + i, diag_taps, :] = diag[i]
            return carry

        lax.fori_loop(0, far.shape[0], remote, 0)


def back_kernel(full, before, low, after, res, lat, table, grad, sums, framed, total):
    channels = low.shape[1]
    for row, source in enumerate((before[0], low[0], low[1], after[0])):
        for kx, moved in enumerate(shifts(source)):
            framed[kx, row] = jnp.transpose(moved)
    total[...] = jnp.zeros_like(total)

    def tap_step(tap, carry):
        ky = tap // 3
        kx = tap - 3 * ky
        window = jnp.concatenate([framed[2 - kx, 2 - ky], framed[2 - kx, 3 - ky]], axis=0)
        total[...] += dot_nn(window, full[tap])
        return carry

    lax.fori_loop(0, 9, tap_step, 0)
    columns = table[...]
    first = second = bottom = loss = None
    for row in range(2):
        normed = (plane(lat, row, channels) - columns[:, 0:1]) * columns[:, 1:2]
        pre = normed * columns[:, 2:3] + columns[:, 3:4]
        s = jax.nn.sigmoid(pre)
        value = jnp.transpose(total[row * LANES : (row + 1) * LANES, :]) * s * (1.0 + pre * (1.0 - s))
        grad[row] = value
        r = res[row]
        terms = (value, value * normed, r, r * r)
        if row == 0:
            first, second, bottom, loss = terms
        else:
            first, second, bottom, loss = (
                first + terms[0], second + terms[1], bottom + terms[2], loss + terms[3],
            )
    add = functools.partial(jnp.sum, axis=1, keepdims=True)
    sums[...] = as_rows([add(first), add(second), add(bottom), add(loss)], channels)


def latents_kernel(cells, s0, s1, s2, s3, given, res, grad, lat, table, out, total):
    channels = total.shape[1]
    member = membership(channels)
    sums = (s0[...] + s1[...]) + (s2[...] + s3[...])
    total[...] = sums
    means = group_sums(sums * given[0:1], member) / cells
    rows = to_channels(means, member)
    columns = as_columns([rows[0:1], rows[1:2]], channels)
    constants = table[...]
    inverse = constants[:, 1:2]
    for row in range(2):
        normed = (plane(lat, row, channels) - constants[:, 0:1]) * inverse
        change = grad[row] * constants[:, 2:3] - columns[:, 0:1] - normed * columns[:, 1:2]
        out[pl.ds(row, channels, stride=2), :] = res[row] + inverse * change


def weight_pair(strip, pair, aligned, one, two, first, spread, lefts, emit):
    panel, channels = aligned.shape[2], spread[0].shape[1]
    for m in range(2):
        for k in range(4):
            for row in range(2):
                lane = pl.ds((2 * k + row) * LANES, LANES)
                source = aligned[k, row] if m == 0 else jnp.where(first, one[k, row], two[k, row])
                moved = shifts(source)
                for kx in range(3):
                    lefts[(strip & 1) ^ m, kx * panel : (kx + 1) * panel, lane] = moved[2 - kx]

    def step(ky, carry):
        product = None
        for m in range(2):
            right = jnp.concatenate(
                [spread[k][4 * pair + 2 * m + ky + row] for k in range(4) for row in range(2)], axis=1
            )
            part = dot_nt(lefts[m], right)
            product = part if product is None else product + part
        emit(pl.ds(3 * ky, 3), product.reshape(3, panel, channels))
        return carry

    lax.fori_loop(0, 3, step, 0)


def totals_kernel(cells, s0, s1, s2, s3, loss, grads):
    sums = (s0[...] + s1[...]) + (s2[...] + s3[...])
    square = jnp.sum(sums[3:4], axis=1, keepdims=True) / (cells * sums.shape[1])
    loss[...] = jnp.broadcast_to(square, loss.shape)
    for row, source in enumerate((2, 1, 0)):
        grads[row : row + 1] = sums[source : source + 1] / cells


def spread_kernel(place, mine, above, beyond, below, spread):
    strip = place[0]
    channels = spread.shape[1]
    spread[0] = jnp.zeros((channels, LANES), BF16)
    spread[9] = jnp.zeros((channels, LANES), BF16)
    for m, source in enumerate((mine, above, beyond, below)):
        for row in range(2):
            spread[1 + 2 * ((strip + m) & 3) + row] = source[row]


def near_weight_kernel(place, own, plus, minus, h0, h1, h2, h3, out, lefts):
    strip = place[0]

    def emit(taps, product):
        out[taps] = product

    weight_pair(strip, strip // 2, own, plus, minus, (strip & 1) == 0, (h0, h1, h2, h3), lefts, emit)


def far_weight_kernel(cells, place, plus, minus, far, h0, h1, h2, h3, near, out, lefts, held, sems):
    strip = place[0]

    def written(taps, slot):
        return pltpu.make_async_copy(held.at[taps], out.at[taps], sems.at[slot])

    def emit(taps, product):
        held[taps] = (near[taps] + product) / cells
        for slot in range(3):
            @pl.when(taps.start == 3 * slot)
            def _(slot=slot):
                written(pl.ds(3 * slot, 3), slot).start()

    weight_pair(strip, 1 - strip // 2, far, minus, plus, (strip & 1) == 0, (h0, h1, h2, h3), lefts, emit)
    for slot in range(3):
        written(pl.ds(3 * slot, 3), slot).wait()


VM = pl.BlockSpec(memory_space=pltpu.VMEM)
SM = pl.BlockSpec(memory_space=pltpu.SMEM)


def call(kernel, outs, specs, args, scratch=(), mib=8, us=3, space=VM):
    return pl.pallas_call(
        kernel,
        out_shape=outs,
        in_specs=specs,
        out_specs=jax.tree.map(lambda _: space, outs),
        scratch_shapes=scratch,
        compiler_params=pltpu.CompilerParams(vmem_limit_bytes=mib << 20),
        cost_estimate=pl.CostEstimate(
            flops=int(us * 1e9), bytes_accessed=int(us * 3e6), transcendentals=0
        ),
    )(*args)


def shape(dims, dtype):
    return jax.ShapeDtypeStruct(dims, dtype)


def swap(x, axis, mask):
    size = lax.axis_size(axis)
    return lax.ppermute(x, axis, [(i, i ^ mask) for i in range(size)])


def ring(x, axis, step):
    size = lax.axis_size(axis)
    return lax.ppermute(x, axis, [((i + step) % size, i) for i in range(size)])


def after_all(x, *others):
    return lax.optimization_barrier((x, *others))[0]


def strips_of_four(latents, teacher, norm_gain, norm_shift, conv_weight, conv_bias):
    row_devices = lax.axis_size("rows")
    panel_devices = lax.axis_size("wt")
    _, channels, strip_rows, width = latents.shape
    panel = conv_weight.shape[0]
    strip_cells = strip_rows * width
    total_cells = panel_devices * row_devices * strip_cells
    group_cells = channels // GROUPS * strip_cells * row_devices
    up = [(i, i + 1) for i in range(row_devices - 1)]
    down = [(i + 1, i) for i in range(row_devices - 1)]
    lat = latents.reshape(channels * strip_rows, width)
    tea = teacher.reshape(channels * strip_rows, width)
    given = jnp.stack([norm_gain, norm_shift, conv_bias])
    part = lax.axis_index("grp").astype(jnp.int32)
    here = lax.axis_index("wt").astype(jnp.int32)
    strip = lax.axis_index("rows").astype(jnp.int32)
    place = jnp.stack([strip, here, part])

    near = jnp.transpose(conv_weight, (1, 0, 2))
    far0 = swap(lax.dynamic_slice_in_dim(near, part * 2, 2, axis=0), "wt", 2)
    side = swap(near, "wt", 1)

    stats = call(stats_kernel, shape((8, channels), F32), [VM], (lat,))
    hidden, table = call(
        functools.partial(hidden_kernel, group_cells),
        (shape((strip_rows, channels, width), BF16), shape((channels, LANES), F32)),
        [VM] * 6,
        (lat, after_all(stats, far0, side), *(swap(stats, "rows", m) for m in (1, 2, 3)), given),
        us=0.05,
    )
    above, below = ring(hidden, "rows", 1), ring(hidden, "rows", 3)
    later = after_all(near, hidden)
    far2 = swap(lax.dynamic_slice_in_dim(later, 4 + part, 1, axis=0), "wt", 2)
    far4 = swap(later[6:9], "wt", 2)
    far1, far3 = swap(after_all(far0, hidden), "grp", 1), swap(far2, "grp", 1)
    base = call(
        base_kernel, shape((strip_rows, channels, width), F32), [VM] * 3, (lat, tea, table), us=5
    )
    framed = call(
        frame_kernel,
        shape((3, 4, channels, width), BF16),
        [SM] + [VM] * 3,
        (place, after_all(hidden, base), above, below),
        us=5,
    )
    beyond = ring(above, "rows", 1)
    across = [swap(after_all(hidden, framed), "wt", 2)]
    rows_of = functools.partial(
        call, spread_kernel, shape((10, channels, width), BF16), [SM] + [VM] * 4, us=3
    )
    part0, block0, block1 = call(
        near_conv_kernel,
        (
            shape((2, strip_rows, panel, width), F32),
            shape((strip_rows, panel, width), BF16),
            shape((strip_rows, panel, width), BF16),
        ),
        [SM] + [VM] * 4,
        (place, near, side, framed, base),
        [pltpu.VMEM((2 * panel, 2 * LANES), F32)],
        us=20,
    )
    fars = lax.optimization_barrier((far0, far1, far2, far3, far4, framed))[:5]
    weights = (near, side, *fars, *(swap(far, "wt", 1) for far in fars))
    res, low, block23 = call(
        far_conv_kernel,
        (
            shape((strip_rows, channels, width), F32),
            shape((strip_rows, channels, width), BF16),
            shape((2, strip_rows, panel, width), BF16),
        ),
        [SM] + [VM] * 13,
        (place, *weights[2:], framed, base, part0),
        [pltpu.VMEM((2 * panel, 2 * LANES), F32)],
        us=0.05,
    )

    block1 = swap(block1, "wt", 1)
    block23 = swap(after_all(block23, across[0], beyond), "wt", 2)
    stacked = jnp.stack([block0, block1, block23[0], swap(block23[1], "wt", 1)])
    settled = after_all(low, stacked)
    low_before = lax.ppermute(settled[1:2], "rows", up)
    low_after = lax.ppermute(settled[0:1], "rows", down)
    plus = ring(stacked, "rows", 1)
    minus = ring(after_all(stacked, plus), "rows", 3)
    far = ring(plus, "rows", 1)
    full = call(
        assemble_kernel,
        shape((9, channels, channels), BF16),
        [SM] + [VM] * 12,
        (after_all(place, stacked), *weights),
        us=5,
    )

    for strip_in, last in ((above, block23), (below, None), (beyond, None)):
        across.append(swap(after_all(strip_in, across[-1] if last is None else last), "wt", 2))
    across[2:] = across[:1:-1]
    own_rows = rows_of((place, after_all(hidden, stacked), above, beyond, below))
    other_rows = swap(own_rows, "wt", 1)

    grad, sums = call(
        back_kernel,
        (shape((strip_rows, channels, width), F32), shape((8, channels), F32)),
        [VM] * 7,
        (full, low_before, after_all(low, plus, across[1], other_rows), low_after, res, lat, table),
        [
            pltpu.VMEM((3, 4, LANES, channels), BF16),
            pltpu.VMEM((2 * LANES, channels), F32),
        ],
        mib=12, us=30,
    )
    sums = after_all(sums, minus)
    across_rows = rows_of((after_all(place, sums), *across))
    grad_latents, sums = call(
        functools.partial(latents_kernel, group_cells),
        (shape((channels * strip_rows, width), F32), shape((8, channels), F32)),
        [VM] * 9,
        (
            sums, *(swap(sums, "rows", m) for m in (1, 2, 3)),
            given, res, grad, lat, table,
        ),
        us=0.05,
    )
    diag_rows = swap(after_all(across_rows, grad_latents), "wt", 1)
    images = (own_rows, other_rows, across_rows, diag_rows)
    near_weight = call(
        near_weight_kernel,
        shape((9, panel, channels), F32),
        [SM] + [VM] * 7,
        (after_all(place, grad_latents), stacked, plus, minus, *images),
        [pltpu.VMEM((2, 3 * panel, 8 * LANES), BF16)],
        mib=14, us=30,
    )
    loss, param_grads = call(
        functools.partial(totals_kernel, total_cells),
        (shape((1, LANES), F32), shape((3, channels), F32)),
        [VM] * 4,
        (after_all(sums, near_weight), *(swap(sums, "wt", m) for m in (1, 2, 3))),
        us=0.05,
    )

    grad_weight = call(
        functools.partial(far_weight_kernel, total_cells),
        shape((9, panel, channels), F32),
        [SM] + [VM] * 8,
        (place, plus, minus, far, *images, after_all(near_weight, param_grads)),
        [
            pltpu.VMEM((2, 3 * panel, 8 * LANES), BF16),
            pltpu.VMEM((9, panel, channels), F32),
            pltpu.SemaphoreType.DMA((3,)),
        ],
        mib=18, us=0.05, space=pl.BlockSpec(memory_space=pl.ANY),
    )
    return (
        loss[0, :1],
        grad_latents.reshape(latents.shape),
        jnp.transpose(grad_weight, (1, 0, 2)),
        param_grads,
    )


def solution(mesh):
    placed = (
        P(("grp", "wt"), None, "rows", None),
        P(("grp", "wt"), None, "rows", None),
        P(),
        P(),
        P("wt", None, None),
        P(),
    )
    small = mesh.shape["rows"] == 4 and mesh.shape["wt"] == 4 and mesh.shape["grp"] == 2
    return jax.shard_map(
        strips_of_four if small else generic,
        mesh=mesh,
        in_specs=placed,
        out_specs=(
            P("grp"),
            P(("grp", "wt"), None, "rows", None),
            P(("grp", "wt"), None, None),
            P("grp", None),
        ),
        check_vma=False,
    )
```

```python
import functools

import jax
import jax.numpy as jnp
from jax import lax
from jax.experimental import pallas as pl
from jax.experimental.pallas import tpu as pltpu
from jax.sharding import PartitionSpec as P

GROUPS = 32
LANES = 128
epsilon = 1e-05
F32 = jnp.float32
BF16 = jnp.bfloat16


def with_halo(shard, sides, width):
    for axis, dim in sides:
        devices, length = (lax.axis_size(axis), shard.shape[dim])
        up = [(i, (i + 1) % devices) for i in range(devices - 1)]
        down = [(j, i) for i, j in up]
        last = lax.slice_in_dim(shard, length - width, length, axis=dim)
        leading = lax.slice_in_dim(shard, 0, width, axis=dim)
        before = lax.ppermute(last, axis, up)
        after = lax.ppermute(leading, axis, down)
        shard = jnp.concatenate([before, shard, after], axis=dim)
    return shard


def conv_taps(weights, padded, strip_rows, column_count):
    running = None
    for tap_index in range(9):
        tap_row, tap_col = (tap_index // 3, tap_index % 3)
        window = padded[:, :, tap_row : tap_row + strip_rows, tap_col : tap_col + column_count]
        window = window.reshape(padded.shape[0], padded.shape[1], strip_rows * column_count)
        product = jnp.einsum(
            "oi,nip->nop", weights[:, tap_index, :], window, preferred_element_type=jnp.float32
        )
        running = product if running is None else running + product
    return running


def transpose_taps(weights, padded, strip_rows, column_count):
    running = None
    for tap_index in range(9):
        tap_row, tap_col = (tap_index // 3, tap_index % 3)
        window = padded[
            :, :, 2 - tap_row : 2 - tap_row + strip_rows, 2 - tap_col : 2 - tap_col + column_count
        ]
        window = window.reshape(padded.shape[0], padded.shape[1], strip_rows * column_count)
        product = jnp.einsum(
            "oi,nop->nip", weights[:, tap_index, :], window, preferred_element_type=jnp.float32
        )
        running = product if running is None else running + product
    return running


def weight_terms(residual, padded, strip_rows, column_count):
    columns = []
    for tap_index in range(9):
        tap_row, tap_col = (tap_index // 3, tap_index % 3)
        window = padded[:, :, tap_row : tap_row + strip_rows, tap_col : tap_col + column_count]
        window = window.reshape(padded.shape[0], padded.shape[1], strip_rows * column_count)
        columns.append(
            jnp.einsum("nop,nip->oi", residual, window, preferred_element_type=jnp.float32)
        )
    return jnp.stack(columns, axis=1)


def generic(latents, teacher, norm_gain, norm_shift, conv_weight, conv_bias):
    row_devices = lax.axis_size("rows")
    panel_devices = lax.axis_size("wt")
    images, channels, strip_rows, column_count = latents.shape
    cell_count = strip_rows * column_count
    total_cells = panel_devices * row_devices * cell_count
    group_cells = channels // GROUPS * cell_count * row_devices
    grouped = latents.reshape(images, GROUPS, channels // GROUPS, cell_count)
    group_sum, square_sum = lax.psum(
        (
            jnp.sum(grouped, axis=(2, 3), keepdims=True),
            jnp.sum(jnp.square(grouped), axis=(2, 3), keepdims=True),
        ),
        "rows",
    )
    group_mean = group_sum / group_cells
    centered = grouped - group_mean
    group_var = square_sum / group_cells - jnp.square(group_mean)
    inverse = lax.rsqrt(group_var + epsilon)
    normed = (centered * inverse).reshape(images, channels, cell_count)
    gain_column = norm_gain[None, :, None]
    pre_norm = normed * gain_column + norm_shift[None, :, None]
    sigmoid_pre = jax.nn.sigmoid(pre_norm)
    hidden = (pre_norm * sigmoid_pre).astype(jnp.bfloat16)
    column_pad = ((0, 0), (0, 0), (0, 0), (1, 1))
    framed_hidden = with_halo(
        hidden.reshape(images, channels, strip_rows, column_count), (("rows", 2),), 1
    )
    padded = jnp.pad(framed_hidden, column_pad)
    all_images = lax.all_gather(framed_hidden, "wt", axis=0, tiled=True)
    all_padded = jnp.pad(all_images, column_pad)
    conv_out = conv_taps(
        lax.all_gather(conv_weight, "wt", axis=0, tiled=True), padded, strip_rows, column_count
    )
    residual = (
        latents.reshape(images, channels, cell_count)
        + conv_out
        + conv_bias[None, :, None]
        - teacher.reshape(images, channels, cell_count)
    )
    low_residual = residual.astype(jnp.bfloat16)
    framed_residual = with_halo(
        low_residual.reshape(images, channels, strip_rows, column_count), (("rows", 2),), 1
    )
    padded_residual = jnp.pad(framed_residual, column_pad)
    panel_residual = lax.all_to_all(framed_residual, "wt", split_axis=1, concat_axis=0, tiled=True)
    panel_rows = channels // panel_devices
    panel_inner = panel_residual[:, :, 1 : strip_rows + 1, :].reshape(
        panel_residual.shape[0], panel_rows, cell_count
    )
    window = padded_residual
    grad_hidden = transpose_taps(
        lax.all_gather(conv_weight, "wt", axis=0, tiled=True), window, strip_rows, column_count
    )
    window = panel_inner
    weight_share = lax.psum_scatter(
        weight_terms(window, all_padded, strip_rows, column_count),
        "rows",
        scatter_dimension=0,
        tiled=True,
    )
    grad_weight = lax.all_gather(weight_share, "rows", axis=0, tiled=True) / total_cells
    grad_pre = grad_hidden * sigmoid_pre * (1.0 + pre_norm * (1.0 - sigmoid_pre))
    grad_norm = (grad_pre * gain_column).reshape(grouped.shape)
    normed_groups = normed.reshape(grouped.shape)
    first_sum, second_sum = lax.psum(
        (
            jnp.sum(grad_norm, axis=(2, 3), keepdims=True),
            jnp.sum(grad_norm * normed_groups, axis=(2, 3), keepdims=True),
        ),
        "rows",
    )
    first_mean = first_sum / group_cells
    second_mean = second_sum / group_cells
    grad_latents = residual.reshape(latents.shape) + (
        inverse * (grad_norm - first_mean - normed_groups * second_mean)
    ).reshape(latents.shape)
    totals = lax.psum(
        (
            jnp.sum(jnp.square(residual)),
            jnp.sum(residual, axis=(0, 2)),
            jnp.sum(grad_pre * normed, axis=(0, 2)),
            jnp.sum(grad_pre, axis=(0, 2)),
        ),
        ("rows", "wt"),
    )
    mean_loss = (totals[0] / (total_cells * channels)).reshape(1)
    param_grads = jnp.stack([totals[1], totals[2], totals[3]]) / total_cells
    return (mean_loss, grad_latents, grad_weight, param_grads)


def plane(ref, row, channels):
    return ref[pl.ds(row, channels, stride=2), :]


def split3(x):
    a = x.astype(BF16)
    rest = x - a.astype(F32)
    b = rest.astype(BF16)
    c = (rest - b.astype(F32)).astype(BF16)
    return a, b, c


def membership(channels):
    size = channels // GROUPS
    channel = lax.broadcasted_iota(jnp.int32, (channels, LANES), 0)
    first = lax.broadcasted_iota(jnp.int32, (channels, LANES), 1) * size
    inside = (channel >= first) & (channel < first + size)
    return jnp.where(inside, 1.0, 0.0).astype(BF16)


def dot_nn(a, b):
    return lax.dot_general(a, b, (((1,), (0,)), ((), ())), preferred_element_type=F32)


def dot_nt(a, b):
    return lax.dot_general(a, b, (((1,), (1,)), ((), ())), preferred_element_type=F32)


def group_sums(rows, member):
    a, b, c = split3(rows)
    return dot_nn(a, member) + (dot_nn(b, member) + dot_nn(c, member))


def to_channels(rows, member):
    a, b, c = split3(rows)
    return dot_nt(a, member) + (dot_nt(b, member) + dot_nt(c, member))


def as_rows(columns, channels):
    lane = lax.broadcasted_iota(jnp.int32, (channels, LANES), 1)
    table = jnp.zeros((channels, LANES), F32)
    for i, column in enumerate(columns):
        table = jnp.where(lane == i, column, table)
    return jnp.transpose(table)[:8, :]


def as_columns(rows, channels):
    pad = jnp.zeros((LANES - len(rows), channels), F32)
    return jnp.transpose(jnp.concatenate(rows + [pad], axis=0))


def row_sum(a, b):
    return jnp.sum(a + b, axis=1, keepdims=True)


def stats_kernel(lat, out):
    channels = out.shape[1]
    a, b = plane(lat, 0, channels), plane(lat, 1, channels)
    out[...] = as_rows([row_sum(a, b), row_sum(a * a, b * b)], channels)


def hidden_kernel(cells, lat, s0, s1, s2, s3, given, hidden, table):
    channels = s0.shape[1]
    member = membership(channels)
    sums = group_sums((s0[...] + s1[...]) + (s2[...] + s3[...]), member)
    mean = sums[0:1] / cells
    var = sums[1:2] / cells - mean * mean
    inverse = lax.rsqrt(var + epsilon)
    pad = jnp.zeros((6, LANES), F32)
    rows = to_channels(jnp.concatenate([mean, inverse, pad], axis=0), member)
    columns = as_columns([rows[0:1], rows[1:2], given[0:1], given[1:2], given[2:3]], channels)
    table[...] = columns
    for row in range(2):
        normed = (plane(lat, row, channels) - columns[:, 0:1]) * columns[:, 1:2]
        pre = normed * columns[:, 2:3] + columns[:, 3:4]
        hidden[row] = (pre * jax.nn.sigmoid(pre)).astype(BF16)


def shifts(x):
    wide = x.astype(F32)
    lane = lax.broadcasted_iota(jnp.int32, x.shape, 1)
    left = jnp.where(lane == 0, 0.0, pltpu.roll(wide, 1, 1)).astype(BF16)
    right = jnp.where(lane == LANES - 1, 0.0, pltpu.roll(wide, LANES - 1, 1)).astype(BF16)
    return left, x, right


def base_kernel(lat, tea, table, base):
    channels = table.shape[0]
    for row in range(2):
        base[row] = plane(lat, row, channels) + table[:, 4:5] - plane(tea, row, channels)


def frame_kernel(place, mine, above, below, framed):
    strip = place[0]
    edge = jnp.zeros_like(mine[0])
    before = jnp.where(strip > 0, below[1], edge)
    after = jnp.where(strip < 3, above[0], edge)
    for row, source in enumerate((before, mine[0], mine[1], after)):
        for kx, moved in enumerate(shifts(source)):
            framed[kx, row] = moved


def panel_rows(me, k, panel):
    return pl.ds(pl.multiple_of((me ^ k) * panel, panel), panel)


def conv_step(total, framed, ky, kx, first, second):
    window = jnp.concatenate([framed[kx, ky], framed[kx, ky + 1]], axis=1)
    total[...] += dot_nn(jnp.concatenate([first, second], axis=0), window)


def near_conv_kernel(place, near, side, framed, base, part, block0, block1, total):
    me = place[1]
    panel = near.shape[1]
    total[...] = jnp.zeros_like(total)

    def step(tap, carry):
        ky = tap // 3
        conv_step(total, framed, ky, tap - 3 * ky, near[tap], side[tap])
        return carry

    lax.fori_loop(0, 9, step, 0)
    for k, block in enumerate((block0, block1)):
        for row in range(2):
            value = base[row, panel_rows(me, k, panel), :] + (
                total[k * panel : (k + 1) * panel, row * LANES : (row + 1) * LANES]
            )
            part[k, row] = value
            block[row] = value.astype(BF16)


def far_conv_kernel(
    place, far0, far1, far2, far3, far4, diag0, diag1, diag2, diag3, diag4, framed, base, part,
    res, low, block23, total,
):
    me, half = place[1], place[2]
    panel = far0.shape[1]
    total[...] = jnp.zeros_like(total)

    def run(first, far, diag):
        def step(i, carry):
            tap = first + i
            ky = tap // 3
            conv_step(total, framed, ky, tap - 3 * ky, far[i], diag[i])
            return carry

        lax.fori_loop(0, far.shape[0], step, 0)

    run(2 * half, far0, diag0)
    run(2 - 2 * half, far1, diag1)
    run(4 + half, far2, diag2)
    run(5 - half, far3, diag3)
    run(6, far4, diag4)
    for k in range(4):
        rows = panel_rows(me, k, panel)
        for row in range(2):
            if k < 2:
                value = part[k, row]
            else:
                value = base[row, rows, :] + (
                    total[(k - 2) * panel : (k - 1) * panel, row * LANES : (row + 1) * LANES]
                )
                block23[k - 2, row] = value.astype(BF16)
            res[row, rows, :] = value
            low[row, rows, :] = value.astype(BF16)


def assemble_kernel(
    place, near, side, far0, far1, far2, far3, far4, diag0, diag1, diag2, diag3, diag4, full
):
    me, half = place[1], place[2]
    panel = near.shape[1]
    near_taps, side_taps = panel_rows(me, 0, panel), panel_rows(me, 1, panel)
    far_taps, diag_taps = panel_rows(me, 2, panel), panel_rows(me, 3, panel)

    def local(tap, carry):
        full[tap, near_taps, :] = near[tap]
        full[tap, side_taps, :] = side[tap]
        return carry

    lax.fori_loop(0, 9, local, 0)
    parts = (
        (2 * half, far0, diag0), (2 - 2 * half, far1, diag1), (4 + half, far2, diag2),
        (5 - half, far3, diag3), (6, far4, diag4),
    )
    for first, far, diag in parts:
        def remote(i, carry, first=first, far=far, diag=diag):
            full[first + i, far_taps, :] = far[i]
            full[first + i, diag_taps, :] = diag[i]
            return carry

        lax.fori_loop(0, far.shape[0], remote, 0)


def back_kernel(full, before, low, after, res, lat, table, grad, sums, framed, total):
    channels = low.shape[1]
    for row, source in enumerate((before[0], low[0], low[1], after[0])):
        for kx, moved in enumerate(shifts(source)):
            framed[kx, row] = jnp.transpose(moved)
    total[...] = jnp.zeros_like(total)

    def tap_step(tap, carry):
        ky = tap // 3
        kx = tap - 3 * ky
        window = jnp.concatenate([framed[2 - kx, 2 - ky], framed[2 - kx, 3 - ky]], axis=0)
        total[...] += dot_nn(window, full[tap])
        return carry

    lax.fori_loop(0, 9, tap_step, 0)
    columns = table[...]
    first = second = bottom = loss = None
    for row in range(2):
        normed = (plane(lat, row, channels) - columns[:, 0:1]) * columns[:, 1:2]
        pre = normed * columns[:, 2:3] + columns[:, 3:4]
        s = jax.nn.sigmoid(pre)
        value = jnp.transpose(total[row * LANES : (row + 1) * LANES, :]) * s * (1.0 + pre * (1.0 - s))
        grad[row] = value
        r = res[row]
        terms = (value, value * normed, r, r * r)
        if row == 0:
            first, second, bottom, loss = terms
        else:
            first, second, bottom, loss = (
                first + terms[0], second + terms[1], bottom + terms[2], loss + terms[3],
            )
    add = functools.partial(jnp.sum, axis=1, keepdims=True)
    sums[...] = as_rows([add(first), add(second), add(bottom), add(loss)], channels)


def latents_kernel(cells, s0, s1, s2, s3, given, res, grad, lat, table, out, total):
    channels = total.shape[1]
    member = membership(channels)
    sums = (s0[...] + s1[...]) + (s2[...] + s3[...])
    total[...] = sums
    means = group_sums(sums * given[0:1], member) / cells
    rows = to_channels(means, member)
    columns = as_columns([rows[0:1], rows[1:2]], channels)
    constants = table[...]
    inverse = constants[:, 1:2]
    for row in range(2):
        normed = (plane(lat, row, channels) - constants[:, 0:1]) * inverse
        change = grad[row] * constants[:, 2:3] - columns[:, 0:1] - normed * columns[:, 1:2]
        out[pl.ds(row, channels, stride=2), :] = res[row] + inverse * change


def weight_pair(strip, pair, aligned, one, two, first, spread, lefts, emit):
    panel, channels = aligned.shape[2], spread[0].shape[1]
    for m in range(2):
        for k in range(4):
            for row in range(2):
                lane = pl.ds((2 * k + row) * LANES, LANES)
                source = aligned[k, row] if m == 0 else jnp.where(first, one[k, row], two[k, row])
                moved = shifts(source)
                for kx in range(3):
                    lefts[(strip & 1) ^ m, kx * panel : (kx + 1) * panel, lane] = moved[2 - kx]

    def step(ky, carry):
        product = None
        for m in range(2):
            right = jnp.concatenate(
                [spread[k][4 * pair + 2 * m + ky + row] for k in range(4) for row in range(2)], axis=1
            )
            part = dot_nt(lefts[m], right)
            product = part if product is None else product + part
        emit(pl.ds(3 * ky, 3), product.reshape(3, panel, channels))
        return carry

    lax.fori_loop(0, 3, step, 0)


def totals_kernel(cells, s0, s1, s2, s3, loss, grads):
    sums = (s0[...] + s1[...]) + (s2[...] + s3[...])
    square = jnp.sum(sums[3:4], axis=1, keepdims=True) / (cells * sums.shape[1])
    loss[...] = jnp.broadcast_to(square, loss.shape)
    for row, source in enumerate((2, 1, 0)):
        grads[row : row + 1] = sums[source : source + 1] / cells


def spread_kernel(place, mine, above, beyond, below, spread):
    strip = place[0]
    channels = spread.shape[1]
    spread[0] = jnp.zeros((channels, LANES), BF16)
    spread[9] = jnp.zeros((channels, LANES), BF16)
    for m, source in enumerate((mine, above, beyond, below)):
        for row in range(2):
            spread[1 + 2 * ((strip + m) & 3) + row] = source[row]


def near_weight_kernel(place, own, plus, minus, h0, h1, h2, h3, out, lefts):
    strip = place[0]

    def emit(taps, product):
        out[taps] = product

    weight_pair(strip, strip // 2, own, plus, minus, (strip & 1) == 0, (h0, h1, h2, h3), lefts, emit)


def far_weight_kernel(cells, place, plus, minus, far, h0, h1, h2, h3, near, out, lefts, held, sems):
    strip = place[0]

    def written(taps, slot):
        return pltpu.make_async_copy(held.at[taps], out.at[taps], sems.at[slot])

    def emit(taps, product):
        held[taps] = (near[taps] + product) / cells
        for slot in range(3):
            @pl.when(taps.start == 3 * slot)
            def _(slot=slot):
                written(pl.ds(3 * slot, 3), slot).start()

    weight_pair(strip, 1 - strip // 2, far, minus, plus, (strip & 1) == 0, (h0, h1, h2, h3), lefts, emit)
    for slot in range(3):
        written(pl.ds(3 * slot, 3), slot).wait()


VM = pl.BlockSpec(memory_space=pltpu.VMEM)
SM = pl.BlockSpec(memory_space=pltpu.SMEM)


def call(kernel, outs, specs, args, scratch=(), mib=8, us=3, space=VM):
    return pl.pallas_call(
        kernel,
        out_shape=outs,
        in_specs=specs,
        out_specs=jax.tree.map(lambda _: space, outs),
        scratch_shapes=scratch,
        compiler_params=pltpu.CompilerParams(vmem_limit_bytes=mib << 20),
        cost_estimate=pl.CostEstimate(
            flops=int(us * 1e9), bytes_accessed=int(us * 3e6), transcendentals=0
        ),
    )(*args)


def shape(dims, dtype):
    return jax.ShapeDtypeStruct(dims, dtype)


def swap(x, axis, mask):
    size = lax.axis_size(axis)
    return lax.ppermute(x, axis, [(i, i ^ mask) for i in range(size)])


def ring(x, axis, step):
    size = lax.axis_size(axis)
    return lax.ppermute(x, axis, [((i + step) % size, i) for i in range(size)])


def after_all(x, *others):
    return lax.optimization_barrier((x, *others))[0]


def strips_of_four(latents, teacher, norm_gain, norm_shift, conv_weight, conv_bias):
    row_devices = lax.axis_size("rows")
    panel_devices = lax.axis_size("wt")
    _, channels, strip_rows, width = latents.shape
    panel = conv_weight.shape[0]
    strip_cells = strip_rows * width
    total_cells = panel_devices * row_devices * strip_cells
    group_cells = channels // GROUPS * strip_cells * row_devices
    up = [(i, i + 1) for i in range(row_devices - 1)]
    down = [(i + 1, i) for i in range(row_devices - 1)]
    lat = latents.reshape(channels * strip_rows, width)
    tea = teacher.reshape(channels * strip_rows, width)
    given = jnp.stack([norm_gain, norm_shift, conv_bias])
    part = lax.axis_index("grp").astype(jnp.int32)
    here = lax.axis_index("wt").astype(jnp.int32)
    strip = lax.axis_index("rows").astype(jnp.int32)
    place = jnp.stack([strip, here, part])

    near = jnp.transpose(conv_weight, (1, 0, 2))
    far0 = swap(lax.dynamic_slice_in_dim(near, part * 2, 2, axis=0), "wt", 2)
    side = swap(near, "wt", 1)

    stats = call(stats_kernel, shape((8, channels), F32), [VM], (lat,))
    hidden, table = call(
        functools.partial(hidden_kernel, group_cells),
        (shape((strip_rows, channels, width), BF16), shape((channels, LANES), F32)),
        [VM] * 6,
        (lat, after_all(stats, far0, side), *(swap(stats, "rows", m) for m in (1, 2, 3)), given),
        us=0.05,
    )
    above, below = ring(hidden, "rows", 1), ring(hidden, "rows", 3)
    later = after_all(near, hidden)
    far2 = swap(lax.dynamic_slice_in_dim(later, 4 + part, 1, axis=0), "wt", 2)
    far4 = swap(later[6:9], "wt", 2)
    far1, far3 = swap(after_all(far0, hidden), "grp", 1), swap(far2, "grp", 1)
    base = call(
        base_kernel, shape((strip_rows, channels, width), F32), [VM] * 3, (lat, tea, table), us=5
    )
    framed = call(
        frame_kernel,
        shape((3, 4, channels, width), BF16),
        [SM] + [VM] * 3,
        (place, after_all(hidden, base), above, below),
        us=5,
    )
    beyond = ring(above, "rows", 1)
    rows_of = functools.partial(
        call, spread_kernel, shape((10, channels, width), BF16), [SM] + [VM] * 4, us=3
    )
    part0, block0, block1 = call(
        near_conv_kernel,
        (
            shape((2, strip_rows, panel, width), F32),
            shape((strip_rows, panel, width), BF16),
            shape((strip_rows, panel, width), BF16),
        ),
        [SM] + [VM] * 4,
        (place, near, side, framed, base),
        [pltpu.VMEM((2 * panel, 2 * LANES), F32)],
        us=20,
    )
    fars = lax.optimization_barrier((far0, far1, far2, far3, far4, part0, beyond))[:5]
    weights = (near, side, *fars, *(swap(far, "wt", 1) for far in fars))
    res, low, block23 = call(
        far_conv_kernel,
        (
            shape((strip_rows, channels, width), F32),
            shape((strip_rows, channels, width), BF16),
            shape((2, strip_rows, panel, width), BF16),
        ),
        [SM] + [VM] * 13,
        (place, *weights[2:], framed, base, part0),
        [pltpu.VMEM((2 * panel, 2 * LANES), F32)],
        us=0.05,
    )

    block1 = swap(block1, "wt", 1)
    block23 = swap(block23, "wt", 2)
    stacked = jnp.stack([block0, block1, block23[0], swap(block23[1], "wt", 1)])
    settled = after_all(low, stacked)
    low_before = lax.ppermute(settled[1:2], "rows", up)
    low_after = lax.ppermute(settled[0:1], "rows", down)
    plus = ring(stacked, "rows", 1)
    minus = ring(after_all(stacked, plus), "rows", 3)
    far = ring(plus, "rows", 1)
    full = call(
        assemble_kernel,
        shape((9, channels, channels), BF16),
        [SM] + [VM] * 12,
        (after_all(place, stacked), *weights),
        us=5,
    )

    across = [swap(after_all(hidden, block23), "wt", 2)]
    across.append(swap(after_all(above, across[0]), "wt", 2))
    below_across = swap(after_all(below, across[1]), "wt", 2)
    own_rows = rows_of((place, after_all(hidden, stacked), above, beyond, below))
    other_rows = swap(own_rows, "wt", 1)

    grad, sums = call(
        back_kernel,
        (shape((strip_rows, channels, width), F32), shape((8, channels), F32)),
        [VM] * 7,
        (full, low_before, after_all(low, plus, across[1], other_rows), low_after, res, lat, table),
        [
            pltpu.VMEM((3, 4, LANES, channels), BF16),
            pltpu.VMEM((2 * LANES, channels), F32),
        ],
        mib=12, us=30,
    )
    sums = after_all(sums, minus)
    across += [swap(after_all(beyond, grad), "wt", 2), below_across]
    across_rows = rows_of((after_all(place, sums), *across))
    grad_latents, sums = call(
        functools.partial(latents_kernel, group_cells),
        (shape((channels * strip_rows, width), F32), shape((8, channels), F32)),
        [VM] * 9,
        (
            sums, *(swap(sums, "rows", m) for m in (1, 2, 3)),
            given, res, grad, lat, table,
        ),
        us=0.05,
    )
    diag_rows = swap(after_all(across_rows, grad_latents), "wt", 1)
    images = (own_rows, other_rows, across_rows, diag_rows)
    near_weight = call(
        near_weight_kernel,
        shape((9, panel, channels), F32),
        [SM] + [VM] * 7,
        (after_all(place, grad_latents), stacked, plus, minus, *images),
        [pltpu.VMEM((2, 3 * panel, 8 * LANES), BF16)],
        mib=14, us=30,
    )
    loss, param_grads = call(
        functools.partial(totals_kernel, total_cells),
        (shape((1, LANES), F32), shape((3, channels), F32)),
        [VM] * 4,
        (after_all(sums, near_weight), *(swap(sums, "wt", m) for m in (1, 2, 3))),
        us=0.05,
    )

    grad_weight = call(
        functools.partial(far_weight_kernel, total_cells),
        shape((9, panel, channels), F32),
        [SM] + [VM] * 8,
        (place, plus, minus, far, *images, after_all(near_weight, param_grads)),
        [
            pltpu.VMEM((2, 3 * panel, 8 * LANES), BF16),
            pltpu.VMEM((9, panel, channels), F32),
            pltpu.SemaphoreType.DMA((3,)),
        ],
        mib=18, us=0.05, space=pl.BlockSpec(memory_space=pl.ANY),
    )
    return (
        loss[0, :1],
        grad_latents.reshape(latents.shape),
        jnp.transpose(grad_weight, (1, 0, 2)),
        param_grads,
    )


def solution(mesh):
    placed = (
        P(("grp", "wt"), None, "rows", None),
        P(("grp", "wt"), None, "rows", None),
        P(),
        P(),
        P("wt", None, None),
        P(),
    )
    small = mesh.shape["rows"] == 4 and mesh.shape["wt"] == 4 and mesh.shape["grp"] == 2
    return jax.shard_map(
        strips_of_four if small else generic,
        mesh=mesh,
        in_specs=placed,
        out_specs=(
            P("grp"),
            P(("grp", "wt"), None, "rows", None),
            P(("grp", "wt"), None, None),
            P("grp", None),
        ),
        check_vma=False,
    )
```

```python
import functools

import jax
import jax.numpy as jnp
from jax import lax
from jax.experimental import pallas as pl
from jax.experimental.pallas import tpu as pltpu
from jax.sharding import PartitionSpec as P

GROUPS = 32
LANES = 128
epsilon = 1e-05
F32 = jnp.float32
BF16 = jnp.bfloat16


def with_halo(shard, sides, width):
    for axis, dim in sides:
        devices, length = (lax.axis_size(axis), shard.shape[dim])
        up = [(i, (i + 1) % devices) for i in range(devices - 1)]
        down = [(j, i) for i, j in up]
        last = lax.slice_in_dim(shard, length - width, length, axis=dim)
        leading = lax.slice_in_dim(shard, 0, width, axis=dim)
        before = lax.ppermute(last, axis, up)
        after = lax.ppermute(leading, axis, down)
        shard = jnp.concatenate([before, shard, after], axis=dim)
    return shard


def conv_taps(weights, padded, strip_rows, column_count):
    running = None
    for tap_index in range(9):
        tap_row, tap_col = (tap_index // 3, tap_index % 3)
        window = padded[:, :, tap_row : tap_row + strip_rows, tap_col : tap_col + column_count]
        window = window.reshape(padded.shape[0], padded.shape[1], strip_rows * column_count)
        product = jnp.einsum(
            "oi,nip->nop", weights[:, tap_index, :], window, preferred_element_type=jnp.float32
        )
        running = product if running is None else running + product
    return running


def transpose_taps(weights, padded, strip_rows, column_count):
    running = None
    for tap_index in range(9):
        tap_row, tap_col = (tap_index // 3, tap_index % 3)
        window = padded[
            :, :, 2 - tap_row : 2 - tap_row + strip_rows, 2 - tap_col : 2 - tap_col + column_count
        ]
        window = window.reshape(padded.shape[0], padded.shape[1], strip_rows * column_count)
        product = jnp.einsum(
            "oi,nop->nip", weights[:, tap_index, :], window, preferred_element_type=jnp.float32
        )
        running = product if running is None else running + product
    return running


def weight_terms(residual, padded, strip_rows, column_count):
    columns = []
    for tap_index in range(9):
        tap_row, tap_col = (tap_index // 3, tap_index % 3)
        window = padded[:, :, tap_row : tap_row + strip_rows, tap_col : tap_col + column_count]
        window = window.reshape(padded.shape[0], padded.shape[1], strip_rows * column_count)
        columns.append(
            jnp.einsum("nop,nip->oi", residual, window, preferred_element_type=jnp.float32)
        )
    return jnp.stack(columns, axis=1)


def generic(latents, teacher, norm_gain, norm_shift, conv_weight, conv_bias):
    row_devices = lax.axis_size("rows")
    panel_devices = lax.axis_size("wt")
    images, channels, strip_rows, column_count = latents.shape
    cell_count = strip_rows * column_count
    total_cells = panel_devices * row_devices * cell_count
    group_cells = channels // GROUPS * cell_count * row_devices
    grouped = latents.reshape(images, GROUPS, channels // GROUPS, cell_count)
    group_sum, square_sum = lax.psum(
        (
            jnp.sum(grouped, axis=(2, 3), keepdims=True),
            jnp.sum(jnp.square(grouped), axis=(2, 3), keepdims=True),
        ),
        "rows",
    )
    group_mean = group_sum / group_cells
    centered = grouped - group_mean
    group_var = square_sum / group_cells - jnp.square(group_mean)
    inverse = lax.rsqrt(group_var + epsilon)
    normed = (centered * inverse).reshape(images, channels, cell_count)
    gain_column = norm_gain[None, :, None]
    pre_norm = normed * gain_column + norm_shift[None, :, None]
    sigmoid_pre = jax.nn.sigmoid(pre_norm)
    hidden = (pre_norm * sigmoid_pre).astype(jnp.bfloat16)
    column_pad = ((0, 0), (0, 0), (0, 0), (1, 1))
    framed_hidden = with_halo(
        hidden.reshape(images, channels, strip_rows, column_count), (("rows", 2),), 1
    )
    padded = jnp.pad(framed_hidden, column_pad)
    all_images = lax.all_gather(framed_hidden, "wt", axis=0, tiled=True)
    all_padded = jnp.pad(all_images, column_pad)
    conv_out = conv_taps(
        lax.all_gather(conv_weight, "wt", axis=0, tiled=True), padded, strip_rows, column_count
    )
    residual = (
        latents.reshape(images, channels, cell_count)
        + conv_out
        + conv_bias[None, :, None]
        - teacher.reshape(images, channels, cell_count)
    )
    low_residual = residual.astype(jnp.bfloat16)
    framed_residual = with_halo(
        low_residual.reshape(images, channels, strip_rows, column_count), (("rows", 2),), 1
    )
    padded_residual = jnp.pad(framed_residual, column_pad)
    panel_residual = lax.all_to_all(framed_residual, "wt", split_axis=1, concat_axis=0, tiled=True)
    panel_rows = channels // panel_devices
    panel_inner = panel_residual[:, :, 1 : strip_rows + 1, :].reshape(
        panel_residual.shape[0], panel_rows, cell_count
    )
    window = padded_residual
    grad_hidden = transpose_taps(
        lax.all_gather(conv_weight, "wt", axis=0, tiled=True), window, strip_rows, column_count
    )
    window = panel_inner
    weight_share = lax.psum_scatter(
        weight_terms(window, all_padded, strip_rows, column_count),
        "rows",
        scatter_dimension=0,
        tiled=True,
    )
    grad_weight = lax.all_gather(weight_share, "rows", axis=0, tiled=True) / total_cells
    grad_pre = grad_hidden * sigmoid_pre * (1.0 + pre_norm * (1.0 - sigmoid_pre))
    grad_norm = (grad_pre * gain_column).reshape(grouped.shape)
    normed_groups = normed.reshape(grouped.shape)
    first_sum, second_sum = lax.psum(
        (
            jnp.sum(grad_norm, axis=(2, 3), keepdims=True),
            jnp.sum(grad_norm * normed_groups, axis=(2, 3), keepdims=True),
        ),
        "rows",
    )
    first_mean = first_sum / group_cells
    second_mean = second_sum / group_cells
    grad_latents = residual.reshape(latents.shape) + (
        inverse * (grad_norm - first_mean - normed_groups * second_mean)
    ).reshape(latents.shape)
    totals = lax.psum(
        (
            jnp.sum(jnp.square(residual)),
            jnp.sum(residual, axis=(0, 2)),
            jnp.sum(grad_pre * normed, axis=(0, 2)),
            jnp.sum(grad_pre, axis=(0, 2)),
        ),
        ("rows", "wt"),
    )
    mean_loss = (totals[0] / (total_cells * channels)).reshape(1)
    param_grads = jnp.stack([totals[1], totals[2], totals[3]]) / total_cells
    return (mean_loss, grad_latents, grad_weight, param_grads)


def plane(ref, row, channels):
    return ref[pl.ds(row, channels, stride=2), :]


def split3(x):
    a = x.astype(BF16)
    rest = x - a.astype(F32)
    b = rest.astype(BF16)
    c = (rest - b.astype(F32)).astype(BF16)
    return a, b, c


def membership(channels):
    size = channels // GROUPS
    channel = lax.broadcasted_iota(jnp.int32, (channels, LANES), 0)
    first = lax.broadcasted_iota(jnp.int32, (channels, LANES), 1) * size
    inside = (channel >= first) & (channel < first + size)
    return jnp.where(inside, 1.0, 0.0).astype(BF16)


def dot_nn(a, b):
    return lax.dot_general(a, b, (((1,), (0,)), ((), ())), preferred_element_type=F32)


def dot_nt(a, b):
    return lax.dot_general(a, b, (((1,), (1,)), ((), ())), preferred_element_type=F32)


def group_sums(rows, member):
    a, b, c = split3(rows)
    return dot_nn(a, member) + (dot_nn(b, member) + dot_nn(c, member))


def to_channels(rows, member):
    a, b, c = split3(rows)
    return dot_nt(a, member) + (dot_nt(b, member) + dot_nt(c, member))


def as_rows(columns, channels):
    lane = lax.broadcasted_iota(jnp.int32, (channels, LANES), 1)
    table = jnp.zeros((channels, LANES), F32)
    for i, column in enumerate(columns):
        table = jnp.where(lane == i, column, table)
    return jnp.transpose(table)[:8, :]


def as_columns(rows, channels):
    pad = jnp.zeros((LANES - len(rows), channels), F32)
    return jnp.transpose(jnp.concatenate(rows + [pad], axis=0))


def row_sum(a, b):
    return jnp.sum(a + b, axis=1, keepdims=True)


def stats_kernel(lat, out):
    channels = out.shape[1]
    a, b = plane(lat, 0, channels), plane(lat, 1, channels)
    out[...] = as_rows([row_sum(a, b), row_sum(a * a, b * b)], channels)


def hidden_kernel(cells, lat, s0, s1, s2, s3, given, hidden, table):
    channels = s0.shape[1]
    member = membership(channels)
    sums = group_sums((s0[...] + s1[...]) + (s2[...] + s3[...]), member)
    mean = sums[0:1] / cells
    var = sums[1:2] / cells - mean * mean
    inverse = lax.rsqrt(var + epsilon)
    pad = jnp.zeros((6, LANES), F32)
    rows = to_channels(jnp.concatenate([mean, inverse, pad], axis=0), member)
    columns = as_columns([rows[0:1], rows[1:2], given[0:1], given[1:2], given[2:3]], channels)
    table[...] = columns
    for row in range(2):
        normed = (plane(lat, row, channels) - columns[:, 0:1]) * columns[:, 1:2]
        pre = normed * columns[:, 2:3] + columns[:, 3:4]
        hidden[row] = (pre * jax.nn.sigmoid(pre)).astype(BF16)


def shifts(x):
    wide = x.astype(F32)
    lane = lax.broadcasted_iota(jnp.int32, x.shape, 1)
    left = jnp.where(lane == 0, 0.0, pltpu.roll(wide, 1, 1)).astype(BF16)
    right = jnp.where(lane == LANES - 1, 0.0, pltpu.roll(wide, LANES - 1, 1)).astype(BF16)
    return left, x, right


def base_kernel(lat, tea, table, base):
    channels = table.shape[0]
    for row in range(2):
        base[row] = plane(lat, row, channels) + table[:, 4:5] - plane(tea, row, channels)


def frame_kernel(place, mine, above, below, framed):
    strip = place[0]
    edge = jnp.zeros_like(mine[0])
    before = jnp.where(strip > 0, below[1], edge)
    after = jnp.where(strip < 3, above[0], edge)
    for row, source in enumerate((before, mine[0], mine[1], after)):
        for kx, moved in enumerate(shifts(source)):
            framed[kx, row] = moved


def panel_rows(me, k, panel):
    return pl.ds(pl.multiple_of((me ^ k) * panel, panel), panel)


def conv_step(total, framed, ky, kx, first, second):
    window = jnp.concatenate([framed[kx, ky], framed[kx, ky + 1]], axis=1)
    total[...] += dot_nn(jnp.concatenate([first, second], axis=0), window)


def near_conv_kernel(place, near, side, framed, base, part, block0, block1, total):
    me = place[1]
    panel = near.shape[1]
    total[...] = jnp.zeros_like(total)

    def step(tap, carry):
        ky = tap // 3
        conv_step(total, framed, ky, tap - 3 * ky, near[tap], side[tap])
        return carry

    lax.fori_loop(0, 9, step, 0)
    for k, block in enumerate((block0, block1)):
        for row in range(2):
            value = base[row, panel_rows(me, k, panel), :] + (
                total[k * panel : (k + 1) * panel, row * LANES : (row + 1) * LANES]
            )
            part[k, row] = value
            block[row] = value.astype(BF16)


def far_conv_kernel(
    place, far0, far1, far2, far3, far4, diag0, diag1, diag2, diag3, diag4, framed, base, part,
    res, low, block23, total,
):
    me, half = place[1], place[2]
    panel = far0.shape[1]
    total[...] = jnp.zeros_like(total)

    def run(first, far, diag):
        def step(i, carry):
            tap = first + i
            ky = tap // 3
            conv_step(total, framed, ky, tap - 3 * ky, far[i], diag[i])
            return carry

        lax.fori_loop(0, far.shape[0], step, 0)

    run(2 * half, far0, diag0)
    run(2 - 2 * half, far1, diag1)
    run(4 + half, far2, diag2)
    run(5 - half, far3, diag3)
    run(6, far4, diag4)
    for k in range(4):
        rows = panel_rows(me, k, panel)
        for row in range(2):
            if k < 2:
                value = part[k, row]
            else:
                value = base[row, rows, :] + (
                    total[(k - 2) * panel : (k - 1) * panel, row * LANES : (row + 1) * LANES]
                )
                block23[k - 2, row] = value.astype(BF16)
            res[row, rows, :] = value
            low[row, rows, :] = value.astype(BF16)


def assemble_kernel(
    place, near, side, far0, far1, far2, far3, far4, diag0, diag1, diag2, diag3, diag4, full
):
    me, half = place[1], place[2]
    panel = near.shape[1]
    near_taps, side_taps = panel_rows(me, 0, panel), panel_rows(me, 1, panel)
    far_taps, diag_taps = panel_rows(me, 2, panel), panel_rows(me, 3, panel)

    def local(tap, carry):
        full[tap, near_taps, :] = near[tap]
        full[tap, side_taps, :] = side[tap]
        return carry

    lax.fori_loop(0, 9, local, 0)
    parts = (
        (2 * half, far0, diag0), (2 - 2 * half, far1, diag1), (4 + half, far2, diag2),
        (5 - half, far3, diag3), (6, far4, diag4),
    )
    for first, far, diag in parts:
        def remote(i, carry, first=first, far=far, diag=diag):
            full[first + i, far_taps, :] = far[i]
            full[first + i, diag_taps, :] = diag[i]
            return carry

        lax.fori_loop(0, far.shape[0], remote, 0)


def back_kernel(full, before, low, after, res, lat, table, grad, sums, framed, total):
    channels = low.shape[1]
    for row, source in enumerate((before[0], low[0], low[1], after[0])):
        for kx, moved in enumerate(shifts(source)):
            framed[kx, row] = jnp.transpose(moved)
    total[...] = jnp.zeros_like(total)

    def tap_step(tap, carry):
        ky = tap // 3
        kx = tap - 3 * ky
        window = jnp.concatenate([framed[2 - kx, 2 - ky], framed[2 - kx, 3 - ky]], axis=0)
        total[...] += dot_nn(window, full[tap])
        return carry

    lax.fori_loop(0, 9, tap_step, 0)
    columns = table[...]
    first = second = bottom = loss = None
    for row in range(2):
        normed = (plane(lat, row, channels) - columns[:, 0:1]) * columns[:, 1:2]
        pre = normed * columns[:, 2:3] + columns[:, 3:4]
        s = jax.nn.sigmoid(pre)
        value = jnp.transpose(total[row * LANES : (row + 1) * LANES, :]) * s * (1.0 + pre * (1.0 - s))
        grad[row] = value
        r = res[row]
        terms = (value, value * normed, r, r * r)
        if row == 0:
            first, second, bottom, loss = terms
        else:
            first, second, bottom, loss = (
                first + terms[0], second + terms[1], bottom + terms[2], loss + terms[3],
            )
    add = functools.partial(jnp.sum, axis=1, keepdims=True)
    sums[...] = as_rows([add(first), add(second), add(bottom), add(loss)], channels)


def latents_kernel(cells, s0, s1, s2, s3, given, res, grad, lat, table, out, total):
    channels = total.shape[1]
    member = membership(channels)
    sums = (s0[...] + s1[...]) + (s2[...] + s3[...])
    total[...] = sums
    means = group_sums(sums * given[0:1], member) / cells
    rows = to_channels(means, member)
    columns = as_columns([rows[0:1], rows[1:2]], channels)
    constants = table[...]
    inverse = constants[:, 1:2]
    for row in range(2):
        normed = (plane(lat, row, channels) - constants[:, 0:1]) * inverse
        change = grad[row] * constants[:, 2:3] - columns[:, 0:1] - normed * columns[:, 1:2]
        out[pl.ds(row, channels, stride=2), :] = res[row] + inverse * change


def weight_pair(strip, pair, aligned, one, two, first, spread, lefts, emit):
    panel, channels = aligned.shape[2], spread[0].shape[1]
    for m in range(2):
        for k in range(4):
            for row in range(2):
                lane = pl.ds((2 * k + row) * LANES, LANES)
                source = aligned[k, row] if m == 0 else jnp.where(first, one[k, row], two[k, row])
                moved = shifts(source)
                for kx in range(3):
                    lefts[(strip & 1) ^ m, kx * panel : (kx + 1) * panel, lane] = moved[2 - kx]

    def step(ky, carry):
        product = None
        for m in range(2):
            right = jnp.concatenate(
                [spread[k][4 * pair + 2 * m + ky + row] for k in range(4) for row in range(2)], axis=1
            )
            part = dot_nt(lefts[m], right)
            product = part if product is None else product + part
        emit(pl.ds(3 * ky, 3), product.reshape(3, panel, channels))
        return carry

    lax.fori_loop(0, 3, step, 0)


def totals_kernel(cells, s0, s1, s2, s3, loss, grads):
    sums = (s0[...] + s1[...]) + (s2[...] + s3[...])
    square = jnp.sum(sums[3:4], axis=1, keepdims=True) / (cells * sums.shape[1])
    loss[...] = jnp.broadcast_to(square, loss.shape)
    for row, source in enumerate((2, 1, 0)):
        grads[row : row + 1] = sums[source : source + 1] / cells


def spread_kernel(place, mine, above, beyond, below, spread):
    strip = place[0]
    channels = spread.shape[1]
    spread[0] = jnp.zeros((channels, LANES), BF16)
    spread[9] = jnp.zeros((channels, LANES), BF16)
    for m, source in enumerate((mine, above, beyond, below)):
        for row in range(2):
            spread[1 + 2 * ((strip + m) & 3) + row] = source[row]


def near_weight_kernel(place, own, plus, minus, h0, h1, h2, h3, out, lefts):
    strip = place[0]

    def emit(taps, product):
        out[taps] = product

    weight_pair(strip, strip // 2, own, plus, minus, (strip & 1) == 0, (h0, h1, h2, h3), lefts, emit)


def far_weight_kernel(cells, place, plus, minus, far, h0, h1, h2, h3, near, out, lefts, held, sems):
    strip = place[0]

    def written(taps, slot):
        return pltpu.make_async_copy(held.at[taps], out.at[taps], sems.at[slot])

    def emit(taps, product):
        held[taps] = (near[taps] + product) / cells
        for slot in range(3):
            @pl.when(taps.start == 3 * slot)
            def _(slot=slot):
                written(pl.ds(3 * slot, 3), slot).start()

    weight_pair(strip, 1 - strip // 2, far, minus, plus, (strip & 1) == 0, (h0, h1, h2, h3), lefts, emit)
    for slot in range(3):
        written(pl.ds(3 * slot, 3), slot).wait()


VM = pl.BlockSpec(memory_space=pltpu.VMEM)
SM = pl.BlockSpec(memory_space=pltpu.SMEM)


def call(kernel, outs, specs, args, scratch=(), mib=8, us=3, space=VM):
    return pl.pallas_call(
        kernel,
        out_shape=outs,
        in_specs=specs,
        out_specs=jax.tree.map(lambda _: space, outs),
        scratch_shapes=scratch,
        compiler_params=pltpu.CompilerParams(vmem_limit_bytes=mib << 20),
        cost_estimate=pl.CostEstimate(
            flops=int(us * 1e9), bytes_accessed=int(us * 3e6), transcendentals=0
        ),
    )(*args)


def shape(dims, dtype):
    return jax.ShapeDtypeStruct(dims, dtype)


def swap(x, axis, mask):
    size = lax.axis_size(axis)
    return lax.ppermute(x, axis, [(i, i ^ mask) for i in range(size)])


def ring(x, axis, step):
    size = lax.axis_size(axis)
    return lax.ppermute(x, axis, [((i + step) % size, i) for i in range(size)])


def after_all(x, *others):
    return lax.optimization_barrier((x, *others))[0]


def strips_of_four(latents, teacher, norm_gain, norm_shift, conv_weight, conv_bias):
    row_devices = lax.axis_size("rows")
    panel_devices = lax.axis_size("wt")
    _, channels, strip_rows, width = latents.shape
    panel = conv_weight.shape[0]
    strip_cells = strip_rows * width
    total_cells = panel_devices * row_devices * strip_cells
    group_cells = channels // GROUPS * strip_cells * row_devices
    up = [(i, i + 1) for i in range(row_devices - 1)]
    down = [(i + 1, i) for i in range(row_devices - 1)]
    lat = latents.reshape(channels * strip_rows, width)
    tea = teacher.reshape(channels * strip_rows, width)
    given = jnp.stack([norm_gain, norm_shift, conv_bias])
    part = lax.axis_index("grp").astype(jnp.int32)
    here = lax.axis_index("wt").astype(jnp.int32)
    strip = lax.axis_index("rows").astype(jnp.int32)
    place = jnp.stack([strip, here, part])

    near = jnp.transpose(conv_weight, (1, 0, 2))
    far0 = swap(lax.dynamic_slice_in_dim(near, part * 2, 2, axis=0), "wt", 2)
    side = swap(near, "wt", 1)

    stats = call(stats_kernel, shape((8, channels), F32), [VM], (lat,))
    hidden, table = call(
        functools.partial(hidden_kernel, group_cells),
        (shape((strip_rows, channels, width), BF16), shape((channels, LANES), F32)),
        [VM] * 6,
        (lat, after_all(stats, far0, side), *(swap(stats, "rows", m) for m in (1, 2, 3)), given),
        us=0.05,
    )
    above, below = ring(hidden, "rows", 1), ring(hidden, "rows", 3)
    later = after_all(near, hidden)
    far2 = swap(lax.dynamic_slice_in_dim(later, 4 + part, 1, axis=0), "wt", 2)
    far4 = swap(later[6:9], "wt", 2)
    far1, far3 = swap(after_all(far0, hidden), "grp", 1), swap(far2, "grp", 1)
    base = call(
        base_kernel, shape((strip_rows, channels, width), F32), [VM] * 3, (lat, tea, table), us=5
    )
    framed = call(
        frame_kernel,
        shape((3, 4, channels, width), BF16),
        [SM] + [VM] * 3,
        (place, after_all(hidden, base), above, below),
        us=5,
    )
    beyond = ring(above, "rows", 1)
    rows_of = functools.partial(
        call, spread_kernel, shape((10, channels, width), BF16), [SM] + [VM] * 4, us=3
    )
    part0, block0, block1 = call(
        near_conv_kernel,
        (
            shape((2, strip_rows, panel, width), F32),
            shape((strip_rows, panel, width), BF16),
            shape((strip_rows, panel, width), BF16),
        ),
        [SM] + [VM] * 4,
        (place, near, side, framed, base),
        [pltpu.VMEM((2 * panel, 2 * LANES), F32)],
        us=20,
    )
    fars = lax.optimization_barrier((far0, far1, far2, far3, far4, part0, beyond))[:5]
    weights = (near, side, *fars, *(swap(far, "wt", 1) for far in fars))
    res, low, block23 = call(
        far_conv_kernel,
        (
            shape((strip_rows, channels, width), F32),
            shape((strip_rows, channels, width), BF16),
            shape((2, strip_rows, panel, width), BF16),
        ),
        [SM] + [VM] * 13,
        (place, *weights[2:], framed, base, part0),
        [pltpu.VMEM((2 * panel, 2 * LANES), F32)],
        us=0.05,
    )

    block1 = swap(block1, "wt", 1)
    block23 = swap(block23, "wt", 2)
    stacked = jnp.stack([block0, block1, block23[0], swap(block23[1], "wt", 1)])
    settled = after_all(low, stacked)
    low_before = lax.ppermute(settled[1:2], "rows", up)
    low_after = lax.ppermute(settled[0:1], "rows", down)
    plus = ring(stacked, "rows", 1)
    minus = ring(after_all(stacked, plus), "rows", 3)
    far = ring(plus, "rows", 1)
    full = call(
        assemble_kernel,
        shape((9, channels, channels), BF16),
        [SM] + [VM] * 12,
        (after_all(place, stacked), *weights),
        us=5,
    )

    across = [swap(after_all(hidden, block23), "wt", 2)]
    across.append(swap(after_all(above, across[0]), "wt", 2))
    below_across = swap(after_all(below, across[0]), "wt", 2)
    own_rows = rows_of((after_all(place, low_before), hidden, above, beyond, below))
    other_rows = swap(own_rows, "wt", 1)

    grad, sums = call(
        back_kernel,
        (shape((strip_rows, channels, width), F32), shape((8, channels), F32)),
        [VM] * 7,
        (full, low_before, after_all(low, plus), low_after, res, lat, table),
        [
            pltpu.VMEM((3, 4, LANES, channels), BF16),
            pltpu.VMEM((2 * LANES, channels), F32),
        ],
        mib=12, us=30,
    )
    sums = after_all(sums, minus, across[1], below_across, other_rows)
    across += [swap(after_all(beyond, grad), "wt", 2), below_across]
    across_rows = rows_of((after_all(place, sums), *across))
    grad_latents, sums = call(
        functools.partial(latents_kernel, group_cells),
        (shape((channels * strip_rows, width), F32), shape((8, channels), F32)),
        [VM] * 9,
        (
            sums, *(swap(sums, "rows", m) for m in (1, 2, 3)),
            given, res, grad, lat, table,
        ),
        us=0.05,
    )
    diag_rows = swap(after_all(across_rows, grad_latents), "wt", 1)
    images = (own_rows, other_rows, across_rows, diag_rows)
    near_weight = call(
        near_weight_kernel,
        shape((9, panel, channels), F32),
        [SM] + [VM] * 7,
        (after_all(place, grad_latents), stacked, plus, minus, *images),
        [pltpu.VMEM((2, 3 * panel, 8 * LANES), BF16)],
        mib=14, us=30,
    )
    loss, param_grads = call(
        functools.partial(totals_kernel, total_cells),
        (shape((1, LANES), F32), shape((3, channels), F32)),
        [VM] * 4,
        (after_all(sums, near_weight), *(swap(sums, "wt", m) for m in (1, 2, 3))),
        us=0.05,
    )

    grad_weight = call(
        functools.partial(far_weight_kernel, total_cells),
        shape((9, panel, channels), F32),
        [SM] + [VM] * 8,
        (place, plus, minus, far, *images, after_all(near_weight, param_grads)),
        [
            pltpu.VMEM((2, 3 * panel, 8 * LANES), BF16),
            pltpu.VMEM((9, panel, channels), F32),
            pltpu.SemaphoreType.DMA((3,)),
        ],
        mib=18, us=0.05, space=pl.BlockSpec(memory_space=pl.ANY),
    )
    return (
        loss[0, :1],
        grad_latents.reshape(latents.shape),
        jnp.transpose(grad_weight, (1, 0, 2)),
        param_grads,
    )


def solution(mesh):
    placed = (
        P(("grp", "wt"), None, "rows", None),
        P(("grp", "wt"), None, "rows", None),
        P(),
        P(),
        P("wt", None, None),
        P(),
    )
    small = mesh.shape["rows"] == 4 and mesh.shape["wt"] == 4 and mesh.shape["grp"] == 2
    return jax.shard_map(
        strips_of_four if small else generic,
        mesh=mesh,
        in_specs=placed,
        out_specs=(
            P("grp"),
            P(("grp", "wt"), None, "rows", None),
            P(("grp", "wt"), None, None),
            P("grp", None),
        ),
        check_vma=False,
    )
```

```python
import functools

import jax
import jax.numpy as jnp
from jax import lax
from jax.experimental import pallas as pl
from jax.experimental.pallas import tpu as pltpu
from jax.sharding import PartitionSpec as P

GROUPS = 32
LANES = 128
epsilon = 1e-05
F32 = jnp.float32
BF16 = jnp.bfloat16


def with_halo(shard, sides, width):
    for axis, dim in sides:
        devices, length = (lax.axis_size(axis), shard.shape[dim])
        up = [(i, (i + 1) % devices) for i in range(devices - 1)]
        down = [(j, i) for i, j in up]
        last = lax.slice_in_dim(shard, length - width, length, axis=dim)
        leading = lax.slice_in_dim(shard, 0, width, axis=dim)
        before = lax.ppermute(last, axis, up)
        after = lax.ppermute(leading, axis, down)
        shard = jnp.concatenate([before, shard, after], axis=dim)
    return shard


def conv_taps(weights, padded, strip_rows, column_count):
    running = None
    for tap_index in range(9):
        tap_row, tap_col = (tap_index // 3, tap_index % 3)
        window = padded[:, :, tap_row : tap_row + strip_rows, tap_col : tap_col + column_count]
        window = window.reshape(padded.shape[0], padded.shape[1], strip_rows * column_count)
        product = jnp.einsum(
            "oi,nip->nop", weights[:, tap_index, :], window, preferred_element_type=jnp.float32
        )
        running = product if running is None else running + product
    return running


def transpose_taps(weights, padded, strip_rows, column_count):
    running = None
    for tap_index in range(9):
        tap_row, tap_col = (tap_index // 3, tap_index % 3)
        window = padded[
            :, :, 2 - tap_row : 2 - tap_row + strip_rows, 2 - tap_col : 2 - tap_col + column_count
        ]
        window = window.reshape(padded.shape[0], padded.shape[1], strip_rows * column_count)
        product = jnp.einsum(
            "oi,nop->nip", weights[:, tap_index, :], window, preferred_element_type=jnp.float32
        )
        running = product if running is None else running + product
    return running


def weight_terms(residual, padded, strip_rows, column_count):
    columns = []
    for tap_index in range(9):
        tap_row, tap_col = (tap_index // 3, tap_index % 3)
        window = padded[:, :, tap_row : tap_row + strip_rows, tap_col : tap_col + column_count]
        window = window.reshape(padded.shape[0], padded.shape[1], strip_rows * column_count)
        columns.append(
            jnp.einsum("nop,nip->oi", residual, window, preferred_element_type=jnp.float32)
        )
    return jnp.stack(columns, axis=1)


def generic(latents, teacher, norm_gain, norm_shift, conv_weight, conv_bias):
    row_devices = lax.axis_size("rows")
    panel_devices = lax.axis_size("wt")
    images, channels, strip_rows, column_count = latents.shape
    cell_count = strip_rows * column_count
    total_cells = panel_devices * row_devices * cell_count
    group_cells = channels // GROUPS * cell_count * row_devices
    grouped = latents.reshape(images, GROUPS, channels // GROUPS, cell_count)
    group_sum, square_sum = lax.psum(
        (
            jnp.sum(grouped, axis=(2, 3), keepdims=True),
            jnp.sum(jnp.square(grouped), axis=(2, 3), keepdims=True),
        ),
        "rows",
    )
    group_mean = group_sum / group_cells
    centered = grouped - group_mean
    group_var = square_sum / group_cells - jnp.square(group_mean)
    inverse = lax.rsqrt(group_var + epsilon)
    normed = (centered * inverse).reshape(images, channels, cell_count)
    gain_column = norm_gain[None, :, None]
    pre_norm = normed * gain_column + norm_shift[None, :, None]
    sigmoid_pre = jax.nn.sigmoid(pre_norm)
    hidden = (pre_norm * sigmoid_pre).astype(jnp.bfloat16)
    column_pad = ((0, 0), (0, 0), (0, 0), (1, 1))
    framed_hidden = with_halo(
        hidden.reshape(images, channels, strip_rows, column_count), (("rows", 2),), 1
    )
    padded = jnp.pad(framed_hidden, column_pad)
    all_images = lax.all_gather(framed_hidden, "wt", axis=0, tiled=True)
    all_padded = jnp.pad(all_images, column_pad)
    conv_out = conv_taps(
        lax.all_gather(conv_weight, "wt", axis=0, tiled=True), padded, strip_rows, column_count
    )
    residual = (
        latents.reshape(images, channels, cell_count)
        + conv_out
        + conv_bias[None, :, None]
        - teacher.reshape(images, channels, cell_count)
    )
    low_residual = residual.astype(jnp.bfloat16)
    framed_residual = with_halo(
        low_residual.reshape(images, channels, strip_rows, column_count), (("rows", 2),), 1
    )
    padded_residual = jnp.pad(framed_residual, column_pad)
    panel_residual = lax.all_to_all(framed_residual, "wt", split_axis=1, concat_axis=0, tiled=True)
    panel_rows = channels // panel_devices
    panel_inner = panel_residual[:, :, 1 : strip_rows + 1, :].reshape(
        panel_residual.shape[0], panel_rows, cell_count
    )
    window = padded_residual
    grad_hidden = transpose_taps(
        lax.all_gather(conv_weight, "wt", axis=0, tiled=True), window, strip_rows, column_count
    )
    window = panel_inner
    weight_share = lax.psum_scatter(
        weight_terms(window, all_padded, strip_rows, column_count),
        "rows",
        scatter_dimension=0,
        tiled=True,
    )
    grad_weight = lax.all_gather(weight_share, "rows", axis=0, tiled=True) / total_cells
    grad_pre = grad_hidden * sigmoid_pre * (1.0 + pre_norm * (1.0 - sigmoid_pre))
    grad_norm = (grad_pre * gain_column).reshape(grouped.shape)
    normed_groups = normed.reshape(grouped.shape)
    first_sum, second_sum = lax.psum(
        (
            jnp.sum(grad_norm, axis=(2, 3), keepdims=True),
            jnp.sum(grad_norm * normed_groups, axis=(2, 3), keepdims=True),
        ),
        "rows",
    )
    first_mean = first_sum / group_cells
    second_mean = second_sum / group_cells
    grad_latents = residual.reshape(latents.shape) + (
        inverse * (grad_norm - first_mean - normed_groups * second_mean)
    ).reshape(latents.shape)
    totals = lax.psum(
        (
            jnp.sum(jnp.square(residual)),
            jnp.sum(residual, axis=(0, 2)),
            jnp.sum(grad_pre * normed, axis=(0, 2)),
            jnp.sum(grad_pre, axis=(0, 2)),
        ),
        ("rows", "wt"),
    )
    mean_loss = (totals[0] / (total_cells * channels)).reshape(1)
    param_grads = jnp.stack([totals[1], totals[2], totals[3]]) / total_cells
    return (mean_loss, grad_latents, grad_weight, param_grads)


def plane(ref, row, channels):
    return ref[pl.ds(row, channels, stride=2), :]


def split3(x):
    a = x.astype(BF16)
    rest = x - a.astype(F32)
    b = rest.astype(BF16)
    c = (rest - b.astype(F32)).astype(BF16)
    return a, b, c


def membership(channels):
    size = channels // GROUPS
    channel = lax.broadcasted_iota(jnp.int32, (channels, LANES), 0)
    first = lax.broadcasted_iota(jnp.int32, (channels, LANES), 1) * size
    inside = (channel >= first) & (channel < first + size)
    return jnp.where(inside, 1.0, 0.0).astype(BF16)


def dot_nn(a, b):
    return lax.dot_general(a, b, (((1,), (0,)), ((), ())), preferred_element_type=F32)


def dot_nt(a, b):
    return lax.dot_general(a, b, (((1,), (1,)), ((), ())), preferred_element_type=F32)


def group_sums(rows, member):
    a, b, c = split3(rows)
    return dot_nn(a, member) + (dot_nn(b, member) + dot_nn(c, member))


def to_channels(rows, member):
    a, b, c = split3(rows)
    return dot_nt(a, member) + (dot_nt(b, member) + dot_nt(c, member))


def as_rows(columns, channels):
    lane = lax.broadcasted_iota(jnp.int32, (channels, LANES), 1)
    table = jnp.zeros((channels, LANES), F32)
    for i, column in enumerate(columns):
        table = jnp.where(lane == i, column, table)
    return jnp.transpose(table)[:8, :]


def as_columns(rows, channels):
    pad = jnp.zeros((LANES - len(rows), channels), F32)
    return jnp.transpose(jnp.concatenate(rows + [pad], axis=0))


def row_sum(a, b):
    return jnp.sum(a + b, axis=1, keepdims=True)


def stats_kernel(lat, out):
    channels = out.shape[1]
    a, b = plane(lat, 0, channels), plane(lat, 1, channels)
    out[...] = as_rows([row_sum(a, b), row_sum(a * a, b * b)], channels)


def hidden_kernel(cells, lat, s0, s1, s2, s3, given, hidden, table):
    channels = s0.shape[1]
    member = membership(channels)
    sums = group_sums((s0[...] + s1[...]) + (s2[...] + s3[...]), member)
    mean = sums[0:1] / cells
    var = sums[1:2] / cells - mean * mean
    inverse = lax.rsqrt(var + epsilon)
    pad = jnp.zeros((6, LANES), F32)
    rows = to_channels(jnp.concatenate([mean, inverse, pad], axis=0), member)
    columns = as_columns([rows[0:1], rows[1:2], given[0:1], given[1:2], given[2:3]], channels)
    table[...] = columns
    for row in range(2):
        normed = (plane(lat, row, channels) - columns[:, 0:1]) * columns[:, 1:2]
        pre = normed * columns[:, 2:3] + columns[:, 3:4]
        hidden[row] = (pre * jax.nn.sigmoid(pre)).astype(BF16)


def shifts(x):
    wide = x.astype(F32)
    lane = lax.broadcasted_iota(jnp.int32, x.shape, 1)
    left = jnp.where(lane == 0, 0.0, pltpu.roll(wide, 1, 1)).astype(BF16)
    right = jnp.where(lane == LANES - 1, 0.0, pltpu.roll(wide, LANES - 1, 1)).astype(BF16)
    return left, x, right


def base_kernel(lat, tea, table, base):
    channels = table.shape[0]
    for row in range(2):
        base[row] = plane(lat, row, channels) + table[:, 4:5] - plane(tea, row, channels)


def frame_kernel(place, mine, above, below, framed):
    strip = place[0]
    edge = jnp.zeros_like(mine[0])
    before = jnp.where(strip > 0, below[1], edge)
    after = jnp.where(strip < 3, above[0], edge)
    for row, source in enumerate((before, mine[0], mine[1], after)):
        for kx, moved in enumerate(shifts(source)):
            framed[kx, row] = moved


def panel_rows(me, k, panel):
    return pl.ds(pl.multiple_of((me ^ k) * panel, panel), panel)


def conv_step(total, framed, ky, kx, first, second):
    window = jnp.concatenate([framed[kx, ky], framed[kx, ky + 1]], axis=1)
    total[...] += dot_nn(jnp.concatenate([first, second], axis=0), window)


def near_conv_kernel(place, near, side, framed, base, part, block0, block1, total):
    me = place[1]
    panel = near.shape[1]
    total[...] = jnp.zeros_like(total)

    def step(tap, carry):
        ky = tap // 3
        conv_step(total, framed, ky, tap - 3 * ky, near[tap], side[tap])
        return carry

    lax.fori_loop(0, 9, step, 0)
    for k, block in enumerate((block0, block1)):
        for row in range(2):
            value = base[row, panel_rows(me, k, panel), :] + (
                total[k * panel : (k + 1) * panel, row * LANES : (row + 1) * LANES]
            )
            part[k, row] = value
            block[row] = value.astype(BF16)


def far_conv_kernel(
    place, far0, far1, far2, far3, far4, diag0, diag1, diag2, diag3, diag4, framed, base, part,
    res, low, block23, total,
):
    me, half = place[1], place[2]
    panel = far0.shape[1]
    total[...] = jnp.zeros_like(total)

    def run(first, far, diag):
        def step(i, carry):
            tap = first + i
            ky = tap // 3
            conv_step(total, framed, ky, tap - 3 * ky, far[i], diag[i])
            return carry

        lax.fori_loop(0, far.shape[0], step, 0)

    run(2 * half, far0, diag0)
    run(2 - 2 * half, far1, diag1)
    run(4 + half, far2, diag2)
    run(5 - half, far3, diag3)
    run(6, far4, diag4)
    for k in range(4):
        rows = panel_rows(me, k, panel)
        for row in range(2):
            if k < 2:
                value = part[k, row]
            else:
                value = base[row, rows, :] + (
                    total[(k - 2) * panel : (k - 1) * panel, row * LANES : (row + 1) * LANES]
                )
                block23[k - 2, row] = value.astype(BF16)
            res[row, rows, :] = value
            low[row, rows, :] = value.astype(BF16)


def assemble_kernel(
    place, near, side, far0, far1, far2, far3, far4, diag0, diag1, diag2, diag3, diag4, full
):
    me, half = place[1], place[2]
    panel = near.shape[1]
    near_taps, side_taps = panel_rows(me, 0, panel), panel_rows(me, 1, panel)
    far_taps, diag_taps = panel_rows(me, 2, panel), panel_rows(me, 3, panel)

    def local(tap, carry):
        full[tap, near_taps, :] = near[tap]
        full[tap, side_taps, :] = side[tap]
        return carry

    lax.fori_loop(0, 9, local, 0)
    parts = (
        (2 * half, far0, diag0), (2 - 2 * half, far1, diag1), (4 + half, far2, diag2),
        (5 - half, far3, diag3), (6, far4, diag4),
    )
    for first, far, diag in parts:
        def remote(i, carry, first=first, far=far, diag=diag):
            full[first + i, far_taps, :] = far[i]
            full[first + i, diag_taps, :] = diag[i]
            return carry

        lax.fori_loop(0, far.shape[0], remote, 0)


def back_kernel(full, before, low, after, res, lat, table, grad, sums, framed, total):
    channels = low.shape[1]
    for row, source in enumerate((before[0], low[0], low[1], after[0])):
        for kx, moved in enumerate(shifts(source)):
            framed[kx, row] = jnp.transpose(moved)
    total[...] = jnp.zeros_like(total)

    def tap_step(tap, carry):
        ky = tap // 3
        kx = tap - 3 * ky
        window = jnp.concatenate([framed[2 - kx, 2 - ky], framed[2 - kx, 3 - ky]], axis=0)
        total[...] += dot_nn(window, full[tap])
        return carry

    lax.fori_loop(0, 9, tap_step, 0)
    columns = table[...]
    first = second = bottom = loss = None
    for row in range(2):
        normed = (plane(lat, row, channels) - columns[:, 0:1]) * columns[:, 1:2]
        pre = normed * columns[:, 2:3] + columns[:, 3:4]
        s = jax.nn.sigmoid(pre)
        value = jnp.transpose(total[row * LANES : (row + 1) * LANES, :]) * s * (1.0 + pre * (1.0 - s))
        grad[row] = value
        r = res[row]
        terms = (value, value * normed, r, r * r)
        if row == 0:
            first, second, bottom, loss = terms
        else:
            first, second, bottom, loss = (
                first + terms[0], second + terms[1], bottom + terms[2], loss + terms[3],
            )
    add = functools.partial(jnp.sum, axis=1, keepdims=True)
    sums[...] = as_rows([add(first), add(second), add(bottom), add(loss)], channels)


def latents_kernel(cells, s0, s1, s2, s3, given, res, grad, lat, table, out, total):
    channels = total.shape[1]
    member = membership(channels)
    sums = (s0[...] + s1[...]) + (s2[...] + s3[...])
    total[...] = sums
    means = group_sums(sums * given[0:1], member) / cells
    rows = to_channels(means, member)
    columns = as_columns([rows[0:1], rows[1:2]], channels)
    constants = table[...]
    inverse = constants[:, 1:2]
    for row in range(2):
        normed = (plane(lat, row, channels) - constants[:, 0:1]) * inverse
        change = grad[row] * constants[:, 2:3] - columns[:, 0:1] - normed * columns[:, 1:2]
        out[pl.ds(row, channels, stride=2), :] = res[row] + inverse * change


def weight_pair(strip, pair, aligned, one, two, first, images, base, lefts, emit):
    panel, channels = aligned.shape[2], images[0].shape[1]
    for m in range(2):
        for k in range(2):
            for row in range(2):
                lane = pl.ds((2 * k + row) * LANES, LANES)
                source = aligned[base + k, row]
                if m == 1:
                    source = jnp.where(first, one[base + k, row], two[base + k, row])
                moved = shifts(source)
                for kx in range(3):
                    lefts[(strip & 1) ^ m, kx * panel : (kx + 1) * panel, lane] = moved[2 - kx]

    def step(ky, carry):
        product = None
        for m in range(2):
            right = jnp.concatenate(
                [images[k][4 * pair + 2 * m + ky + row] for k in range(2) for row in range(2)], axis=1
            )
            part = dot_nt(lefts[m], right)
            product = part if product is None else product + part
        emit(pl.ds(3 * ky, 3), product.reshape(3, panel, channels))
        return carry

    lax.fori_loop(0, 3, step, 0)


def totals_kernel(cells, s0, s1, s2, s3, loss, grads):
    sums = (s0[...] + s1[...]) + (s2[...] + s3[...])
    square = jnp.sum(sums[3:4], axis=1, keepdims=True) / (cells * sums.shape[1])
    loss[...] = jnp.broadcast_to(square, loss.shape)
    for row, source in enumerate((2, 1, 0)):
        grads[row : row + 1] = sums[source : source + 1] / cells


def spread_kernel(place, mine, above, beyond, below, spread):
    strip = place[0]
    channels = spread.shape[1]
    spread[0] = jnp.zeros((channels, LANES), BF16)
    spread[9] = jnp.zeros((channels, LANES), BF16)
    for m, source in enumerate((mine, above, beyond, below)):
        for row in range(2):
            spread[1 + 2 * ((strip + m) & 3) + row] = source[row]


def near_weight_kernel(place, own, plus, minus, h0, h1, out, lefts):
    strip = place[0]

    def emit(taps, product):
        out[taps] = product

    weight_pair(strip, strip // 2, own, plus, minus, (strip & 1) == 0, (h0, h1), 0, lefts, emit)


def next_weight_kernel(place, own, plus, minus, h2, h3, near, out, lefts):
    strip = place[0]

    def emit(taps, product):
        out[taps] = near[taps] + product

    weight_pair(strip, strip // 2, own, plus, minus, (strip & 1) == 0, (h2, h3), 2, lefts, emit)


def far_weight_kernel(cells, place, plus, minus, far, h0, h1, h2, h3, near, out, lefts, held, sems):
    strip = place[0]
    pair, even = 1 - strip // 2, (strip & 1) == 0

    def written(taps, slot):
        return pltpu.make_async_copy(held.at[taps], out.at[taps], sems.at[slot])

    def keep(taps, product):
        held[taps] = product

    def emit(taps, product):
        held[taps] = (near[taps] + (held[taps] + product)) / cells
        for slot in range(3):
            @pl.when(taps.start == 3 * slot)
            def _(slot=slot):
                written(pl.ds(3 * slot, 3), slot).start()

    weight_pair(strip, pair, far, minus, plus, even, (h0, h1), 0, lefts, keep)
    weight_pair(strip, pair, far, minus, plus, even, (h2, h3), 2, lefts, emit)
    for slot in range(3):
        written(pl.ds(3 * slot, 3), slot).wait()


VM = pl.BlockSpec(memory_space=pltpu.VMEM)
SM = pl.BlockSpec(memory_space=pltpu.SMEM)


def call(kernel, outs, specs, args, scratch=(), mib=8, us=3, space=VM):
    return pl.pallas_call(
        kernel,
        out_shape=outs,
        in_specs=specs,
        out_specs=jax.tree.map(lambda _: space, outs),
        scratch_shapes=scratch,
        compiler_params=pltpu.CompilerParams(vmem_limit_bytes=mib << 20),
        cost_estimate=pl.CostEstimate(
            flops=int(us * 1e9), bytes_accessed=int(us * 3e6), transcendentals=0
        ),
    )(*args)


def shape(dims, dtype):
    return jax.ShapeDtypeStruct(dims, dtype)


def swap(x, axis, mask):
    size = lax.axis_size(axis)
    return lax.ppermute(x, axis, [(i, i ^ mask) for i in range(size)])


def ring(x, axis, step):
    size = lax.axis_size(axis)
    return lax.ppermute(x, axis, [((i + step) % size, i) for i in range(size)])


def after_all(x, *others):
    return lax.optimization_barrier((x, *others))[0]


def strips_of_four(latents, teacher, norm_gain, norm_shift, conv_weight, conv_bias):
    row_devices = lax.axis_size("rows")
    panel_devices = lax.axis_size("wt")
    _, channels, strip_rows, width = latents.shape
    panel = conv_weight.shape[0]
    strip_cells = strip_rows * width
    total_cells = panel_devices * row_devices * strip_cells
    group_cells = channels // GROUPS * strip_cells * row_devices
    up = [(i, i + 1) for i in range(row_devices - 1)]
    down = [(i + 1, i) for i in range(row_devices - 1)]
    lat = latents.reshape(channels * strip_rows, width)
    tea = teacher.reshape(channels * strip_rows, width)
    given = jnp.stack([norm_gain, norm_shift, conv_bias])
    part = lax.axis_index("grp").astype(jnp.int32)
    here = lax.axis_index("wt").astype(jnp.int32)
    strip = lax.axis_index("rows").astype(jnp.int32)
    place = jnp.stack([strip, here, part])

    near = jnp.transpose(conv_weight, (1, 0, 2))
    far0 = swap(lax.dynamic_slice_in_dim(near, part * 2, 2, axis=0), "wt", 2)
    side = swap(near, "wt", 1)

    stats = call(stats_kernel, shape((8, channels), F32), [VM], (lat,))
    hidden, table = call(
        functools.partial(hidden_kernel, group_cells),
        (shape((strip_rows, channels, width), BF16), shape((channels, LANES), F32)),
        [VM] * 6,
        (lat, after_all(stats, far0, side), *(swap(stats, "rows", m) for m in (1, 2, 3)), given),
        us=0.05,
    )
    above, below = ring(hidden, "rows", 1), ring(hidden, "rows", 3)
    later = after_all(near, hidden)
    far2 = swap(lax.dynamic_slice_in_dim(later, 4 + part, 1, axis=0), "wt", 2)
    far4 = swap(later[6:9], "wt", 2)
    far1, far3 = swap(after_all(far0, hidden), "grp", 1), swap(far2, "grp", 1)
    base = call(
        base_kernel, shape((strip_rows, channels, width), F32), [VM] * 3, (lat, tea, table), us=5
    )
    framed = call(
        frame_kernel,
        shape((3, 4, channels, width), BF16),
        [SM] + [VM] * 3,
        (place, after_all(hidden, base), above, below),
        us=5,
    )
    beyond = ring(above, "rows", 1)
    rows_of = functools.partial(
        call, spread_kernel, shape((10, channels, width), BF16), [SM] + [VM] * 4, us=3
    )
    part0, block0, block1 = call(
        near_conv_kernel,
        (
            shape((2, strip_rows, panel, width), F32),
            shape((strip_rows, panel, width), BF16),
            shape((strip_rows, panel, width), BF16),
        ),
        [SM] + [VM] * 4,
        (place, near, side, framed, base),
        [pltpu.VMEM((2 * panel, 2 * LANES), F32)],
        us=20,
    )
    fars = lax.optimization_barrier((far0, far1, far2, far3, far4, part0, beyond))[:5]
    weights = (near, side, *fars, *(swap(far, "wt", 1) for far in fars))
    res, low, block23 = call(
        far_conv_kernel,
        (
            shape((strip_rows, channels, width), F32),
            shape((strip_rows, channels, width), BF16),
            shape((2, strip_rows, panel, width), BF16),
        ),
        [SM] + [VM] * 13,
        (place, *weights[2:], framed, base, part0),
        [pltpu.VMEM((2 * panel, 2 * LANES), F32)],
        us=0.05,
    )

    block1 = swap(block1, "wt", 1)
    block23 = swap(block23, "wt", 2)
    stacked = jnp.stack([block0, block1, block23[0], swap(block23[1], "wt", 1)])
    settled = after_all(low, stacked)
    low_before = lax.ppermute(settled[1:2], "rows", up)
    low_after = lax.ppermute(settled[0:1], "rows", down)
    plus = ring(stacked, "rows", 1)
    minus = ring(after_all(stacked, plus), "rows", 3)
    far = ring(plus, "rows", 1)
    full = call(
        assemble_kernel,
        shape((9, channels, channels), BF16),
        [SM] + [VM] * 12,
        (after_all(place, stacked), *weights),
        us=5,
    )

    across = [swap(after_all(hidden, block23), "wt", 2)]
    across.append(swap(after_all(above, across[0]), "wt", 2))
    below_across = swap(after_all(below, across[1]), "wt", 2)
    own_rows = rows_of((after_all(place, full), hidden, above, beyond, below))
    other_rows = swap(own_rows, "wt", 1)

    grad, sums = call(
        back_kernel,
        (shape((strip_rows, channels, width), F32), shape((8, channels), F32)),
        [VM] * 7,
        (full, low_before, after_all(low, plus, across[1]), low_after, res, lat, table),
        [
            pltpu.VMEM((3, 4, LANES, channels), BF16),
            pltpu.VMEM((2 * LANES, channels), F32),
        ],
        mib=12, us=30,
    )
    sums = after_all(sums, minus, other_rows, below_across)
    across += [swap(after_all(beyond, grad), "wt", 2), below_across]
    across_rows = rows_of((after_all(place, sums), *across))
    near_weight = call(
        near_weight_kernel,
        shape((9, panel, channels), F32),
        [SM] + [VM] * 5,
        (after_all(place, sums), stacked, plus, minus, own_rows, other_rows),
        [pltpu.VMEM((2, 3 * panel, 4 * LANES), BF16)],
        mib=14, us=30,
    )
    grad_latents, sums = call(
        functools.partial(latents_kernel, group_cells),
        (shape((channels * strip_rows, width), F32), shape((8, channels), F32)),
        [VM] * 9,
        (
            after_all(sums, near_weight), *(swap(sums, "rows", m) for m in (1, 2, 3)),
            given, res, grad, lat, table,
        ),
        us=0.05,
    )
    diag_rows = swap(after_all(across_rows, grad_latents), "wt", 1)
    images = (own_rows, other_rows, across_rows, diag_rows)
    next_weight = call(
        next_weight_kernel,
        shape((9, panel, channels), F32),
        [SM] + [VM] * 6,
        (after_all(place, grad_latents), stacked, plus, minus, across_rows, diag_rows, near_weight),
        [pltpu.VMEM((2, 3 * panel, 4 * LANES), BF16)],
        mib=16, us=30,
    )
    loss, param_grads = call(
        functools.partial(totals_kernel, total_cells),
        (shape((1, LANES), F32), shape((3, channels), F32)),
        [VM] * 4,
        (after_all(sums, next_weight), *(swap(sums, "wt", m) for m in (1, 2, 3))),
        us=0.05,
    )

    grad_weight = call(
        functools.partial(far_weight_kernel, total_cells),
        shape((9, panel, channels), F32),
        [SM] + [VM] * 8,
        (place, plus, minus, far, *images, after_all(next_weight, param_grads)),
        [
            pltpu.VMEM((2, 3 * panel, 4 * LANES), BF16),
            pltpu.VMEM((9, panel, channels), F32),
            pltpu.SemaphoreType.DMA((3,)),
        ],
        mib=18, us=0.05, space=pl.BlockSpec(memory_space=pl.ANY),
    )
    return (
        loss[0, :1],
        grad_latents.reshape(latents.shape),
        jnp.transpose(grad_weight, (1, 0, 2)),
        param_grads,
    )


def solution(mesh):
    placed = (
        P(("grp", "wt"), None, "rows", None),
        P(("grp", "wt"), None, "rows", None),
        P(),
        P(),
        P("wt", None, None),
        P(),
    )
    small = mesh.shape["rows"] == 4 and mesh.shape["wt"] == 4 and mesh.shape["grp"] == 2
    return jax.shard_map(
        strips_of_four if small else generic,
        mesh=mesh,
        in_specs=placed,
        out_specs=(
            P("grp"),
            P(("grp", "wt"), None, "rows", None),
            P(("grp", "wt"), None, None),
            P("grp", None),
        ),
        check_vma=False,
    )
```

```python
import functools

import jax
import jax.numpy as jnp
from jax import lax
from jax.experimental import pallas as pl
from jax.experimental.pallas import tpu as pltpu
from jax.sharding import PartitionSpec as P

GROUPS = 32
LANES = 128
epsilon = 1e-05
F32 = jnp.float32
BF16 = jnp.bfloat16


def with_halo(shard, sides, width):
    for axis, dim in sides:
        devices, length = (lax.axis_size(axis), shard.shape[dim])
        up = [(i, (i + 1) % devices) for i in range(devices - 1)]
        down = [(j, i) for i, j in up]
        last = lax.slice_in_dim(shard, length - width, length, axis=dim)
        leading = lax.slice_in_dim(shard, 0, width, axis=dim)
        before = lax.ppermute(last, axis, up)
        after = lax.ppermute(leading, axis, down)
        shard = jnp.concatenate([before, shard, after], axis=dim)
    return shard


def conv_taps(weights, padded, strip_rows, column_count):
    running = None
    for tap_index in range(9):
        tap_row, tap_col = (tap_index // 3, tap_index % 3)
        window = padded[:, :, tap_row : tap_row + strip_rows, tap_col : tap_col + column_count]
        window = window.reshape(padded.shape[0], padded.shape[1], strip_rows * column_count)
        product = jnp.einsum(
            "oi,nip->nop", weights[:, tap_index, :], window, preferred_element_type=jnp.float32
        )
        running = product if running is None else running + product
    return running


def transpose_taps(weights, padded, strip_rows, column_count):
    running = None
    for tap_index in range(9):
        tap_row, tap_col = (tap_index // 3, tap_index % 3)
        window = padded[
            :, :, 2 - tap_row : 2 - tap_row + strip_rows, 2 - tap_col : 2 - tap_col + column_count
        ]
        window = window.reshape(padded.shape[0], padded.shape[1], strip_rows * column_count)
        product = jnp.einsum(
            "oi,nop->nip", weights[:, tap_index, :], window, preferred_element_type=jnp.float32
        )
        running = product if running is None else running + product
    return running


def weight_terms(residual, padded, strip_rows, column_count):
    columns = []
    for tap_index in range(9):
        tap_row, tap_col = (tap_index // 3, tap_index % 3)
        window = padded[:, :, tap_row : tap_row + strip_rows, tap_col : tap_col + column_count]
        window = window.reshape(padded.shape[0], padded.shape[1], strip_rows * column_count)
        columns.append(
            jnp.einsum("nop,nip->oi", residual, window, preferred_element_type=jnp.float32)
        )
    return jnp.stack(columns, axis=1)


def generic(latents, teacher, norm_gain, norm_shift, conv_weight, conv_bias):
    row_devices = lax.axis_size("rows")
    panel_devices = lax.axis_size("wt")
    images, channels, strip_rows, column_count = latents.shape
    cell_count = strip_rows * column_count
    total_cells = panel_devices * row_devices * cell_count
    group_cells = channels // GROUPS * cell_count * row_devices
    grouped = latents.reshape(images, GROUPS, channels // GROUPS, cell_count)
    group_sum, square_sum = lax.psum(
        (
            jnp.sum(grouped, axis=(2, 3), keepdims=True),
            jnp.sum(jnp.square(grouped), axis=(2, 3), keepdims=True),
        ),
        "rows",
    )
    group_mean = group_sum / group_cells
    centered = grouped - group_mean
    group_var = square_sum / group_cells - jnp.square(group_mean)
    inverse = lax.rsqrt(group_var + epsilon)
    normed = (centered * inverse).reshape(images, channels, cell_count)
    gain_column = norm_gain[None, :, None]
    pre_norm = normed * gain_column + norm_shift[None, :, None]
    sigmoid_pre = jax.nn.sigmoid(pre_norm)
    hidden = (pre_norm * sigmoid_pre).astype(jnp.bfloat16)
    column_pad = ((0, 0), (0, 0), (0, 0), (1, 1))
    framed_hidden = with_halo(
        hidden.reshape(images, channels, strip_rows, column_count), (("rows", 2),), 1
    )
    padded = jnp.pad(framed_hidden, column_pad)
    all_images = lax.all_gather(framed_hidden, "wt", axis=0, tiled=True)
    all_padded = jnp.pad(all_images, column_pad)
    conv_out = conv_taps(
        lax.all_gather(conv_weight, "wt", axis=0, tiled=True), padded, strip_rows, column_count
    )
    residual = (
        latents.reshape(images, channels, cell_count)
        + conv_out
        + conv_bias[None, :, None]
        - teacher.reshape(images, channels, cell_count)
    )
    low_residual = residual.astype(jnp.bfloat16)
    framed_residual = with_halo(
        low_residual.reshape(images, channels, strip_rows, column_count), (("rows", 2),), 1
    )
    padded_residual = jnp.pad(framed_residual, column_pad)
    panel_residual = lax.all_to_all(framed_residual, "wt", split_axis=1, concat_axis=0, tiled=True)
    panel_rows = channels // panel_devices
    panel_inner = panel_residual[:, :, 1 : strip_rows + 1, :].reshape(
        panel_residual.shape[0], panel_rows, cell_count
    )
    window = padded_residual
    grad_hidden = transpose_taps(
        lax.all_gather(conv_weight, "wt", axis=0, tiled=True), window, strip_rows, column_count
    )
    window = panel_inner
    weight_share = lax.psum_scatter(
        weight_terms(window, all_padded, strip_rows, column_count),
        "rows",
        scatter_dimension=0,
        tiled=True,
    )
    grad_weight = lax.all_gather(weight_share, "rows", axis=0, tiled=True) / total_cells
    grad_pre = grad_hidden * sigmoid_pre * (1.0 + pre_norm * (1.0 - sigmoid_pre))
    grad_norm = (grad_pre * gain_column).reshape(grouped.shape)
    normed_groups = normed.reshape(grouped.shape)
    first_sum, second_sum = lax.psum(
        (
            jnp.sum(grad_norm, axis=(2, 3), keepdims=True),
            jnp.sum(grad_norm * normed_groups, axis=(2, 3), keepdims=True),
        ),
        "rows",
    )
    first_mean = first_sum / group_cells
    second_mean = second_sum / group_cells
    grad_latents = residual.reshape(latents.shape) + (
        inverse * (grad_norm - first_mean - normed_groups * second_mean)
    ).reshape(latents.shape)
    totals = lax.psum(
        (
            jnp.sum(jnp.square(residual)),
            jnp.sum(residual, axis=(0, 2)),
            jnp.sum(grad_pre * normed, axis=(0, 2)),
            jnp.sum(grad_pre, axis=(0, 2)),
        ),
        ("rows", "wt"),
    )
    mean_loss = (totals[0] / (total_cells * channels)).reshape(1)
    param_grads = jnp.stack([totals[1], totals[2], totals[3]]) / total_cells
    return (mean_loss, grad_latents, grad_weight, param_grads)


def plane(ref, row, channels):
    return ref[pl.ds(row, channels, stride=2), :]


def split3(x):
    a = x.astype(BF16)
    rest = x - a.astype(F32)
    b = rest.astype(BF16)
    c = (rest - b.astype(F32)).astype(BF16)
    return a, b, c


def membership(channels):
    size = channels // GROUPS
    channel = lax.broadcasted_iota(jnp.int32, (channels, LANES), 0)
    first = lax.broadcasted_iota(jnp.int32, (channels, LANES), 1) * size
    inside = (channel >= first) & (channel < first + size)
    return jnp.where(inside, 1.0, 0.0).astype(BF16)


def dot_nn(a, b):
    return lax.dot_general(a, b, (((1,), (0,)), ((), ())), preferred_element_type=F32)


def dot_nt(a, b):
    return lax.dot_general(a, b, (((1,), (1,)), ((), ())), preferred_element_type=F32)


def group_sums(rows, member):
    a, b, c = split3(rows)
    return dot_nn(a, member) + (dot_nn(b, member) + dot_nn(c, member))


def to_channels(rows, member):
    a, b, c = split3(rows)
    return dot_nt(a, member) + (dot_nt(b, member) + dot_nt(c, member))


def as_rows(columns, channels):
    lane = lax.broadcasted_iota(jnp.int32, (channels, LANES), 1)
    table = jnp.zeros((channels, LANES), F32)
    for i, column in enumerate(columns):
        table = jnp.where(lane == i, column, table)
    return jnp.transpose(table)[:8, :]


def as_columns(rows, channels):
    pad = jnp.zeros((LANES - len(rows), channels), F32)
    return jnp.transpose(jnp.concatenate(rows + [pad], axis=0))


def row_sum(a, b):
    return jnp.sum(a + b, axis=1, keepdims=True)


def stats_kernel(lat, out):
    channels = out.shape[1]
    a, b = plane(lat, 0, channels), plane(lat, 1, channels)
    out[...] = as_rows([row_sum(a, b), row_sum(a * a, b * b)], channels)


def hidden_kernel(cells, lat, s0, s1, s2, s3, given, hidden, table):
    channels = s0.shape[1]
    member = membership(channels)
    sums = group_sums((s0[...] + s1[...]) + (s2[...] + s3[...]), member)
    mean = sums[0:1] / cells
    var = sums[1:2] / cells - mean * mean
    inverse = lax.rsqrt(var + epsilon)
    pad = jnp.zeros((6, LANES), F32)
    rows = to_channels(jnp.concatenate([mean, inverse, pad], axis=0), member)
    columns = as_columns([rows[0:1], rows[1:2], given[0:1], given[1:2], given[2:3]], channels)
    table[...] = columns
    for row in range(2):
        normed = (plane(lat, row, channels) - columns[:, 0:1]) * columns[:, 1:2]
        pre = normed * columns[:, 2:3] + columns[:, 3:4]
        hidden[row] = (pre * jax.nn.sigmoid(pre)).astype(BF16)


def shifts(x):
    wide = x.astype(F32)
    lane = lax.broadcasted_iota(jnp.int32, x.shape, 1)
    left = jnp.where(lane == 0, 0.0, pltpu.roll(wide, 1, 1)).astype(BF16)
    right = jnp.where(lane == LANES - 1, 0.0, pltpu.roll(wide, LANES - 1, 1)).astype(BF16)
    return left, x, right


def base_kernel(lat, tea, table, base):
    channels = table.shape[0]
    for row in range(2):
        base[row] = plane(lat, row, channels) + table[:, 4:5] - plane(tea, row, channels)


def frame_kernel(place, mine, above, below, framed):
    strip = place[0]
    edge = jnp.zeros_like(mine[0])
    before = jnp.where(strip > 0, below[1], edge)
    after = jnp.where(strip < 3, above[0], edge)
    for row, source in enumerate((before, mine[0], mine[1], after)):
        for kx, moved in enumerate(shifts(source)):
            framed[kx, row] = moved


def panel_rows(me, k, panel):
    return pl.ds(pl.multiple_of((me ^ k) * panel, panel), panel)


def conv_step(total, framed, ky, kx, first, second):
    window = jnp.concatenate([framed[kx, ky], framed[kx, ky + 1]], axis=1)
    total[...] += dot_nn(jnp.concatenate([first, second], axis=0), window)


def near_conv_kernel(place, near, side, framed, base, part, block0, block1, total):
    me = place[1]
    panel = near.shape[1]
    total[...] = jnp.zeros_like(total)

    def step(tap, carry):
        ky = tap // 3
        conv_step(total, framed, ky, tap - 3 * ky, near[tap], side[tap])
        return carry

    lax.fori_loop(0, 9, step, 0)
    for k, block in enumerate((block0, block1)):
        for row in range(2):
            value = base[row, panel_rows(me, k, panel), :] + (
                total[k * panel : (k + 1) * panel, row * LANES : (row + 1) * LANES]
            )
            part[k, row] = value
            block[row] = value.astype(BF16)


def far_conv_kernel(
    place, far0, far1, far2, far3, far4, diag0, diag1, diag2, diag3, diag4, framed, base, part,
    res, low, block23, total,
):
    me, half = place[1], place[2]
    panel = far0.shape[1]
    total[...] = jnp.zeros_like(total)

    def run(first, far, diag):
        def step(i, carry):
            tap = first + i
            ky = tap // 3
            conv_step(total, framed, ky, tap - 3 * ky, far[i], diag[i])
            return carry

        lax.fori_loop(0, far.shape[0], step, 0)

    run(2 * half, far0, diag0)
    run(2 - 2 * half, far1, diag1)
    run(4 + half, far2, diag2)
    run(5 - half, far3, diag3)
    run(6, far4, diag4)
    for k in range(4):
        rows = panel_rows(me, k, panel)
        for row in range(2):
            if k < 2:
                value = part[k, row]
            else:
                value = base[row, rows, :] + (
                    total[(k - 2) * panel : (k - 1) * panel, row * LANES : (row + 1) * LANES]
                )
                block23[k - 2, row] = value.astype(BF16)
            res[row, rows, :] = value
            low[row, rows, :] = value.astype(BF16)


def assemble_kernel(
    place, near, side, far0, far1, far2, far3, far4, diag0, diag1, diag2, diag3, diag4, full
):
    me, half = place[1], place[2]
    panel = near.shape[1]
    near_taps, side_taps = panel_rows(me, 0, panel), panel_rows(me, 1, panel)
    far_taps, diag_taps = panel_rows(me, 2, panel), panel_rows(me, 3, panel)

    def local(tap, carry):
        full[tap, near_taps, :] = near[tap]
        full[tap, side_taps, :] = side[tap]
        return carry

    lax.fori_loop(0, 9, local, 0)
    parts = (
        (2 * half, far0, diag0), (2 - 2 * half, far1, diag1), (4 + half, far2, diag2),
        (5 - half, far3, diag3), (6, far4, diag4),
    )
    for first, far, diag in parts:
        def remote(i, carry, first=first, far=far, diag=diag):
            full[first + i, far_taps, :] = far[i]
            full[first + i, diag_taps, :] = diag[i]
            return carry

        lax.fori_loop(0, far.shape[0], remote, 0)


def back_kernel(full, before, low, after, res, lat, table, grad, sums, framed, total):
    channels = low.shape[1]
    for row, source in enumerate((before[0], low[0], low[1], after[0])):
        for kx, moved in enumerate(shifts(source)):
            framed[kx, row] = jnp.transpose(moved)
    total[...] = jnp.zeros_like(total)

    def tap_step(tap, carry):
        ky = tap // 3
        kx = tap - 3 * ky
        window = jnp.concatenate([framed[2 - kx, 2 - ky], framed[2 - kx, 3 - ky]], axis=0)
        total[...] += dot_nn(window, full[tap])
        return carry

    lax.fori_loop(0, 9, tap_step, 0)
    columns = table[...]
    first = second = bottom = loss = None
    for row in range(2):
        normed = (plane(lat, row, channels) - columns[:, 0:1]) * columns[:, 1:2]
        pre = normed * columns[:, 2:3] + columns[:, 3:4]
        s = jax.nn.sigmoid(pre)
        value = jnp.transpose(total[row * LANES : (row + 1) * LANES, :]) * s * (1.0 + pre * (1.0 - s))
        grad[row] = value
        r = res[row]
        terms = (value, value * normed, r, r * r)
        if row == 0:
            first, second, bottom, loss = terms
        else:
            first, second, bottom, loss = (
                first + terms[0], second + terms[1], bottom + terms[2], loss + terms[3],
            )
    add = functools.partial(jnp.sum, axis=1, keepdims=True)
    sums[...] = as_rows([add(first), add(second), add(bottom), add(loss)], channels)


def latents_kernel(cells, s0, s1, s2, s3, given, res, grad, lat, table, out, total):
    channels = total.shape[1]
    member = membership(channels)
    sums = (s0[...] + s1[...]) + (s2[...] + s3[...])
    total[...] = sums
    means = group_sums(sums * given[0:1], member) / cells
    rows = to_channels(means, member)
    columns = as_columns([rows[0:1], rows[1:2]], channels)
    constants = table[...]
    inverse = constants[:, 1:2]
    for row in range(2):
        normed = (plane(lat, row, channels) - constants[:, 0:1]) * inverse
        change = grad[row] * constants[:, 2:3] - columns[:, 0:1] - normed * columns[:, 1:2]
        out[pl.ds(row, channels, stride=2), :] = res[row] + inverse * change


def weight_pair(strip, pair, aligned, one, two, first, images, base, lefts, emit):
    panel, channels = aligned.shape[2], images[0].shape[1]
    for m in range(2):
        for k in range(2):
            for row in range(2):
                lane = pl.ds((2 * k + row) * LANES, LANES)
                source = aligned[base + k, row]
                if m == 1:
                    source = jnp.where(first, one[base + k, row], two[base + k, row])
                moved = shifts(source)
                for kx in range(3):
                    lefts[(strip & 1) ^ m, kx * panel : (kx + 1) * panel, lane] = moved[2 - kx]

    def step(ky, carry):
        product = None
        for m in range(2):
            right = jnp.concatenate(
                [images[k][4 * pair + 2 * m + ky + row] for k in range(2) for row in range(2)], axis=1
            )
            part = dot_nt(lefts[m], right)
            product = part if product is None else product + part
        emit(pl.ds(3 * ky, 3), product.reshape(3, panel, channels))
        return carry

    lax.fori_loop(0, 3, step, 0)


def totals_kernel(cells, s0, s1, s2, s3, loss, grads):
    sums = (s0[...] + s1[...]) + (s2[...] + s3[...])
    square = jnp.sum(sums[3:4], axis=1, keepdims=True) / (cells * sums.shape[1])
    loss[...] = jnp.broadcast_to(square, loss.shape)
    for row, source in enumerate((2, 1, 0)):
        grads[row : row + 1] = sums[source : source + 1] / cells


def spread_kernel(place, mine, above, beyond, below, spread):
    strip = place[0]
    channels = spread.shape[1]
    spread[0] = jnp.zeros((channels, LANES), BF16)
    spread[9] = jnp.zeros((channels, LANES), BF16)
    for m, source in enumerate((mine, above, beyond, below)):
        for row in range(2):
            spread[1 + 2 * ((strip + m) & 3) + row] = source[row]


def near_weight_kernel(place, own, plus, minus, h0, h1, out, lefts):
    strip = place[0]

    def emit(taps, product):
        out[taps] = product

    weight_pair(strip, strip // 2, own, plus, minus, (strip & 1) == 0, (h0, h1), 0, lefts, emit)


def next_weight_kernel(place, own, plus, minus, h2, h3, near, out, lefts):
    strip = place[0]

    def emit(taps, product):
        out[taps] = near[taps] + product

    weight_pair(strip, strip // 2, own, plus, minus, (strip & 1) == 0, (h2, h3), 2, lefts, emit)


def far_weight_kernel(cells, place, plus, minus, far, h0, h1, h2, h3, near, out, lefts, held, sems):
    strip = place[0]
    pair, even = 1 - strip // 2, (strip & 1) == 0

    def written(taps, slot):
        return pltpu.make_async_copy(held.at[taps], out.at[taps], sems.at[slot])

    def keep(taps, product):
        held[taps] = product

    def emit(taps, product):
        held[taps] = (near[taps] + (held[taps] + product)) / cells
        for slot in range(3):
            @pl.when(taps.start == 3 * slot)
            def _(slot=slot):
                written(pl.ds(3 * slot, 3), slot).start()

    weight_pair(strip, pair, far, minus, plus, even, (h0, h1), 0, lefts, keep)
    weight_pair(strip, pair, far, minus, plus, even, (h2, h3), 2, lefts, emit)
    for slot in range(3):
        written(pl.ds(3 * slot, 3), slot).wait()


VM = pl.BlockSpec(memory_space=pltpu.VMEM)
SM = pl.BlockSpec(memory_space=pltpu.SMEM)


def call(kernel, outs, specs, args, scratch=(), mib=8, us=3, space=VM):
    return pl.pallas_call(
        kernel,
        out_shape=outs,
        in_specs=specs,
        out_specs=jax.tree.map(lambda _: space, outs),
        scratch_shapes=scratch,
        compiler_params=pltpu.CompilerParams(vmem_limit_bytes=mib << 20),
        cost_estimate=pl.CostEstimate(
            flops=int(us * 1e9), bytes_accessed=int(us * 3e6), transcendentals=0
        ),
    )(*args)


def shape(dims, dtype):
    return jax.ShapeDtypeStruct(dims, dtype)


def swap(x, axis, mask):
    size = lax.axis_size(axis)
    return lax.ppermute(x, axis, [(i, i ^ mask) for i in range(size)])


def ring(x, axis, step):
    size = lax.axis_size(axis)
    return lax.ppermute(x, axis, [((i + step) % size, i) for i in range(size)])


def after_all(x, *others):
    return lax.optimization_barrier((x, *others))[0]


def strips_of_four(latents, teacher, norm_gain, norm_shift, conv_weight, conv_bias):
    row_devices = lax.axis_size("rows")
    panel_devices = lax.axis_size("wt")
    _, channels, strip_rows, width = latents.shape
    panel = conv_weight.shape[0]
    strip_cells = strip_rows * width
    total_cells = panel_devices * row_devices * strip_cells
    group_cells = channels // GROUPS * strip_cells * row_devices
    up = [(i, i + 1) for i in range(row_devices - 1)]
    down = [(i + 1, i) for i in range(row_devices - 1)]
    lat = latents.reshape(channels * strip_rows, width)
    tea = teacher.reshape(channels * strip_rows, width)
    given = jnp.stack([norm_gain, norm_shift, conv_bias])
    part = lax.axis_index("grp").astype(jnp.int32)
    here = lax.axis_index("wt").astype(jnp.int32)
    strip = lax.axis_index("rows").astype(jnp.int32)
    place = jnp.stack([strip, here, part])

    near = jnp.transpose(conv_weight, (1, 0, 2))
    far0 = swap(lax.dynamic_slice_in_dim(near, part * 2, 2, axis=0), "wt", 2)
    side = swap(near, "wt", 1)

    stats = call(stats_kernel, shape((8, channels), F32), [VM], (lat,))
    hidden, table = call(
        functools.partial(hidden_kernel, group_cells),
        (shape((strip_rows, channels, width), BF16), shape((channels, LANES), F32)),
        [VM] * 6,
        (lat, after_all(stats, far0, side), *(swap(stats, "rows", m) for m in (1, 2, 3)), given),
        us=0.05,
    )
    above, below = ring(hidden, "rows", 1), ring(hidden, "rows", 3)
    later = after_all(near, hidden)
    far2 = swap(lax.dynamic_slice_in_dim(later, 4 + part, 1, axis=0), "wt", 2)
    far4 = swap(later[6:9], "wt", 2)
    far1, far3 = swap(after_all(far0, hidden), "grp", 1), swap(far2, "grp", 1)
    base = call(
        base_kernel, shape((strip_rows, channels, width), F32), [VM] * 3, (lat, tea, table), us=5
    )
    framed = call(
        frame_kernel,
        shape((3, 4, channels, width), BF16),
        [SM] + [VM] * 3,
        (place, after_all(hidden, base), above, below),
        us=5,
    )
    beyond = ring(above, "rows", 1)
    rows_of = functools.partial(
        call, spread_kernel, shape((10, channels, width), BF16), [SM] + [VM] * 4, us=3
    )
    part0, block0, block1 = call(
        near_conv_kernel,
        (
            shape((2, strip_rows, panel, width), F32),
            shape((strip_rows, panel, width), BF16),
            shape((strip_rows, panel, width), BF16),
        ),
        [SM] + [VM] * 4,
        (place, near, side, framed, base),
        [pltpu.VMEM((2 * panel, 2 * LANES), F32)],
        us=20,
    )
    fars = lax.optimization_barrier((far0, far1, far2, far3, far4, part0, beyond))[:5]
    weights = (near, side, *fars, *(swap(far, "wt", 1) for far in fars))
    res, low, block23 = call(
        far_conv_kernel,
        (
            shape((strip_rows, channels, width), F32),
            shape((strip_rows, channels, width), BF16),
            shape((2, strip_rows, panel, width), BF16),
        ),
        [SM] + [VM] * 13,
        (place, *weights[2:], framed, base, part0),
        [pltpu.VMEM((2 * panel, 2 * LANES), F32)],
        us=0.05,
    )

    block1 = swap(block1, "wt", 1)
    block23 = swap(block23, "wt", 2)
    stacked = jnp.stack([block0, block1, block23[0], swap(block23[1], "wt", 1)])
    settled = after_all(low, stacked)
    low_before = lax.ppermute(settled[1:2], "rows", up)
    low_after = lax.ppermute(settled[0:1], "rows", down)
    plus = ring(stacked, "rows", 1)
    minus = ring(after_all(stacked, plus), "rows", 3)
    far = ring(plus, "rows", 1)
    full = call(
        assemble_kernel,
        shape((9, channels, channels), BF16),
        [SM] + [VM] * 12,
        (after_all(place, stacked), *weights),
        us=5,
    )

    across = [swap(after_all(hidden, block23), "wt", 2)]
    across.append(swap(after_all(above, across[0]), "wt", 2))
    below_across = swap(after_all(below, across[0]), "wt", 2)
    own_rows = rows_of((after_all(place, full), hidden, above, beyond, below))
    other_rows = swap(own_rows, "wt", 1)

    grad, sums = call(
        back_kernel,
        (shape((strip_rows, channels, width), F32), shape((8, channels), F32)),
        [VM] * 7,
        (full, low_before, after_all(low, plus), low_after, res, lat, table),
        [
            pltpu.VMEM((3, 4, LANES, channels), BF16),
            pltpu.VMEM((2 * LANES, channels), F32),
        ],
        mib=12, us=30,
    )
    sums = after_all(sums, minus, other_rows, across[1], below_across)
    across += [swap(after_all(beyond, grad), "wt", 2), below_across]
    across_rows = rows_of((after_all(place, sums), *across))
    near_weight = call(
        near_weight_kernel,
        shape((9, panel, channels), F32),
        [SM] + [VM] * 5,
        (after_all(place, sums), stacked, plus, minus, own_rows, other_rows),
        [pltpu.VMEM((2, 3 * panel, 4 * LANES), BF16)],
        mib=14, us=30,
    )
    grad_latents, sums = call(
        functools.partial(latents_kernel, group_cells),
        (shape((channels * strip_rows, width), F32), shape((8, channels), F32)),
        [VM] * 9,
        (
            after_all(sums, near_weight), *(swap(sums, "rows", m) for m in (1, 2, 3)),
            given, res, grad, lat, table,
        ),
        us=0.05,
    )
    diag_rows = swap(after_all(across_rows, grad_latents), "wt", 1)
    images = (own_rows, other_rows, across_rows, diag_rows)
    next_weight = call(
        next_weight_kernel,
        shape((9, panel, channels), F32),
        [SM] + [VM] * 6,
        (after_all(place, grad_latents), stacked, plus, minus, across_rows, diag_rows, near_weight),
        [pltpu.VMEM((2, 3 * panel, 4 * LANES), BF16)],
        mib=16, us=30,
    )
    loss, param_grads = call(
        functools.partial(totals_kernel, total_cells),
        (shape((1, LANES), F32), shape((3, channels), F32)),
        [VM] * 4,
        (after_all(sums, next_weight), *(swap(sums, "wt", m) for m in (1, 2, 3))),
        us=0.05,
    )

    grad_weight = call(
        functools.partial(far_weight_kernel, total_cells),
        shape((9, panel, channels), F32),
        [SM] + [VM] * 8,
        (place, plus, minus, far, *images, after_all(next_weight, param_grads)),
        [
            pltpu.VMEM((2, 3 * panel, 4 * LANES), BF16),
            pltpu.VMEM((9, panel, channels), F32),
            pltpu.SemaphoreType.DMA((3,)),
        ],
        mib=18, us=0.05, space=pl.BlockSpec(memory_space=pl.ANY),
    )
    return (
        loss[0, :1],
        grad_latents.reshape(latents.shape),
        jnp.transpose(grad_weight, (1, 0, 2)),
        param_grads,
    )


def solution(mesh):
    placed = (
        P(("grp", "wt"), None, "rows", None),
        P(("grp", "wt"), None, "rows", None),
        P(),
        P(),
        P("wt", None, None),
        P(),
    )
    small = mesh.shape["rows"] == 4 and mesh.shape["wt"] == 4 and mesh.shape["grp"] == 2
    return jax.shard_map(
        strips_of_four if small else generic,
        mesh=mesh,
        in_specs=placed,
        out_specs=(
            P("grp"),
            P(("grp", "wt"), None, "rows", None),
            P(("grp", "wt"), None, None),
            P("grp", None),
        ),
        check_vma=False,
    )
```

```python
import functools

import jax
import jax.numpy as jnp
from jax import lax
from jax.experimental import pallas as pl
from jax.experimental.pallas import tpu as pltpu
from jax.sharding import PartitionSpec as P

GROUPS = 32
LANES = 128
epsilon = 1e-05
F32 = jnp.float32
BF16 = jnp.bfloat16


def with_halo(shard, sides, width):
    for axis, dim in sides:
        devices, length = (lax.axis_size(axis), shard.shape[dim])
        up = [(i, (i + 1) % devices) for i in range(devices - 1)]
        down = [(j, i) for i, j in up]
        last = lax.slice_in_dim(shard, length - width, length, axis=dim)
        leading = lax.slice_in_dim(shard, 0, width, axis=dim)
        before = lax.ppermute(last, axis, up)
        after = lax.ppermute(leading, axis, down)
        shard = jnp.concatenate([before, shard, after], axis=dim)
    return shard


def conv_taps(weights, padded, strip_rows, column_count):
    running = None
    for tap_index in range(9):
        tap_row, tap_col = (tap_index // 3, tap_index % 3)
        window = padded[:, :, tap_row : tap_row + strip_rows, tap_col : tap_col + column_count]
        window = window.reshape(padded.shape[0], padded.shape[1], strip_rows * column_count)
        product = jnp.einsum(
            "oi,nip->nop", weights[:, tap_index, :], window, preferred_element_type=jnp.float32
        )
        running = product if running is None else running + product
    return running


def transpose_taps(weights, padded, strip_rows, column_count):
    running = None
    for tap_index in range(9):
        tap_row, tap_col = (tap_index // 3, tap_index % 3)
        window = padded[
            :, :, 2 - tap_row : 2 - tap_row + strip_rows, 2 - tap_col : 2 - tap_col + column_count
        ]
        window = window.reshape(padded.shape[0], padded.shape[1], strip_rows * column_count)
        product = jnp.einsum(
            "oi,nop->nip", weights[:, tap_index, :], window, preferred_element_type=jnp.float32
        )
        running = product if running is None else running + product
    return running


def weight_terms(residual, padded, strip_rows, column_count):
    columns = []
    for tap_index in range(9):
        tap_row, tap_col = (tap_index // 3, tap_index % 3)
        window = padded[:, :, tap_row : tap_row + strip_rows, tap_col : tap_col + column_count]
        window = window.reshape(padded.shape[0], padded.shape[1], strip_rows * column_count)
        columns.append(
            jnp.einsum("nop,nip->oi", residual, window, preferred_element_type=jnp.float32)
        )
    return jnp.stack(columns, axis=1)


def generic(latents, teacher, norm_gain, norm_shift, conv_weight, conv_bias):
    row_devices = lax.axis_size("rows")
    panel_devices = lax.axis_size("wt")
    images, channels, strip_rows, column_count = latents.shape
    cell_count = strip_rows * column_count
    total_cells = panel_devices * row_devices * cell_count
    group_cells = channels // GROUPS * cell_count * row_devices
    grouped = latents.reshape(images, GROUPS, channels // GROUPS, cell_count)
    group_sum, square_sum = lax.psum(
        (
            jnp.sum(grouped, axis=(2, 3), keepdims=True),
            jnp.sum(jnp.square(grouped), axis=(2, 3), keepdims=True),
        ),
        "rows",
    )
    group_mean = group_sum / group_cells
    centered = grouped - group_mean
    group_var = square_sum / group_cells - jnp.square(group_mean)
    inverse = lax.rsqrt(group_var + epsilon)
    normed = (centered * inverse).reshape(images, channels, cell_count)
    gain_column = norm_gain[None, :, None]
    pre_norm = normed * gain_column + norm_shift[None, :, None]
    sigmoid_pre = jax.nn.sigmoid(pre_norm)
    hidden = (pre_norm * sigmoid_pre).astype(jnp.bfloat16)
    column_pad = ((0, 0), (0, 0), (0, 0), (1, 1))
    framed_hidden = with_halo(
        hidden.reshape(images, channels, strip_rows, column_count), (("rows", 2),), 1
    )
    padded = jnp.pad(framed_hidden, column_pad)
    all_images = lax.all_gather(framed_hidden, "wt", axis=0, tiled=True)
    all_padded = jnp.pad(all_images, column_pad)
    conv_out = conv_taps(
        lax.all_gather(conv_weight, "wt", axis=0, tiled=True), padded, strip_rows, column_count
    )
    residual = (
        latents.reshape(images, channels, cell_count)
        + conv_out
        + conv_bias[None, :, None]
        - teacher.reshape(images, channels, cell_count)
    )
    low_residual = residual.astype(jnp.bfloat16)
    framed_residual = with_halo(
        low_residual.reshape(images, channels, strip_rows, column_count), (("rows", 2),), 1
    )
    padded_residual = jnp.pad(framed_residual, column_pad)
    panel_residual = lax.all_to_all(framed_residual, "wt", split_axis=1, concat_axis=0, tiled=True)
    panel_rows = channels // panel_devices
    panel_inner = panel_residual[:, :, 1 : strip_rows + 1, :].reshape(
        panel_residual.shape[0], panel_rows, cell_count
    )
    window = padded_residual
    grad_hidden = transpose_taps(
        lax.all_gather(conv_weight, "wt", axis=0, tiled=True), window, strip_rows, column_count
    )
    window = panel_inner
    weight_share = lax.psum_scatter(
        weight_terms(window, all_padded, strip_rows, column_count),
        "rows",
        scatter_dimension=0,
        tiled=True,
    )
    grad_weight = lax.all_gather(weight_share, "rows", axis=0, tiled=True) / total_cells
    grad_pre = grad_hidden * sigmoid_pre * (1.0 + pre_norm * (1.0 - sigmoid_pre))
    grad_norm = (grad_pre * gain_column).reshape(grouped.shape)
    normed_groups = normed.reshape(grouped.shape)
    first_sum, second_sum = lax.psum(
        (
            jnp.sum(grad_norm, axis=(2, 3), keepdims=True),
            jnp.sum(grad_norm * normed_groups, axis=(2, 3), keepdims=True),
        ),
        "rows",
    )
    first_mean = first_sum / group_cells
    second_mean = second_sum / group_cells
    grad_latents = residual.reshape(latents.shape) + (
        inverse * (grad_norm - first_mean - normed_groups * second_mean)
    ).reshape(latents.shape)
    totals = lax.psum(
        (
            jnp.sum(jnp.square(residual)),
            jnp.sum(residual, axis=(0, 2)),
            jnp.sum(grad_pre * normed, axis=(0, 2)),
            jnp.sum(grad_pre, axis=(0, 2)),
        ),
        ("rows", "wt"),
    )
    mean_loss = (totals[0] / (total_cells * channels)).reshape(1)
    param_grads = jnp.stack([totals[1], totals[2], totals[3]]) / total_cells
    return (mean_loss, grad_latents, grad_weight, param_grads)


def plane(ref, row, channels):
    return ref[pl.ds(row, channels, stride=2), :]


def split3(x):
    a = x.astype(BF16)
    rest = x - a.astype(F32)
    b = rest.astype(BF16)
    c = (rest - b.astype(F32)).astype(BF16)
    return a, b, c


def membership(channels):
    size = channels // GROUPS
    channel = lax.broadcasted_iota(jnp.int32, (channels, LANES), 0)
    first = lax.broadcasted_iota(jnp.int32, (channels, LANES), 1) * size
    inside = (channel >= first) & (channel < first + size)
    return jnp.where(inside, 1.0, 0.0).astype(BF16)


def dot_nn(a, b):
    return lax.dot_general(a, b, (((1,), (0,)), ((), ())), preferred_element_type=F32)


def dot_nt(a, b):
    return lax.dot_general(a, b, (((1,), (1,)), ((), ())), preferred_element_type=F32)


def group_sums(rows, member):
    a, b, c = split3(rows)
    return dot_nn(a, member) + (dot_nn(b, member) + dot_nn(c, member))


def to_channels(rows, member):
    a, b, c = split3(rows)
    return dot_nt(a, member) + (dot_nt(b, member) + dot_nt(c, member))


def as_rows(columns, channels):
    lane = lax.broadcasted_iota(jnp.int32, (channels, LANES), 1)
    table = jnp.zeros((channels, LANES), F32)
    for i, column in enumerate(columns):
        table = jnp.where(lane == i, column, table)
    return jnp.transpose(table)[:8, :]


def as_columns(rows, channels):
    pad = jnp.zeros((LANES - len(rows), channels), F32)
    return jnp.transpose(jnp.concatenate(rows + [pad], axis=0))


def row_sum(a, b):
    return jnp.sum(a + b, axis=1, keepdims=True)


def stats_kernel(lat, out):
    channels = out.shape[1]
    a, b = plane(lat, 0, channels), plane(lat, 1, channels)
    out[...] = as_rows([row_sum(a, b), row_sum(a * a, b * b)], channels)


def hidden_kernel(cells, lat, s0, s1, s2, s3, given, hidden, table):
    channels = s0.shape[1]
    member = membership(channels)
    sums = group_sums((s0[...] + s1[...]) + (s2[...] + s3[...]), member)
    mean = sums[0:1] / cells
    var = sums[1:2] / cells - mean * mean
    inverse = lax.rsqrt(var + epsilon)
    pad = jnp.zeros((6, LANES), F32)
    rows = to_channels(jnp.concatenate([mean, inverse, pad], axis=0), member)
    columns = as_columns([rows[0:1], rows[1:2], given[0:1], given[1:2], given[2:3]], channels)
    table[...] = columns
    for row in range(2):
        normed = (plane(lat, row, channels) - columns[:, 0:1]) * columns[:, 1:2]
        pre = normed * columns[:, 2:3] + columns[:, 3:4]
        hidden[row] = (pre * jax.nn.sigmoid(pre)).astype(BF16)


def shifts(x):
    wide = x.astype(F32)
    lane = lax.broadcasted_iota(jnp.int32, x.shape, 1)
    left = jnp.where(lane == 0, 0.0, pltpu.roll(wide, 1, 1)).astype(BF16)
    right = jnp.where(lane == LANES - 1, 0.0, pltpu.roll(wide, LANES - 1, 1)).astype(BF16)
    return left, x, right


def base_kernel(lat, tea, table, base):
    channels = table.shape[0]
    for row in range(2):
        base[row] = plane(lat, row, channels) + table[:, 4:5] - plane(tea, row, channels)


def frame_kernel(place, mine, above, below, framed):
    strip = place[0]
    edge = jnp.zeros_like(mine[0])
    before = jnp.where(strip > 0, below[1], edge)
    after = jnp.where(strip < 3, above[0], edge)
    for row, source in enumerate((before, mine[0], mine[1], after)):
        for kx, moved in enumerate(shifts(source)):
            framed[kx, row] = moved


def panel_rows(me, k, panel):
    return pl.ds(pl.multiple_of((me ^ k) * panel, panel), panel)


def conv_step(total, framed, ky, kx, first, second):
    window = jnp.concatenate([framed[kx, ky], framed[kx, ky + 1]], axis=1)
    total[...] += dot_nn(jnp.concatenate([first, second], axis=0), window)


def near_conv_kernel(place, near, side, framed, base, part, block0, block1, total):
    me = place[1]
    panel = near.shape[1]
    total[...] = jnp.zeros_like(total)

    def step(tap, carry):
        ky = tap // 3
        conv_step(total, framed, ky, tap - 3 * ky, near[tap], side[tap])
        return carry

    lax.fori_loop(0, 9, step, 0)
    for k, block in enumerate((block0, block1)):
        for row in range(2):
            value = base[row, panel_rows(me, k, panel), :] + (
                total[k * panel : (k + 1) * panel, row * LANES : (row + 1) * LANES]
            )
            part[k, row] = value
            block[row] = value.astype(BF16)


def far_conv_kernel(
    place, far0, far1, far2, far3, far4, diag0, diag1, diag2, diag3, diag4, framed, base, part,
    res, low, block23, total,
):
    me, half = place[1], place[2]
    panel = far0.shape[1]
    total[...] = jnp.zeros_like(total)

    def run(first, far, diag):
        def step(i, carry):
            tap = first + i
            ky = tap // 3
            conv_step(total, framed, ky, tap - 3 * ky, far[i], diag[i])
            return carry

        lax.fori_loop(0, far.shape[0], step, 0)

    run(2 * half, far0, diag0)
    run(2 - 2 * half, far1, diag1)
    run(4 + half, far2, diag2)
    run(5 - half, far3, diag3)
    run(6, far4, diag4)
    for k in range(4):
        rows = panel_rows(me, k, panel)
        for row in range(2):
            if k < 2:
                value = part[k, row]
            else:
                value = base[row, rows, :] + (
                    total[(k - 2) * panel : (k - 1) * panel, row * LANES : (row + 1) * LANES]
                )
                block23[k - 2, row] = value.astype(BF16)
            res[row, rows, :] = value
            low[row, rows, :] = value.astype(BF16)


def assemble_kernel(
    place, near, side, far0, far1, far2, far3, far4, diag0, diag1, diag2, diag3, diag4, full
):
    me, half = place[1], place[2]
    panel = near.shape[1]
    near_taps, side_taps = panel_rows(me, 0, panel), panel_rows(me, 1, panel)
    far_taps, diag_taps = panel_rows(me, 2, panel), panel_rows(me, 3, panel)

    def local(tap, carry):
        full[tap, near_taps, :] = near[tap]
        full[tap, side_taps, :] = side[tap]
        return carry

    lax.fori_loop(0, 9, local, 0)
    parts = (
        (2 * half, far0, diag0), (2 - 2 * half, far1, diag1), (4 + half, far2, diag2),
        (5 - half, far3, diag3), (6, far4, diag4),
    )
    for first, far, diag in parts:
        def remote(i, carry, first=first, far=far, diag=diag):
            full[first + i, far_taps, :] = far[i]
            full[first + i, diag_taps, :] = diag[i]
            return carry

        lax.fori_loop(0, far.shape[0], remote, 0)


def back_kernel(full, before, low, after, res, lat, table, grad, sums, framed, total):
    channels = low.shape[1]
    for row, source in enumerate((before[0], low[0], low[1], after[0])):
        for kx, moved in enumerate(shifts(source)):
            framed[kx, row] = jnp.transpose(moved)
    total[...] = jnp.zeros_like(total)

    def tap_step(tap, carry):
        ky = tap // 3
        kx = tap - 3 * ky
        window = jnp.concatenate([framed[2 - kx, 2 - ky], framed[2 - kx, 3 - ky]], axis=0)
        total[...] += dot_nn(window, full[tap])
        return carry

    lax.fori_loop(0, 9, tap_step, 0)
    columns = table[...]
    first = second = bottom = loss = None
    for row in range(2):
        normed = (plane(lat, row, channels) - columns[:, 0:1]) * columns[:, 1:2]
        pre = normed * columns[:, 2:3] + columns[:, 3:4]
        s = jax.nn.sigmoid(pre)
        value = jnp.transpose(total[row * LANES : (row + 1) * LANES, :]) * s * (1.0 + pre * (1.0 - s))
        grad[row] = value
        r = res[row]
        terms = (value, value * normed, r, r * r)
        if row == 0:
            first, second, bottom, loss = terms
        else:
            first, second, bottom, loss = (
                first + terms[0], second + terms[1], bottom + terms[2], loss + terms[3],
            )
    add = functools.partial(jnp.sum, axis=1, keepdims=True)
    sums[...] = as_rows([add(first), add(second), add(bottom), add(loss)], channels)


def latents_kernel(cells, s0, s1, s2, s3, given, res, grad, lat, table, out, total):
    channels = total.shape[1]
    member = membership(channels)
    sums = (s0[...] + s1[...]) + (s2[...] + s3[...])
    total[...] = sums
    means = group_sums(sums * given[0:1], member) / cells
    rows = to_channels(means, member)
    columns = as_columns([rows[0:1], rows[1:2]], channels)
    constants = table[...]
    inverse = constants[:, 1:2]
    for row in range(2):
        normed = (plane(lat, row, channels) - constants[:, 0:1]) * inverse
        change = grad[row] * constants[:, 2:3] - columns[:, 0:1] - normed * columns[:, 1:2]
        out[pl.ds(row, channels, stride=2), :] = res[row] + inverse * change


def weight_pair(strip, pair, aligned, one, two, first, images, base, lefts, emit):
    panel, channels = aligned.shape[2], images[0].shape[1]
    for m in range(2):
        for k in range(2):
            for row in range(2):
                lane = pl.ds((2 * k + row) * LANES, LANES)
                source = aligned[base + k, row]
                if m == 1:
                    source = jnp.where(first, one[base + k, row], two[base + k, row])
                moved = shifts(source)
                for kx in range(3):
                    lefts[(strip & 1) ^ m, kx * panel : (kx + 1) * panel, lane] = moved[2 - kx]

    def step(ky, carry):
        product = None
        for m in range(2):
            right = jnp.concatenate(
                [images[k][4 * pair + 2 * m + ky + row] for k in range(2) for row in range(2)], axis=1
            )
            part = dot_nt(lefts[m], right)
            product = part if product is None else product + part
        emit(pl.ds(3 * ky, 3), product.reshape(3, panel, channels))
        return carry

    lax.fori_loop(0, 3, step, 0)


def totals_kernel(cells, s0, s1, s2, s3, loss, grads):
    sums = (s0[...] + s1[...]) + (s2[...] + s3[...])
    square = jnp.sum(sums[3:4], axis=1, keepdims=True) / (cells * sums.shape[1])
    loss[...] = jnp.broadcast_to(square, loss.shape)
    for row, source in enumerate((2, 1, 0)):
        grads[row : row + 1] = sums[source : source + 1] / cells


def spread_kernel(place, mine, above, beyond, below, spread):
    strip = place[0]
    channels = spread.shape[1]
    spread[0] = jnp.zeros((channels, LANES), BF16)
    spread[9] = jnp.zeros((channels, LANES), BF16)
    for m, source in enumerate((mine, above, beyond, below)):
        for row in range(2):
            spread[1 + 2 * ((strip + m) & 3) + row] = source[row]


def near_weight_kernel(place, own, plus, minus, h0, h1, out, lefts):
    strip = place[0]

    def emit(taps, product):
        out[taps] = product

    weight_pair(strip, strip // 2, own, plus, minus, (strip & 1) == 0, (h0, h1), 0, lefts, emit)


def next_weight_kernel(place, own, plus, minus, h2, h3, near, out, lefts):
    strip = place[0]

    def emit(taps, product):
        out[taps] = near[taps] + product

    weight_pair(strip, strip // 2, own, plus, minus, (strip & 1) == 0, (h2, h3), 2, lefts, emit)


def far_weight_kernel(cells, place, plus, minus, far, h0, h1, h2, h3, near, out, lefts, held, sems):
    strip = place[0]
    pair, even = 1 - strip // 2, (strip & 1) == 0

    def written(taps, slot):
        return pltpu.make_async_copy(held.at[taps], out.at[taps], sems.at[slot])

    def keep(taps, product):
        held[taps] = product

    def emit(taps, product):
        held[taps] = (near[taps] + (held[taps] + product)) / cells
        for slot in range(3):
            @pl.when(taps.start == 3 * slot)
            def _(slot=slot):
                written(pl.ds(3 * slot, 3), slot).start()

    weight_pair(strip, pair, far, minus, plus, even, (h0, h1), 0, lefts, keep)
    weight_pair(strip, pair, far, minus, plus, even, (h2, h3), 2, lefts, emit)
    for slot in range(3):
        written(pl.ds(3 * slot, 3), slot).wait()


VM = pl.BlockSpec(memory_space=pltpu.VMEM)
SM = pl.BlockSpec(memory_space=pltpu.SMEM)


def call(kernel, outs, specs, args, scratch=(), mib=8, us=3, space=VM):
    return pl.pallas_call(
        kernel,
        out_shape=outs,
        in_specs=specs,
        out_specs=jax.tree.map(lambda _: space, outs),
        scratch_shapes=scratch,
        compiler_params=pltpu.CompilerParams(vmem_limit_bytes=mib << 20),
        cost_estimate=pl.CostEstimate(
            flops=int(us * 1e9), bytes_accessed=int(us * 3e6), transcendentals=0
        ),
    )(*args)


def shape(dims, dtype):
    return jax.ShapeDtypeStruct(dims, dtype)


def swap(x, axis, mask):
    size = lax.axis_size(axis)
    return lax.ppermute(x, axis, [(i, i ^ mask) for i in range(size)])


def ring(x, axis, step):
    size = lax.axis_size(axis)
    return lax.ppermute(x, axis, [((i + step) % size, i) for i in range(size)])


def after_all(x, *others):
    return lax.optimization_barrier((x, *others))[0]


def strips_of_four(latents, teacher, norm_gain, norm_shift, conv_weight, conv_bias):
    row_devices = lax.axis_size("rows")
    panel_devices = lax.axis_size("wt")
    _, channels, strip_rows, width = latents.shape
    panel = conv_weight.shape[0]
    strip_cells = strip_rows * width
    total_cells = panel_devices * row_devices * strip_cells
    group_cells = channels // GROUPS * strip_cells * row_devices
    up = [(i, i + 1) for i in range(row_devices - 1)]
    down = [(i + 1, i) for i in range(row_devices - 1)]
    lat = latents.reshape(channels * strip_rows, width)
    tea = teacher.reshape(channels * strip_rows, width)
    given = jnp.stack([norm_gain, norm_shift, conv_bias])
    part = lax.axis_index("grp").astype(jnp.int32)
    here = lax.axis_index("wt").astype(jnp.int32)
    strip = lax.axis_index("rows").astype(jnp.int32)
    place = jnp.stack([strip, here, part])

    near = jnp.transpose(conv_weight, (1, 0, 2))
    far0 = swap(lax.dynamic_slice_in_dim(near, part * 2, 2, axis=0), "wt", 2)
    side = swap(near, "wt", 1)

    stats = call(stats_kernel, shape((8, channels), F32), [VM], (lat,))
    hidden, table = call(
        functools.partial(hidden_kernel, group_cells),
        (shape((strip_rows, channels, width), BF16), shape((channels, LANES), F32)),
        [VM] * 6,
        (lat, after_all(stats, far0, side), *(swap(stats, "rows", m) for m in (1, 2, 3)), given),
        us=0.05,
    )
    above, below = ring(hidden, "rows", 1), ring(hidden, "rows", 3)
    later = after_all(near, hidden)
    far2 = swap(lax.dynamic_slice_in_dim(later, 4 + part, 1, axis=0), "wt", 2)
    far4 = swap(later[6:9], "wt", 2)
    far1, far3 = swap(after_all(far0, hidden), "grp", 1), swap(far2, "grp", 1)
    base = call(
        base_kernel, shape((strip_rows, channels, width), F32), [VM] * 3, (lat, tea, table), us=5
    )
    framed = call(
        frame_kernel,
        shape((3, 4, channels, width), BF16),
        [SM] + [VM] * 3,
        (place, after_all(hidden, base), above, below),
        us=5,
    )
    beyond = ring(above, "rows", 1)
    rows_of = functools.partial(
        call, spread_kernel, shape((10, channels, width), BF16), [SM] + [VM] * 4, us=3
    )
    part0, block0, block1 = call(
        near_conv_kernel,
        (
            shape((2, strip_rows, panel, width), F32),
            shape((strip_rows, panel, width), BF16),
            shape((strip_rows, panel, width), BF16),
        ),
        [SM] + [VM] * 4,
        (place, near, side, framed, base),
        [pltpu.VMEM((2 * panel, 2 * LANES), F32)],
        us=20,
    )
    fars = lax.optimization_barrier((far0, far1, far2, far3, far4, part0, beyond))[:5]
    weights = (near, side, *fars, *(swap(far, "wt", 1) for far in fars))
    res, low, block23 = call(
        far_conv_kernel,
        (
            shape((strip_rows, channels, width), F32),
            shape((strip_rows, channels, width), BF16),
            shape((2, strip_rows, panel, width), BF16),
        ),
        [SM] + [VM] * 13,
        (place, *weights[2:], framed, base, part0),
        [pltpu.VMEM((2 * panel, 2 * LANES), F32)],
        us=0.05,
    )

    block1 = swap(block1, "wt", 1)
    block23 = swap(block23, "wt", 2)
    stacked = jnp.stack([block0, block1, block23[0], swap(block23[1], "wt", 1)])
    settled = after_all(low, stacked)
    low_before = lax.ppermute(settled[1:2], "rows", up)
    low_after = lax.ppermute(settled[0:1], "rows", down)
    plus = ring(stacked, "rows", 1)
    minus = ring(after_all(stacked, plus), "rows", 3)
    far = ring(plus, "rows", 1)
    full = call(
        assemble_kernel,
        shape((9, channels, channels), BF16),
        [SM] + [VM] * 12,
        (after_all(place, stacked), *weights),
        us=5,
    )

    across = [swap(after_all(hidden, block23), "wt", 2)]
    across.append(swap(after_all(above, across[0]), "wt", 2))
    below_across = swap(after_all(below, across[0]), "wt", 2)
    own_rows = rows_of((after_all(place, full), hidden, above, beyond, below))
    other_rows = swap(own_rows, "wt", 1)

    grad, sums = call(
        back_kernel,
        (shape((strip_rows, channels, width), F32), shape((8, channels), F32)),
        [VM] * 7,
        (full, low_before, after_all(low, plus), low_after, res, lat, table),
        [
            pltpu.VMEM((3, 4, LANES, channels), BF16),
            pltpu.VMEM((2 * LANES, channels), F32),
        ],
        mib=12, us=30,
    )
    across += [swap(after_all(beyond, grad), "wt", 2), below_across]
    sums = after_all(sums, minus)
    near_weight = call(
        near_weight_kernel,
        shape((9, panel, channels), F32),
        [SM] + [VM] * 5,
        (after_all(place, sums, across[1], below_across), stacked, plus, minus, own_rows, other_rows),
        [pltpu.VMEM((2, 3 * panel, 4 * LANES), BF16)],
        mib=14, us=30,
    )
    across_rows = rows_of((after_all(place, near_weight), *across))
    grad_latents, sums = call(
        functools.partial(latents_kernel, group_cells),
        (shape((channels * strip_rows, width), F32), shape((8, channels), F32)),
        [VM] * 9,
        (
            after_all(sums, near_weight), *(swap(sums, "rows", m) for m in (1, 2, 3)),
            given, res, grad, lat, table,
        ),
        us=0.05,
    )
    diag_rows = swap(after_all(across_rows, grad_latents), "wt", 1)
    images = (own_rows, other_rows, across_rows, diag_rows)
    next_weight = call(
        next_weight_kernel,
        shape((9, panel, channels), F32),
        [SM] + [VM] * 6,
        (after_all(place, grad_latents), stacked, plus, minus, across_rows, diag_rows, near_weight),
        [pltpu.VMEM((2, 3 * panel, 4 * LANES), BF16)],
        mib=16, us=30,
    )
    loss, param_grads = call(
        functools.partial(totals_kernel, total_cells),
        (shape((1, LANES), F32), shape((3, channels), F32)),
        [VM] * 4,
        (after_all(sums, next_weight), *(swap(sums, "wt", m) for m in (1, 2, 3))),
        us=0.05,
    )

    grad_weight = call(
        functools.partial(far_weight_kernel, total_cells),
        shape((9, panel, channels), F32),
        [SM] + [VM] * 8,
        (place, plus, minus, far, *images, after_all(next_weight, param_grads)),
        [
            pltpu.VMEM((2, 3 * panel, 4 * LANES), BF16),
            pltpu.VMEM((9, panel, channels), F32),
            pltpu.SemaphoreType.DMA((3,)),
        ],
        mib=18, us=0.05, space=pl.BlockSpec(memory_space=pl.ANY),
    )
    return (
        loss[0, :1],
        grad_latents.reshape(latents.shape),
        jnp.transpose(grad_weight, (1, 0, 2)),
        param_grads,
    )


def solution(mesh):
    placed = (
        P(("grp", "wt"), None, "rows", None),
        P(("grp", "wt"), None, "rows", None),
        P(),
        P(),
        P("wt", None, None),
        P(),
    )
    small = mesh.shape["rows"] == 4 and mesh.shape["wt"] == 4 and mesh.shape["grp"] == 2
    return jax.shard_map(
        strips_of_four if small else generic,
        mesh=mesh,
        in_specs=placed,
        out_specs=(
            P("grp"),
            P(("grp", "wt"), None, "rows", None),
            P(("grp", "wt"), None, None),
            P("grp", None),
        ),
        check_vma=False,
    )
```

```python
import functools

import jax
import jax.numpy as jnp
from jax import lax
from jax.experimental import pallas as pl
from jax.experimental.pallas import tpu as pltpu
from jax.sharding import PartitionSpec as P

GROUPS = 32
LANES = 128
epsilon = 1e-05
F32 = jnp.float32
BF16 = jnp.bfloat16


def with_halo(shard, sides, width):
    for axis, dim in sides:
        devices, length = (lax.axis_size(axis), shard.shape[dim])
        up = [(i, (i + 1) % devices) for i in range(devices - 1)]
        down = [(j, i) for i, j in up]
        last = lax.slice_in_dim(shard, length - width, length, axis=dim)
        leading = lax.slice_in_dim(shard, 0, width, axis=dim)
        before = lax.ppermute(last, axis, up)
        after = lax.ppermute(leading, axis, down)
        shard = jnp.concatenate([before, shard, after], axis=dim)
    return shard


def conv_taps(weights, padded, strip_rows, column_count):
    running = None
    for tap_index in range(9):
        tap_row, tap_col = (tap_index // 3, tap_index % 3)
        window = padded[:, :, tap_row : tap_row + strip_rows, tap_col : tap_col + column_count]
        window = window.reshape(padded.shape[0], padded.shape[1], strip_rows * column_count)
        product = jnp.einsum(
            "oi,nip->nop", weights[:, tap_index, :], window, preferred_element_type=jnp.float32
        )
        running = product if running is None else running + product
    return running


def transpose_taps(weights, padded, strip_rows, column_count):
    running = None
    for tap_index in range(9):
        tap_row, tap_col = (tap_index // 3, tap_index % 3)
        window = padded[
            :, :, 2 - tap_row : 2 - tap_row + strip_rows, 2 - tap_col : 2 - tap_col + column_count
        ]
        window = window.reshape(padded.shape[0], padded.shape[1], strip_rows * column_count)
        product = jnp.einsum(
            "oi,nop->nip", weights[:, tap_index, :], window, preferred_element_type=jnp.float32
        )
        running = product if running is None else running + product
    return running


def weight_terms(residual, padded, strip_rows, column_count):
    columns = []
    for tap_index in range(9):
        tap_row, tap_col = (tap_index // 3, tap_index % 3)
        window = padded[:, :, tap_row : tap_row + strip_rows, tap_col : tap_col + column_count]
        window = window.reshape(padded.shape[0], padded.shape[1], strip_rows * column_count)
        columns.append(
            jnp.einsum("nop,nip->oi", residual, window, preferred_element_type=jnp.float32)
        )
    return jnp.stack(columns, axis=1)


def generic(latents, teacher, norm_gain, norm_shift, conv_weight, conv_bias):
    row_devices = lax.axis_size("rows")
    panel_devices = lax.axis_size("wt")
    images, channels, strip_rows, column_count = latents.shape
    cell_count = strip_rows * column_count
    total_cells = panel_devices * row_devices * cell_count
    group_cells = channels // GROUPS * cell_count * row_devices
    grouped = latents.reshape(images, GROUPS, channels // GROUPS, cell_count)
    group_sum, square_sum = lax.psum(
        (
            jnp.sum(grouped, axis=(2, 3), keepdims=True),
            jnp.sum(jnp.square(grouped), axis=(2, 3), keepdims=True),
        ),
        "rows",
    )
    group_mean = group_sum / group_cells
    centered = grouped - group_mean
    group_var = square_sum / group_cells - jnp.square(group_mean)
    inverse = lax.rsqrt(group_var + epsilon)
    normed = (centered * inverse).reshape(images, channels, cell_count)
    gain_column = norm_gain[None, :, None]
    pre_norm = normed * gain_column + norm_shift[None, :, None]
    sigmoid_pre = jax.nn.sigmoid(pre_norm)
    hidden = (pre_norm * sigmoid_pre).astype(jnp.bfloat16)
    column_pad = ((0, 0), (0, 0), (0, 0), (1, 1))
    framed_hidden = with_halo(
        hidden.reshape(images, channels, strip_rows, column_count), (("rows", 2),), 1
    )
    padded = jnp.pad(framed_hidden, column_pad)
    all_images = lax.all_gather(framed_hidden, "wt", axis=0, tiled=True)
    all_padded = jnp.pad(all_images, column_pad)
    conv_out = conv_taps(
        lax.all_gather(conv_weight, "wt", axis=0, tiled=True), padded, strip_rows, column_count
    )
    residual = (
        latents.reshape(images, channels, cell_count)
        + conv_out
        + conv_bias[None, :, None]
        - teacher.reshape(images, channels, cell_count)
    )
    low_residual = residual.astype(jnp.bfloat16)
    framed_residual = with_halo(
        low_residual.reshape(images, channels, strip_rows, column_count), (("rows", 2),), 1
    )
    padded_residual = jnp.pad(framed_residual, column_pad)
    panel_residual = lax.all_to_all(framed_residual, "wt", split_axis=1, concat_axis=0, tiled=True)
    panel_rows = channels // panel_devices
    panel_inner = panel_residual[:, :, 1 : strip_rows + 1, :].reshape(
        panel_residual.shape[0], panel_rows, cell_count
    )
    window = padded_residual
    grad_hidden = transpose_taps(
        lax.all_gather(conv_weight, "wt", axis=0, tiled=True), window, strip_rows, column_count
    )
    window = panel_inner
    weight_share = lax.psum_scatter(
        weight_terms(window, all_padded, strip_rows, column_count),
        "rows",
        scatter_dimension=0,
        tiled=True,
    )
    grad_weight = lax.all_gather(weight_share, "rows", axis=0, tiled=True) / total_cells
    grad_pre = grad_hidden * sigmoid_pre * (1.0 + pre_norm * (1.0 - sigmoid_pre))
    grad_norm = (grad_pre * gain_column).reshape(grouped.shape)
    normed_groups = normed.reshape(grouped.shape)
    first_sum, second_sum = lax.psum(
        (
            jnp.sum(grad_norm, axis=(2, 3), keepdims=True),
            jnp.sum(grad_norm * normed_groups, axis=(2, 3), keepdims=True),
        ),
        "rows",
    )
    first_mean = first_sum / group_cells
    second_mean = second_sum / group_cells
    grad_latents = residual.reshape(latents.shape) + (
        inverse * (grad_norm - first_mean - normed_groups * second_mean)
    ).reshape(latents.shape)
    totals = lax.psum(
        (
            jnp.sum(jnp.square(residual)),
            jnp.sum(residual, axis=(0, 2)),
            jnp.sum(grad_pre * normed, axis=(0, 2)),
            jnp.sum(grad_pre, axis=(0, 2)),
        ),
        ("rows", "wt"),
    )
    mean_loss = (totals[0] / (total_cells * channels)).reshape(1)
    param_grads = jnp.stack([totals[1], totals[2], totals[3]]) / total_cells
    return (mean_loss, grad_latents, grad_weight, param_grads)


def plane(ref, row, channels):
    return ref[pl.ds(row, channels, stride=2), :]


def split3(x):
    a = x.astype(BF16)
    rest = x - a.astype(F32)
    b = rest.astype(BF16)
    c = (rest - b.astype(F32)).astype(BF16)
    return a, b, c


def membership(channels):
    size = channels // GROUPS
    channel = lax.broadcasted_iota(jnp.int32, (channels, LANES), 0)
    first = lax.broadcasted_iota(jnp.int32, (channels, LANES), 1) * size
    inside = (channel >= first) & (channel < first + size)
    return jnp.where(inside, 1.0, 0.0).astype(BF16)


def dot_nn(a, b):
    return lax.dot_general(a, b, (((1,), (0,)), ((), ())), preferred_element_type=F32)


def dot_nt(a, b):
    return lax.dot_general(a, b, (((1,), (1,)), ((), ())), preferred_element_type=F32)


def group_sums(rows, member):
    a, b, c = split3(rows)
    return dot_nn(a, member) + (dot_nn(b, member) + dot_nn(c, member))


def to_channels(rows, member):
    a, b, c = split3(rows)
    return dot_nt(a, member) + (dot_nt(b, member) + dot_nt(c, member))


def as_rows(columns, channels):
    lane = lax.broadcasted_iota(jnp.int32, (channels, LANES), 1)
    table = jnp.zeros((channels, LANES), F32)
    for i, column in enumerate(columns):
        table = jnp.where(lane == i, column, table)
    return jnp.transpose(table)[:8, :]


def as_columns(rows, channels):
    pad = jnp.zeros((LANES - len(rows), channels), F32)
    return jnp.transpose(jnp.concatenate(rows + [pad], axis=0))


def row_sum(a, b):
    return jnp.sum(a + b, axis=1, keepdims=True)


def stats_kernel(lat, out):
    channels = out.shape[1]
    a, b = plane(lat, 0, channels), plane(lat, 1, channels)
    out[...] = as_rows([row_sum(a, b), row_sum(a * a, b * b)], channels)


def hidden_kernel(cells, lat, s0, s1, s2, s3, given, hidden, table):
    channels = s0.shape[1]
    member = membership(channels)
    sums = group_sums((s0[...] + s1[...]) + (s2[...] + s3[...]), member)
    mean = sums[0:1] / cells
    var = sums[1:2] / cells - mean * mean
    inverse = lax.rsqrt(var + epsilon)
    pad = jnp.zeros((6, LANES), F32)
    rows = to_channels(jnp.concatenate([mean, inverse, pad], axis=0), member)
    columns = as_columns([rows[0:1], rows[1:2], given[0:1], given[1:2], given[2:3]], channels)
    table[...] = columns
    for row in range(2):
        normed = (plane(lat, row, channels) - columns[:, 0:1]) * columns[:, 1:2]
        pre = normed * columns[:, 2:3] + columns[:, 3:4]
        hidden[row] = (pre * jax.nn.sigmoid(pre)).astype(BF16)


def shifts(x):
    wide = x.astype(F32)
    lane = lax.broadcasted_iota(jnp.int32, x.shape, 1)
    left = jnp.where(lane == 0, 0.0, pltpu.roll(wide, 1, 1)).astype(BF16)
    right = jnp.where(lane == LANES - 1, 0.0, pltpu.roll(wide, LANES - 1, 1)).astype(BF16)
    return left, x, right


def base_kernel(lat, tea, table, base):
    channels = table.shape[0]
    for row in range(2):
        base[row] = plane(lat, row, channels) + table[:, 4:5] - plane(tea, row, channels)


def frame_kernel(place, mine, above, below, framed):
    strip = place[0]
    edge = jnp.zeros_like(mine[0])
    before = jnp.where(strip > 0, below[1], edge)
    after = jnp.where(strip < 3, above[0], edge)
    for row, source in enumerate((before, mine[0], mine[1], after)):
        for kx, moved in enumerate(shifts(source)):
            framed[kx, row] = moved


def panel_rows(me, k, panel):
    return pl.ds(pl.multiple_of((me ^ k) * panel, panel), panel)


def conv_step(total, framed, ky, kx, first, second):
    window = jnp.concatenate([framed[kx, ky], framed[kx, ky + 1]], axis=1)
    total[...] += dot_nn(jnp.concatenate([first, second], axis=0), window)


def near_conv_kernel(place, near, side, framed, base, part, block0, block1, total):
    me = place[1]
    panel = near.shape[1]
    total[...] = jnp.zeros_like(total)

    def step(tap, carry):
        ky = tap // 3
        conv_step(total, framed, ky, tap - 3 * ky, near[tap], side[tap])
        return carry

    lax.fori_loop(0, 9, step, 0)
    for k, block in enumerate((block0, block1)):
        for row in range(2):
            value = base[row, panel_rows(me, k, panel), :] + (
                total[k * panel : (k + 1) * panel, row * LANES : (row + 1) * LANES]
            )
            part[k, row] = value
            block[row] = value.astype(BF16)


def far_conv_kernel(
    place, far0, far1, far2, far3, far4, diag0, diag1, diag2, diag3, diag4, framed, base, part,
    res, low, block23, total,
):
    me, half = place[1], place[2]
    panel = far0.shape[1]
    total[...] = jnp.zeros_like(total)

    def run(first, far, diag):
        def step(i, carry):
            tap = first + i
            ky = tap // 3
            conv_step(total, framed, ky, tap - 3 * ky, far[i], diag[i])
            return carry

        lax.fori_loop(0, far.shape[0], step, 0)

    run(2 * half, far0, diag0)
    run(2 - 2 * half, far1, diag1)
    run(4 + half, far2, diag2)
    run(5 - half, far3, diag3)
    run(6, far4, diag4)
    for k in range(4):
        rows = panel_rows(me, k, panel)
        for row in range(2):
            if k < 2:
                value = part[k, row]
            else:
                value = base[row, rows, :] + (
                    total[(k - 2) * panel : (k - 1) * panel, row * LANES : (row + 1) * LANES]
                )
                block23[k - 2, row] = value.astype(BF16)
            res[row, rows, :] = value
            low[row, rows, :] = value.astype(BF16)


def assemble_kernel(
    place, near, side, far0, far1, far2, far3, far4, diag0, diag1, diag2, diag3, diag4, full
):
    me, half = place[1], place[2]
    panel = near.shape[1]
    near_taps, side_taps = panel_rows(me, 0, panel), panel_rows(me, 1, panel)
    far_taps, diag_taps = panel_rows(me, 2, panel), panel_rows(me, 3, panel)

    def local(tap, carry):
        full[tap, near_taps, :] = near[tap]
        full[tap, side_taps, :] = side[tap]
        return carry

    lax.fori_loop(0, 9, local, 0)
    parts = (
        (2 * half, far0, diag0), (2 - 2 * half, far1, diag1), (4 + half, far2, diag2),
        (5 - half, far3, diag3), (6, far4, diag4),
    )
    for first, far, diag in parts:
        def remote(i, carry, first=first, far=far, diag=diag):
            full[first + i, far_taps, :] = far[i]
            full[first + i, diag_taps, :] = diag[i]
            return carry

        lax.fori_loop(0, far.shape[0], remote, 0)


def back_kernel(full, before, low, after, res, lat, table, grad, sums, framed, total):
    channels = low.shape[1]
    for row, source in enumerate((before[0], low[0], low[1], after[0])):
        for kx, moved in enumerate(shifts(source)):
            framed[kx, row] = jnp.transpose(moved)
    total[...] = jnp.zeros_like(total)

    def tap_step(tap, carry):
        ky = tap // 3
        kx = tap - 3 * ky
        window = jnp.concatenate([framed[2 - kx, 2 - ky], framed[2 - kx, 3 - ky]], axis=0)
        total[...] += dot_nn(window, full[tap])
        return carry

    lax.fori_loop(0, 9, tap_step, 0)
    columns = table[...]
    first = second = bottom = loss = None
    for row in range(2):
        normed = (plane(lat, row, channels) - columns[:, 0:1]) * columns[:, 1:2]
        pre = normed * columns[:, 2:3] + columns[:, 3:4]
        s = jax.nn.sigmoid(pre)
        value = jnp.transpose(total[row * LANES : (row + 1) * LANES, :]) * s * (1.0 + pre * (1.0 - s))
        grad[row] = value
        r = res[row]
        terms = (value, value * normed, r, r * r)
        if row == 0:
            first, second, bottom, loss = terms
        else:
            first, second, bottom, loss = (
                first + terms[0], second + terms[1], bottom + terms[2], loss + terms[3],
            )
    add = functools.partial(jnp.sum, axis=1, keepdims=True)
    sums[...] = as_rows([add(first), add(second), add(bottom), add(loss)], channels)


def latents_kernel(cells, s0, s1, s2, s3, given, res, grad, lat, table, out, total):
    channels = total.shape[1]
    member = membership(channels)
    sums = (s0[...] + s1[...]) + (s2[...] + s3[...])
    total[...] = sums
    means = group_sums(sums * given[0:1], member) / cells
    rows = to_channels(means, member)
    columns = as_columns([rows[0:1], rows[1:2]], channels)
    constants = table[...]
    inverse = constants[:, 1:2]
    for row in range(2):
        normed = (plane(lat, row, channels) - constants[:, 0:1]) * inverse
        change = grad[row] * constants[:, 2:3] - columns[:, 0:1] - normed * columns[:, 1:2]
        out[pl.ds(row, channels, stride=2), :] = res[row] + inverse * change


def weight_pair(strip, pair, aligned, one, two, first, images, base, lefts, emit):
    panel, channels = aligned.shape[2], images[0].shape[1]
    for m in range(2):
        for k in range(2):
            for row in range(2):
                lane = pl.ds((2 * k + row) * LANES, LANES)
                source = aligned[base + k, row]
                if m == 1:
                    source = jnp.where(first, one[base + k, row], two[base + k, row])
                moved = shifts(source)
                for kx in range(3):
                    lefts[(strip & 1) ^ m, kx * panel : (kx + 1) * panel, lane] = moved[2 - kx]

    def step(ky, carry):
        product = None
        for m in range(2):
            right = jnp.concatenate(
                [images[k][4 * pair + 2 * m + ky + row] for k in range(2) for row in range(2)], axis=1
            )
            part = dot_nt(lefts[m], right)
            product = part if product is None else product + part
        emit(pl.ds(3 * ky, 3), product.reshape(3, panel, channels))
        return carry

    lax.fori_loop(0, 3, step, 0)


def totals_kernel(cells, s0, s1, s2, s3, loss, grads):
    sums = (s0[...] + s1[...]) + (s2[...] + s3[...])
    square = jnp.sum(sums[3:4], axis=1, keepdims=True) / (cells * sums.shape[1])
    loss[...] = jnp.broadcast_to(square, loss.shape)
    for row, source in enumerate((2, 1, 0)):
        grads[row : row + 1] = sums[source : source + 1] / cells


def spread_kernel(place, mine, above, beyond, below, spread):
    strip = place[0]
    channels = spread.shape[1]
    spread[0] = jnp.zeros((channels, LANES), BF16)
    spread[9] = jnp.zeros((channels, LANES), BF16)
    for m, source in enumerate((mine, above, beyond, below)):
        for row in range(2):
            spread[1 + 2 * ((strip + m) & 3) + row] = source[row]


def near_weight_kernel(place, own, plus, minus, h0, h1, out, lefts):
    strip = place[0]

    def emit(taps, product):
        out[taps] = product

    weight_pair(strip, strip // 2, own, plus, minus, (strip & 1) == 0, (h0, h1), 0, lefts, emit)


def next_weight_kernel(place, own, plus, minus, h2, h3, near, out, lefts):
    strip = place[0]

    def emit(taps, product):
        out[taps] = near[taps] + product

    weight_pair(strip, strip // 2, own, plus, minus, (strip & 1) == 0, (h2, h3), 2, lefts, emit)


def far_weight_kernel(cells, place, plus, minus, far, h0, h1, h2, h3, near, out, lefts, held, sems):
    strip = place[0]
    pair, even = 1 - strip // 2, (strip & 1) == 0

    def written(taps, slot):
        return pltpu.make_async_copy(held.at[taps], out.at[taps], sems.at[slot])

    def keep(taps, product):
        held[taps] = product

    def emit(taps, product):
        held[taps] = (near[taps] + (held[taps] + product)) / cells
        for slot in range(3):
            @pl.when(taps.start == 3 * slot)
            def _(slot=slot):
                written(pl.ds(3 * slot, 3), slot).start()

    weight_pair(strip, pair, far, minus, plus, even, (h0, h1), 0, lefts, keep)
    weight_pair(strip, pair, far, minus, plus, even, (h2, h3), 2, lefts, emit)
    for slot in range(3):
        written(pl.ds(3 * slot, 3), slot).wait()


VM = pl.BlockSpec(memory_space=pltpu.VMEM)
SM = pl.BlockSpec(memory_space=pltpu.SMEM)


def call(kernel, outs, specs, args, scratch=(), mib=8, us=3, space=VM):
    return pl.pallas_call(
        kernel,
        out_shape=outs,
        in_specs=specs,
        out_specs=jax.tree.map(lambda _: space, outs),
        scratch_shapes=scratch,
        compiler_params=pltpu.CompilerParams(vmem_limit_bytes=mib << 20),
        cost_estimate=pl.CostEstimate(
            flops=int(us * 1e9), bytes_accessed=int(us * 3e6), transcendentals=0
        ),
    )(*args)


def shape(dims, dtype):
    return jax.ShapeDtypeStruct(dims, dtype)


def swap(x, axis, mask):
    size = lax.axis_size(axis)
    return lax.ppermute(x, axis, [(i, i ^ mask) for i in range(size)])


def ring(x, axis, step):
    size = lax.axis_size(axis)
    return lax.ppermute(x, axis, [((i + step) % size, i) for i in range(size)])


def after_all(x, *others):
    return lax.optimization_barrier((x, *others))[0]


def strips_of_four(latents, teacher, norm_gain, norm_shift, conv_weight, conv_bias):
    row_devices = lax.axis_size("rows")
    panel_devices = lax.axis_size("wt")
    _, channels, strip_rows, width = latents.shape
    panel = conv_weight.shape[0]
    strip_cells = strip_rows * width
    total_cells = panel_devices * row_devices * strip_cells
    group_cells = channels // GROUPS * strip_cells * row_devices
    up = [(i, i + 1) for i in range(row_devices - 1)]
    down = [(i + 1, i) for i in range(row_devices - 1)]
    lat = latents.reshape(channels * strip_rows, width)
    tea = teacher.reshape(channels * strip_rows, width)
    given = jnp.stack([norm_gain, norm_shift, conv_bias])
    part = lax.axis_index("grp").astype(jnp.int32)
    here = lax.axis_index("wt").astype(jnp.int32)
    strip = lax.axis_index("rows").astype(jnp.int32)
    place = jnp.stack([strip, here, part])

    near = jnp.transpose(conv_weight, (1, 0, 2))
    far0 = swap(lax.dynamic_slice_in_dim(near, part * 2, 2, axis=0), "wt", 2)
    side = swap(near, "wt", 1)

    stats = call(stats_kernel, shape((8, channels), F32), [VM], (lat,))
    hidden, table = call(
        functools.partial(hidden_kernel, group_cells),
        (shape((strip_rows, channels, width), BF16), shape((channels, LANES), F32)),
        [VM] * 6,
        (lat, after_all(stats, far0, side), *(swap(stats, "rows", m) for m in (1, 2, 3)), given),
        us=0.05,
    )
    above, below = ring(hidden, "rows", 1), ring(hidden, "rows", 3)
    later = after_all(near, hidden)
    far2 = swap(lax.dynamic_slice_in_dim(later, 4 + part, 1, axis=0), "wt", 2)
    far4 = swap(later[6:9], "wt", 2)
    far1, far3 = swap(after_all(far0, hidden), "grp", 1), swap(far2, "grp", 1)
    base = call(
        base_kernel, shape((strip_rows, channels, width), F32), [VM] * 3, (lat, tea, table), us=5
    )
    framed = call(
        frame_kernel,
        shape((3, 4, channels, width), BF16),
        [SM] + [VM] * 3,
        (place, after_all(hidden, base), above, below),
        us=5,
    )
    beyond = ring(above, "rows", 1)
    rows_of = functools.partial(
        call, spread_kernel, shape((10, channels, width), BF16), [SM] + [VM] * 4, us=3
    )
    part0, block0, block1 = call(
        near_conv_kernel,
        (
            shape((2, strip_rows, panel, width), F32),
            shape((strip_rows, panel, width), BF16),
            shape((strip_rows, panel, width), BF16),
        ),
        [SM] + [VM] * 4,
        (place, near, side, framed, base),
        [pltpu.VMEM((2 * panel, 2 * LANES), F32)],
        us=20,
    )
    fars = lax.optimization_barrier((far0, far1, far2, far3, far4, part0, beyond))[:5]
    weights = (near, side, *fars, *(swap(far, "wt", 1) for far in fars))
    res, low, block23 = call(
        far_conv_kernel,
        (
            shape((strip_rows, channels, width), F32),
            shape((strip_rows, channels, width), BF16),
            shape((2, strip_rows, panel, width), BF16),
        ),
        [SM] + [VM] * 13,
        (place, *weights[2:], framed, base, part0),
        [pltpu.VMEM((2 * panel, 2 * LANES), F32)],
        us=0.05,
    )

    block1 = swap(block1, "wt", 1)
    block23 = swap(block23, "wt", 2)
    stacked = jnp.stack([block0, block1, block23[0], swap(block23[1], "wt", 1)])
    settled = after_all(low, stacked)
    low_before = lax.ppermute(settled[1:2], "rows", up)
    low_after = lax.ppermute(settled[0:1], "rows", down)
    plus = ring(stacked, "rows", 1)
    minus = ring(after_all(stacked, plus), "rows", 3)
    far = ring(plus, "rows", 1)
    full = call(
        assemble_kernel,
        shape((9, channels, channels), BF16),
        [SM] + [VM] * 12,
        (after_all(place, stacked), *weights),
        us=5,
    )

    across = [swap(after_all(hidden, block23), "wt", 2)]
    across.append(swap(after_all(above, across[0]), "wt", 2))
    below_across = swap(after_all(below, across[0]), "wt", 2)
    own_rows = rows_of((after_all(place, full), hidden, above, beyond, below))
    other_rows = swap(own_rows, "wt", 1)

    grad, sums = call(
        back_kernel,
        (shape((strip_rows, channels, width), F32), shape((8, channels), F32)),
        [VM] * 7,
        (full, low_before, after_all(low, plus), low_after, res, lat, table),
        [
            pltpu.VMEM((3, 4, LANES, channels), BF16),
            pltpu.VMEM((2 * LANES, channels), F32),
        ],
        mib=12, us=30,
    )
    across += [swap(after_all(beyond, grad), "wt", 2), below_across]
    sums = after_all(sums, minus)
    near_weight = call(
        near_weight_kernel,
        shape((9, panel, channels), F32),
        [SM] + [VM] * 5,
        (after_all(place, sums, across[1], below_across), stacked, plus, minus, own_rows, other_rows),
        [pltpu.VMEM((2, 3 * panel, 4 * LANES), BF16)],
        mib=14, us=30,
    )
    across_rows = rows_of((after_all(place, near_weight), *across))
    grad_latents, sums = call(
        functools.partial(latents_kernel, group_cells),
        (shape((channels * strip_rows, width), F32), shape((8, channels), F32)),
        [VM] * 9,
        (
            after_all(sums, near_weight), *(swap(sums, "rows", m) for m in (1, 2, 3)),
            given, res, grad, lat, table,
        ),
        us=0.05,
    )
    diag_rows = swap(after_all(across_rows, grad_latents, far), "wt", 1)
    images = (own_rows, other_rows, across_rows, diag_rows)
    next_weight = call(
        next_weight_kernel,
        shape((9, panel, channels), F32),
        [SM] + [VM] * 6,
        (after_all(place, grad_latents), stacked, plus, minus, across_rows, diag_rows, near_weight),
        [pltpu.VMEM((2, 3 * panel, 4 * LANES), BF16)],
        mib=16, us=30,
    )
    loss, param_grads = call(
        functools.partial(totals_kernel, total_cells),
        (shape((1, LANES), F32), shape((3, channels), F32)),
        [VM] * 4,
        (after_all(sums, next_weight), *(swap(sums, "wt", m) for m in (1, 2, 3))),
        us=0.05,
    )

    grad_weight = call(
        functools.partial(far_weight_kernel, total_cells),
        shape((9, panel, channels), F32),
        [SM] + [VM] * 8,
        (place, plus, minus, far, *images, after_all(next_weight, param_grads)),
        [
            pltpu.VMEM((2, 3 * panel, 4 * LANES), BF16),
            pltpu.VMEM((9, panel, channels), F32),
            pltpu.SemaphoreType.DMA((3,)),
        ],
        mib=18, us=0.05, space=pl.BlockSpec(memory_space=pl.ANY),
    )
    return (
        loss[0, :1],
        grad_latents.reshape(latents.shape),
        jnp.transpose(grad_weight, (1, 0, 2)),
        param_grads,
    )


def solution(mesh):
    placed = (
        P(("grp", "wt"), None, "rows", None),
        P(("grp", "wt"), None, "rows", None),
        P(),
        P(),
        P("wt", None, None),
        P(),
    )
    small = mesh.shape["rows"] == 4 and mesh.shape["wt"] == 4 and mesh.shape["grp"] == 2
    return jax.shard_map(
        strips_of_four if small else generic,
        mesh=mesh,
        in_specs=placed,
        out_specs=(
            P("grp"),
            P(("grp", "wt"), None, "rows", None),
            P(("grp", "wt"), None, None),
            P("grp", None),
        ),
        check_vma=False,
    )
```
